32 devices in a mesh: dp: 8 (over y, x, core), seq: 4 (over z).
Axes of the slice: x: 2, y: 2, z: 4, core: 2. Of those that a mesh axis runs over, the one named last changes fastest.
Arguments:
- enc_states: bfloat16 [8, 256, 4096], P('dp'), may hold values from -6 to 6
- lengths: int32 [8], replicated, may hold values from 1 to 128, as said below
- prompt_owner_sample: int32 [8], replicated, may hold values from 0 to 7, each once
- t5_gain: float32 [4096], replicated, may hold values from 0.5 to 1.5
- t5_in_weight: bfloat16 [2, 4096, 5120], P(None, None, 'seq'), may hold values from -0.09375 to 0.09375
- t5_out_weight: bfloat16 [5120, 4096], P('seq'), may hold values from -0.078125 to 0.078125
- t5_final_gain: float32 [4096], replicated, may hold values from 0.5 to 1.5
- context_weight: bfloat16 [4096, 3072], P('seq', 'dp'), may hold values from -0.09375 to 0.09375
- text_shift: float32 [8, 3072], P('dp'), may hold values from -3 to 3
- text_scale: float32 [8, 3072], P('dp'), may hold values from -0.5 to 0.5
- kv_weight: bfloat16 [3072, 2, 3072], P('dp', None, 'seq'), may hold values from -0.109375 to 0.109375
- text_key_gain: float32 [128], replicated, may hold values from 0.25 to 1.75
- image_query_key_value: bfloat16 [8, 512, 3, 3072], P('dp', 'seq'), may hold values from -6 to 6
- image_qk_gain: float32 [2, 128], replicated, may hold values from 0.25 to 1.75
- proj_weight: bfloat16 [3072, 3072], P('seq', 'dp'), may hold values from -0.109375 to 0.109375
- dora_a: float32 [3072, 64], P('seq'), may hold values from -0.109375 to 0.109375
- dora_b: float32 [64, 3072], P(None, 'dp'), may hold values from -0.375 to 0.375
- magnitude: float32 [3072], P('dp'), may hold values from 0.5 to 2
- grad_out: bfloat16 [8, 512, 3072], P('dp', 'seq'), may hold values from -6 to 6
Outputs:
- image_out: bfloat16 [8, 512, 3072], P('dp', 'seq')
- grad_a: float32 [3072, 64], P('seq')
- grad_b: float32 [64, 3072], P(None, 'dp')
- grad_magnitude: float32 [3072], P('dp')
The draws below stay inside these ranges and needn't reach their ends.
Inputs may be any that keep to these rules, and one draw needn't show every extreme that they name: `lengths`: prompt token counts; in every draw one prompt has exactly 128 tokens. `prompt_owner_sample`: each DiT sample index appears exactly once.
All inputs are finite; a program needn't handle non-finite values.
Results may differ from the reference program's by a relative error of at most 0.024.
Values may be sent and summed in bfloat16 or wider, within the bound.
A program may use at most 128 MiB of HBM per device.

```python
import math
import jax
import jax.numpy as jnp
from jax import lax

D5 = 4096
F5 = 5120
D = 3072
HEADS = 24
HD = 128
RANK = 64
LTXT = 256
BLK = 128
IMG = 512
SAMPLES = 8
N_SEQ = 4


def draw_lengths(key, part):
    length_key, pick_key = jax.random.split(key)
    drawn_lengths = jax.random.randint(length_key, (SAMPLES,), 1, BLK + 1, dtype=jnp.int32)
    longest = jax.random.randint(pick_key, (), 0, SAMPLES, dtype=jnp.int32)
    return jnp.where(jnp.arange(SAMPLES, dtype=jnp.int32) == longest, BLK, drawn_lengths).astype(jnp.int32)


def shard_levels(key, extent, pieces, low, top_value):
    def one(axis_at, shards_of):
        steps = jax.random.uniform(jax.random.fold_in(jax.random.fold_in(key, 6), axis_at), (shards_of,), jnp.float32, low / len(pieces), top_value / len(pieces))
        return jnp.repeat(jnp.exp(steps), extent[axis_at] // shards_of).reshape((-1,) + (1,) * (len(extent) - axis_at - 1))

    factor_of = one(*pieces[0])
    for cut in pieces[1:]:
        factor_of = factor_of * one(*cut)
    return factor_of


def noise(own_key, shape, scale, reach, shards=(), kind=jnp.bfloat16):
    values = jax.random.normal(own_key, shape, jnp.float32) * scale
    if len(shards) > 0:
        values = shard_levels(own_key, shape, shards, -0.22, 0.18) * values
    return jnp.clip(values, min=-reach, max=reach).astype(kind)


def setup_inputs(seed: int = 0) -> dict:
    keys = jax.random.split(jax.random.key(seed), 20)
    enc_states = noise(keys[0], (SAMPLES, LTXT, D5), 1.0, 6.0, ((0, 8),))
    lengths = draw_lengths(jax.random.fold_in(keys[19], 71), 0)
    prompt_owner_sample = jax.random.permutation(keys[2], SAMPLES).astype(jnp.int32)
    t5_gain = jnp.clip(1.0 + 0.1 * jax.random.normal(keys[3], (D5,), jnp.float32), 0.5, 1.5)
    t5_in_weight = noise(keys[4], (2, D5, F5), D5 ** -0.5, 0.09375, ((2, 4),))
    t5_out_weight = noise(keys[5], (F5, D5), F5 ** -0.5, 0.078125, ((0, 4),))
    t5_final_gain = jnp.clip(1.0 + 0.1 * jax.random.normal(keys[6], (D5,), jnp.float32), 0.5, 1.5)
    context_weight = noise(keys[7], (D5, D), D5 ** -0.5, 0.09375, ((0, 4), (1, 8)))
    text_shift = noise(keys[8], (SAMPLES, D), 0.5, 3.0, ((0, 8),), jnp.float32)
    text_scale = jnp.clip(jax.random.uniform(keys[9], (SAMPLES, D), jnp.float32, -0.5, 0.5) * shard_levels(keys[9], (SAMPLES, D), ((0, 8),), -0.4, 0.0), -0.5, 0.5)
    kv_weight = noise(keys[10], (D, 2, D), D ** -0.5, 0.109375, ((0, 8), (2, 4)))
    text_key_gain = jnp.clip(1.0 + 0.15 * jax.random.normal(keys[11], (HD,), jnp.float32), 0.25, 1.75)
    image_query_key_value = noise(keys[12], (SAMPLES, IMG, 3, D), 1.0, 6.0, ((0, 8), (1, 4)))
    image_qk_gain = jnp.clip(1.0 + 0.15 * jax.random.normal(keys[13], (2, HD), jnp.float32), 0.25, 1.75)
    proj_weight = noise(keys[14], (D, D), D ** -0.5, 0.109375, ((0, 4), (1, 8)))
    dora_a = noise(keys[15], (D, RANK), D ** -0.5, 0.109375, ((0, 4),), jnp.float32)
    dora_b = noise(keys[16], (RANK, D), (4 * RANK) ** -0.5, 0.375, ((1, 8),), jnp.float32)
    magnitude = jnp.clip(jnp.exp(math.log(2.0) - 1.3862944 * jax.random.uniform(keys[17], (D,), jnp.float32) ** shard_levels(keys[17], (D,), ((0, 8),), -0.2, 0.2)), 0.5, 2.0)
    grad_out = noise(keys[18], (SAMPLES, IMG, D), 1.0, 6.0, ((0, 8), (1, 4)))
    return {"enc_states": enc_states, "lengths": lengths, "prompt_owner_sample": prompt_owner_sample, "t5_gain": t5_gain, "t5_in_weight": t5_in_weight, "t5_out_weight": t5_out_weight, "t5_final_gain": t5_final_gain, "context_weight": context_weight, "text_shift": text_shift, "text_scale": text_scale, "kv_weight": kv_weight, "text_key_gain": text_key_gain, "image_query_key_value": image_query_key_value, "image_qk_gain": image_qk_gain, "proj_weight": proj_weight, "dora_a": dora_a, "dora_b": dora_b, "magnitude": magnitude, "grad_out": grad_out}


EPSILON = 1e-06

def rms_scale(values, gain):
    return values * lax.rsqrt(lax.optimization_barrier(jnp.mean(values * values, -1, keepdims=True)) + EPSILON) * gain

def reference(enc_states, lengths, prompt_owner_sample, t5_gain, t5_in_weight, t5_out_weight, t5_final_gain, context_weight, text_shift, text_scale, kv_weight, text_key_gain, image_query_key_value, image_qk_gain, proj_weight, dora_a, dora_b, magnitude, grad_out):
    flat_tokens = enc_states.reshape(SAMPLES * LTXT, D5).astype(jnp.float32)
    normed = rms_scale(flat_tokens, t5_gain).astype(jnp.bfloat16)
    gate_proj = jnp.dot(normed, t5_in_weight[0], preferred_element_type=jnp.float32)
    upward = jnp.dot(normed, t5_in_weight[1], preferred_element_type=jnp.float32)
    hidden = (jax.nn.gelu(gate_proj, approximate=True) * upward).astype(jnp.bfloat16)
    hidden_slice = F5 // N_SEQ
    ffn_sum = jnp.zeros((SAMPLES * LTXT, D5), jnp.float32)
    for shard_index in range(N_SEQ):
        partial_value = jnp.dot(hidden[:, shard_index * hidden_slice:(shard_index + 1) * hidden_slice], t5_out_weight[shard_index * hidden_slice:(shard_index + 1) * hidden_slice], preferred_element_type=jnp.float32)
        ffn_sum = ffn_sum + lax.optimization_barrier(partial_value.astype(jnp.bfloat16)).astype(jnp.float32)
    encoded = ((flat_tokens + ffn_sum) * t5_final_gain).astype(jnp.bfloat16)
    feature_slice = D5 // N_SEQ
    context_sum = jnp.zeros((SAMPLES * LTXT, D), jnp.float32)
    for shard_index in range(N_SEQ):
        partial_value = jnp.dot(encoded[:, shard_index * feature_slice:(shard_index + 1) * feature_slice], context_weight[shard_index * feature_slice:(shard_index + 1) * feature_slice], preferred_element_type=jnp.float32)
        context_sum = context_sum + lax.optimization_barrier(partial_value.astype(jnp.bfloat16)).astype(jnp.float32)
    text_embed = context_sum.astype(jnp.bfloat16).reshape(SAMPLES, LTXT, D)
    routed = jnp.zeros_like(text_embed).at[prompt_owner_sample].set(text_embed)
    diffusion_lengths = jnp.zeros_like(lengths).at[prompt_owner_sample].set(lengths)
    routed_values = routed.astype(jnp.float32)
    centre = lax.optimization_barrier(jnp.mean(routed_values, -1, keepdims=True))
    spread = lax.optimization_barrier(jnp.mean((routed_values - centre) * (routed_values - centre), -1, keepdims=True))
    layer_normed = (routed_values - centre) * lax.rsqrt(spread + EPSILON)
    modulated = ((1.0 + text_scale[:, None, :]) * layer_normed + text_shift[:, None, :]).astype(jnp.bfloat16)
    key_value = jnp.dot(modulated.reshape(SAMPLES * LTXT, D), kv_weight.reshape(D, 2 * D), preferred_element_type=jnp.float32).reshape(SAMPLES, LTXT, 2, HEADS, HD)
    prompt_key_rows = rms_scale(key_value[:, :, 0], text_key_gain).astype(jnp.bfloat16)
    prompt_value_rows = key_value[:, :, 1].astype(jnp.bfloat16)
    score_scale = 1.0 / math.sqrt(HD)

    def sample_attention(inputs):
        qkv_rows, keys_text, values_text, prompt_length = inputs
        split_heads = qkv_rows.reshape(IMG, 3, HEADS, HD)
        queries = rms_scale(split_heads[:, 0].astype(jnp.float32), image_qk_gain[0]).astype(jnp.bfloat16)
        key_image = rms_scale(split_heads[:, 1].astype(jnp.float32), image_qk_gain[1]).astype(jnp.bfloat16)
        value_image = split_heads[:, 2]
        key_valid_mask = jnp.arange(LTXT, dtype=jnp.int32) < prompt_length
        text_scores = jnp.einsum('qhd,khd->hqk', queries.astype(jnp.float32), keys_text.astype(jnp.float32)) * score_scale
        text_weight = jnp.where(key_valid_mask[None, None, :], jnp.exp(text_scores), 0.0)
        image_scores = jnp.einsum('qhd,khd->hqk', queries.astype(jnp.float32), key_image.astype(jnp.float32)) * score_scale
        image_weight = jnp.exp(image_scores)
        denominator = lax.optimization_barrier(jnp.sum(text_weight, -1)) + lax.optimization_barrier(jnp.sum(image_weight, -1))
        text_probs = (text_weight / denominator[..., None]).astype(jnp.bfloat16)
        image_probs = (image_weight / denominator[..., None]).astype(jnp.bfloat16)
        mixture = jnp.einsum('hqk,khd->qhd', text_probs.astype(jnp.float32), values_text.astype(jnp.float32))
        mixture = mixture + jnp.einsum('hqk,khd->qhd', image_probs.astype(jnp.float32), value_image.astype(jnp.float32))
        return mixture.astype(jnp.bfloat16).reshape(IMG, D)
    attended_rows = lax.map(sample_attention, (image_query_key_value, prompt_key_rows, prompt_value_rows, diffusion_lengths))
    flat_attended = attended_rows.reshape(SAMPLES * IMG, D)
    direction = proj_weight.astype(jnp.float32) + jnp.dot(dora_a, dora_b, precision=lax.Precision.HIGHEST)
    column_norm = jnp.sqrt(lax.optimization_barrier(jnp.sum(direction * direction, 0)) + EPSILON)
    column_ratio = magnitude / column_norm
    scaled = (direction * column_ratio).astype(jnp.bfloat16)
    head_width = D // N_SEQ
    out_sum = jnp.zeros((SAMPLES * IMG, D), jnp.float32)
    for shard_index in range(N_SEQ):
        partial_value = jnp.dot(flat_attended[:, shard_index * head_width:(shard_index + 1) * head_width], scaled[shard_index * head_width:(shard_index + 1) * head_width], preferred_element_type=jnp.float32)
        out_sum = out_sum + lax.optimization_barrier(partial_value.astype(jnp.bfloat16)).astype(jnp.float32)
    image_out = out_sum.astype(jnp.bfloat16).reshape(SAMPLES, IMG, D)
    weight_grad = jnp.dot(flat_attended.T, grad_out.reshape(SAMPLES * IMG, D), preferred_element_type=jnp.float32)
    grad_magnitude = lax.optimization_barrier(jnp.sum(weight_grad * direction, 0)) / column_norm
    scaled_grad = weight_grad * column_ratio
    grad_a = jnp.dot(scaled_grad, dora_b.T, precision=lax.Precision.HIGHEST)
    grad_b = jnp.dot(dora_a.T, scaled_grad, precision=lax.Precision.HIGHEST)
    return (image_out, grad_a, grad_b, grad_magnitude)
```

```python
import math

import jax
import jax.numpy as jnp
from jax import lax
from jax.experimental import pallas as pl
from jax.experimental.pallas import tpu as pltpu
from jax.sharding import PartitionSpec as P

HD = 128
MAX_PROMPT = 128
EPSILON = 1e-06


def rms_scale(values, gain):
    return values * lax.rsqrt(jnp.mean(values * values, -1, keepdims=True) + EPSILON) * gain


def attention_kernel(length_ref, text_gain_ref, image_gain_ref, text_key_ref, text_value_ref, image_ref, out_ref):
    def stacked(kind):
        return jnp.concatenate([image_ref[k, kind] for k in range(image_ref.shape[0])], 0)

    queries = rms_scale(stacked(0).astype(jnp.float32), image_gain_ref[0:1, :])
    queries = (queries).astype(jnp.bfloat16)
    key_image = rms_scale(stacked(1).astype(jnp.float32), image_gain_ref[1:2, :]).astype(jnp.bfloat16)
    key_text = rms_scale(text_key_ref[...], text_gain_ref[...]).astype(jnp.bfloat16)
    scale = 1.0 / math.sqrt(HD)
    dims = (((1,), (1,)), ((), ()))
    text_scores = lax.dot_general(queries, key_text, dims, preferred_element_type=jnp.float32) * scale
    image_scores = lax.dot_general(queries, key_image, dims, preferred_element_type=jnp.float32) * scale
    position = lax.broadcasted_iota(jnp.int32, text_scores.shape, 1)
    text_weight = jnp.where(position < length_ref[0], jnp.exp(text_scores), 0.0)
    image_weight = jnp.exp(image_scores)
    denominator = jnp.sum(text_weight, -1, keepdims=True) + jnp.sum(image_weight, -1, keepdims=True)
    mixture = jnp.dot(
        text_weight.astype(jnp.bfloat16),
        text_value_ref[...].astype(jnp.bfloat16),
        preferred_element_type=jnp.float32,
    )
    mixture = mixture + jnp.dot(
        image_weight.astype(jnp.bfloat16), stacked(2), preferred_element_type=jnp.float32
    )
    out_ref[...] = (mixture / denominator).astype(jnp.bfloat16)


def attention(length, text_gain, image_gain, key_value, image_all):
    blocks, kinds, rows, width = image_all.shape
    heads = width // HD
    text = key_value.shape[0]
    vmem = lambda shape, index: pl.BlockSpec(shape, index)
    return pl.pallas_call(
        attention_kernel,
        grid=(heads,),
        out_shape=jax.ShapeDtypeStruct((blocks * rows, width), jnp.bfloat16),
        in_specs=[
            pl.BlockSpec(memory_space=pltpu.SMEM),
            vmem((1, HD), lambda h: (0, 0)),
            vmem((2, HD), lambda h: (0, 0)),
            vmem((text, HD), lambda h: (0, h)),
            vmem((text, HD), lambda h: (0, heads + h)),
            vmem((blocks, kinds, rows, HD), lambda h: (0, 0, 0, h)),
        ],
        out_specs=vmem((blocks * rows, HD), lambda h: (0, h)),
        cost_estimate=pl.CostEstimate(
            flops=4 * heads * blocks * rows * (blocks * rows + text) * HD,
            bytes_accessed=8 * blocks * rows * width,
            transcendentals=heads * blocks * rows * (blocks * rows + text),
        ),
    )(length.reshape(1), text_gain.reshape(1, HD), image_gain, key_value, key_value, image_all)


def peers(axis):
    size, rank = lax.axis_size(axis), lax.axis_index(axis)
    return [(k, lax.rem(rank + k, size)) for k in range(1, size)]


def greet(*axes):
    barrier = pltpu.get_barrier_semaphore()
    count = 0
    for axis in axes:
        for _, peer in peers(axis):
            pl.semaphore_signal(
                barrier, inc=1, device_id={axis: peer}, device_id_type=pl.DeviceIdType.MESH
            )
            count += 1
    pl.semaphore_wait(barrier, count)


def send(source, target, send_sem, recv_sem, axis, peer):
    copy = pltpu.make_async_remote_copy(
        src_ref=source,
        dst_ref=target,
        send_sem=send_sem,
        recv_sem=recv_sem,
        device_id={axis: peer},
        device_id_type=pl.DeviceIdType.MESH,
    )
    copy.start()
    return copy


def finish(copies):
    for copy in copies:
        copy.wait()


def sems(count):
    return [pltpu.SemaphoreType.DMA((count,)), pltpu.SemaphoreType.DMA((count,))]


VMEM = pl.BlockSpec(memory_space=pltpu.VMEM)
SMEM = pl.BlockSpec(memory_space=pltpu.SMEM)


def params(collective_id):
    return pltpu.CompilerParams(
        collective_id=collective_id, has_side_effects=True, vmem_limit_bytes=40 * 2**20
    )


MESH = pl.DeviceIdType.MESH


class Wires:
    def __init__(self, send_sems, recv_sems):
        self.send_sems, self.recv_sems, self.copies = send_sems, recv_sems, []

    def send(self, source, target, axis, peer):
        index = len(self.copies)
        copy = pltpu.make_async_remote_copy(
            src_ref=source,
            dst_ref=target,
            send_sem=self.send_sems.at[index],
            recv_sem=self.recv_sems.at[index],
            device_id={axis: peer},
            device_id_type=MESH,
        )
        copy.start()
        self.copies.append(copy)
        return copy

    def drain(self):
        for copy in self.copies:
            copy.wait_send()


class Place:
    def __init__(self):
        self.pairs = lax.axis_size("dp") // 4
        index = lax.axis_index("dp")
        self.index = index
        self.core = lax.rem(index, 2)
        self.low = lax.rem(lax.div(index, 2), 2)
        self.high = lax.div(index, 4)

    def at(self, step=0, other_low=False, other_core=False):
        high = lax.rem(self.high + step + self.pairs, self.pairs) if step else self.high
        low = 1 - self.low if other_low else self.low
        core = 1 - self.core if other_core else self.core
        return (high * 2 + low) * 2 + core


class Gather:
    def __init__(self, wires, place, own, full, view):
        self.wires, self.place, self.own, self.full, self.view = wires, place, own, full, view
        self.sibling = place.at(other_core=True)
        self.late = []

    def share(self, owner, half=None):
        where = self.view(self.full, owner, half)
        self.late.append(self.wires.send(where, where, "dp", self.sibling))

    def first(self):
        place = self.place
        mine = self.view(self.full, place.index, None)
        send = self.wires.send
        self.low = send(self.own, mine, "dp", place.at(other_low=True))
        self.high = [send(self.own, mine, "dp", place.at(j)) for j in range(1, place.pairs)]
        self.late.append(send(self.own, mine, "dp", self.sibling))

    def second(self):
        place = self.place
        send = self.wires.send
        self.relayed = []
        self.low.wait_recv()
        owner = place.at(other_low=True)
        for j in range(1, place.pairs):
            where = self.view(self.full, owner, 0)
            self.relayed.append((j, 0, send(where, where, "dp", place.at(j))))
        self.share(owner)
        for j in range(1, place.pairs):
            self.high[j - 1].wait_recv()
            owner = place.at(-j)
            where = self.view(self.full, owner, 1)
            self.relayed.append((j, 1, send(where, where, "dp", place.at(other_low=True))))
            self.share(owner)

    def third(self):
        for j, half, copy in self.relayed:
            copy.wait_recv()
            self.share(self.place.at(-j, other_low=True), half)

    def done(self):
        for copy in self.late:
            copy.wait_recv()


def by_rows(rows):
    def view(full, owner, half):
        start, size = owner * rows, rows
        if half is not None:
            size = rows // 2
            start = start + half * size
        return full.at[pl.ds(pl.multiple_of(start, 16), size)]

    return view


def by_columns(rows, width, flat):
    def view(full, owner, half):
        part = pl.ds(0, rows) if half is None else pl.ds(half * (rows // 2), rows // 2)
        if flat:
            return full.at[part, pl.ds(pl.multiple_of(owner * width, 128), width)]
        return full.at[owner, part]

    return view


def flat_columns(width):
    return width % 128 == 0


def column_shape(devices, rows, width):
    return (rows, devices * width) if flat_columns(width) else (devices, rows, width)


def tile_of(width, largest):
    return next(t for t in (largest, largest // 2, 256, 128, width) if width % t == 0)


def front_kernel(
    owner_ref, enc_ref, gain_ref, in_ref, out_ref, final_ref, context_ref, kv_ref, image_ref,
    proj_ref, down_ref, up_ref, magnitude_ref, scale_ref, shift_ref,
    image_all, key_value, gathered, ratio_ref,
    tokens, normed, in_tiles, out_all, hidden, part, sum_slots, encoded, context_all, kv_all,
    context_part, row_slots, stage, prompts, sibling_prompts, final, text_all,
    direction, squares, square_slots, own_scaled,
    in_sems, local_sems, send_sems, recv_sems,
):
    f32, bf16 = jnp.float32, jnp.bfloat16
    count, devices = lax.axis_size("seq"), lax.axis_size("dp")
    rank, data_rank = lax.axis_index("seq"), lax.axis_index("dp")
    place = Place()
    wires = Wires(send_sems, recv_sems)
    text, width_enc = tokens.shape
    feat = encoded.shape[1]
    width = context_part.shape[1]
    rows = stage.shape[0]
    slots, _, _, tile = in_tiles.shape
    tiles = hidden.shape[1] // tile
    depth, own_cols = proj_ref.shape
    flat = flat_columns(own_cols)
    late = count // 2

    def in_copy(i, slot):
        return pltpu.make_async_copy(
            in_ref.at[:, :, pl.ds(pl.multiple_of(i * tile, 128), tile)], in_tiles.at[slot], in_sems.at[slot]
        )

    def local(source, target, index):
        return pltpu.make_async_copy(source, target, local_sems.at[index])

    token_copy = local(enc_ref.at[0, pl.ds(0, text)], tokens, 0)
    token_copy.start()
    for i in range(min(slots, tiles)):
        in_copy(i, i).start()
    out_copy = local(out_ref, out_all, 1)
    out_copy.start()

    def heads_of(owner):
        head_width = image_all.shape[3]
        return pl.ds(pl.multiple_of(owner * head_width, 128), head_width)

    context_view = by_columns(context_ref.shape[0], own_cols, flat)
    scaled_view = by_columns(own_scaled.shape[0], own_cols, flat)
    kv_view = by_rows(kv_ref.shape[0])
    context_gather = Gather(wires, place, context_ref, context_all, context_view)
    kv_gather = Gather(wires, place, kv_ref, kv_all, kv_view)
    scaled_gather = Gather(wires, place, own_scaled, gathered, scaled_view)

    locals_ = [
        local(image_ref.at[:, :, heads_of(rank)], image_all.at[0], 2),
        local(context_ref, context_view(context_all, data_rank, None), 3),
        local(kv_ref, kv_view(kv_all, data_rank, None), 4),
    ]
    greet("seq", "dp")
    context_gather.first()
    image_copies = [
        wires.send(image_ref.at[:, :, heads_of(peer)], image_all.at[k], "seq", peer)
        for k, peer in peers("seq")
        if k != late
    ]

    def late_image(kind):
        peer = lax.rem(rank + late, count)
        image_copies.append(
            wires.send(image_ref.at[kind, :, heads_of(peer)], image_all.at[late, kind], "seq", peer)
        )

    for copy in locals_:
        copy.start()

    token_copy.wait()
    for r in range(0, text, 32):
        block = tokens[r : r + 32, :].astype(f32)
        normed[r : r + 32, :] = rms_scale(block, gain_ref[...]).astype(bf16)

    def in_step(i, carry):
        slot = lax.rem(i, slots)
        in_copy(i, slot).wait()
        gate = jnp.dot(normed[...], in_tiles[slot, 0], preferred_element_type=f32)
        upward = jnp.dot(normed[...], in_tiles[slot, 1], preferred_element_type=f32)
        columns = pl.ds(pl.multiple_of(i * tile, 128), tile)
        hidden[:, columns] = (jax.nn.gelu(gate, approximate=True) * upward).astype(bf16)

        @pl.when(i + slots < tiles)
        def _():
            in_copy(i + slots, slot).start()

        return carry

    lax.fori_loop(0, tiles, in_step, 0)

    out_copy.wait()
    out_tile = tile_of(feat, 512)
    sums = []
    for k in [late] + [k for k in range(1, count) if k != late] + [0]:
        owner = lax.rem(rank + k, count)
        for t in range(0, feat, out_tile):
            columns = pl.ds(pl.multiple_of(owner * feat + t, 128), out_tile)
            part[k, :, t : t + out_tile] = jnp.dot(
                hidden[...], out_all[:, columns], preferred_element_type=f32
            ).astype(bf16)
            if k:
                sums.append(
                    wires.send(
                        part.at[k, :, t : t + out_tile], sum_slots.at[k - 1, :, t : t + out_tile], "seq", owner
                    )
                )

    context_gather.second()
    kv_gather.first()

    total = jnp.zeros((1, own_cols), f32)
    for r in range(0, depth, 128):
        block = proj_ref[r : r + 128, :].astype(f32) + lax.dot_general(
            down_ref[:, r : r + 128],
            up_ref[...],
            (((0,), (0,)), ((), ())),
            precision=lax.Precision.HIGHEST,
            preferred_element_type=f32,
        )
        direction[r : r + 128, :] = block
        total = total + jnp.sum(block * block, 0, keepdims=True)
    squares[...] = total
    square_copies = [wires.send(squares, square_slots.at[k - 1], "seq", peer) for k, peer in peers("seq")]

    context_gather.third()
    for copy in sums:
        copy.wait_recv()
    late_image(0)
    own = pl.ds(pl.multiple_of(rank * feat, 128), feat)
    for r in range(0, text, 32):
        total = part[0, r : r + 32, :].astype(f32)
        for k in range(1, count):
            total = total + sum_slots[k - 1, r : r + 32, :].astype(f32)
        encoded[r : r + 32, :] = (
            (tokens[r : r + 32, own].astype(f32) + total) * final_ref[:, own]
        ).astype(bf16)

    locals_[1].wait()
    context_gather.done()
    if flat:
        step = tile_of(width, 512)
        for c in range(0, width, step):
            context_part[:, c : c + step] = jnp.dot(
                encoded[...], context_all[:, c : c + step], preferred_element_type=f32
            ).astype(bf16)
    else:
        for d in range(devices):
            context_part[:, d * own_cols : (d + 1) * own_cols] = jnp.dot(
                encoded[...], context_all[d], preferred_element_type=f32
            ).astype(bf16)

    def block_of(index):
        return pl.ds(pl.multiple_of(index * rows, 16), rows)

    row_copies = [
        wires.send(context_part.at[block_of(peer)], row_slots.at[k - 1], "seq", peer) for k, peer in peers("seq")
    ]
    kv_gather.second()
    for copy in square_copies:
        copy.wait_recv()
    total = squares[...]
    for k in range(1, count):
        total = total + square_slots[k - 1]
    ratio = magnitude_ref[...] / jnp.sqrt(total + EPSILON)
    ratio_ref[...] = ratio
    for r in range(0, depth, 128):
        own_scaled[r : r + 128, :] = (direction[r : r + 128, :] * ratio).astype(bf16)
    own_scaled[depth:, :] = (up_ref[...] * ratio).astype(bf16)

    for copy in row_copies:
        copy.wait_recv()
    total = context_part[block_of(rank), :].astype(f32)
    for k in range(1, count):
        total = total + row_slots[k - 1].astype(f32)
    stage[...] = total.astype(bf16)

    chips = devices // 2
    chip = lax.div(data_rank, 2)
    sibling = place.at(other_core=True)
    prompt_copies = [
        wires.send(stage, prompts.at[j - 1], "dp", lax.rem(chip + j, chips) * 2 + place.core)
        for j in range(1, chips)
    ]
    shared = [wires.send(stage, sibling_prompts.at[0], "dp", sibling)]
    scaled_gather.first()
    local_scaled = local(own_scaled, scaled_view(gathered, data_rank, None), 5)
    local_scaled.start()
    late_image(1)
    for j in range(1, chips):
        prompt_copies[j - 1].wait_recv()
        shared.append(wires.send(prompts.at[j - 1], sibling_prompts.at[j], "dp", sibling))
    routed = jnp.where(owner_ref[data_rank] == data_rank, stage[...].astype(f32), 0.0)
    for j in range(1, chips):
        prompt = lax.rem(chip + chips - j, chips) * 2 + place.core
        routed = routed + jnp.where(owner_ref[prompt] == data_rank, prompts[j - 1].astype(f32), 0.0)
    for j in range(chips):
        shared[j].wait_recv()
        prompt = lax.rem(chip + chips - j, chips) * 2 + 1 - place.core
        routed = routed + jnp.where(owner_ref[prompt] == data_rank, sibling_prompts[j].astype(f32), 0.0)
    centre = jnp.mean(routed, -1, keepdims=True)
    spread = jnp.mean((routed - centre) * (routed - centre), -1, keepdims=True)
    layer_normed = (routed - centre) * lax.rsqrt(spread + EPSILON)
    final[...] = ((1.0 + scale_ref[...]) * layer_normed + shift_ref[...]).astype(bf16)
    text_copies = [wires.send(final, text_all.at[block_of(rank)], "seq", peer) for _, peer in peers("seq")]
    text_all[block_of(rank), :] = final[...]
    late_image(2)
    kv_gather.third()
    scaled_gather.second()
    locals_[2].wait()
    kv_gather.done()
    for copy in text_copies:
        copy.wait_recv()
    step = tile_of(kv_all.shape[1], 512)
    for c in range(0, kv_all.shape[1], step):
        key_value[:, c : c + step] = jnp.dot(
            text_all[...], kv_all[:, c : c + step], preferred_element_type=f32
        )
    scaled_gather.third()
    locals_[0].wait()
    local_scaled.wait()
    for copy in image_copies:
        copy.wait_recv()
    scaled_gather.done()
    wires.drain()


def wires_needed(count, pairs, sum_tiles):
    others = count - 1
    gathers = 3 * (pairs + 4 * (pairs - 1) + pairs + 2)
    return others + 3 + others * (sum_tiles + 3) + 4 * pairs + gathers


def front(owner, enc, gain, w_in, w_out, final_gain, context, kv, image, proj, down, up, magnitude, scale, shift):
    count, devices = lax.axis_size("seq"), lax.axis_size("dp")
    bf16, f32 = jnp.bfloat16, jnp.float32
    width_enc, hidden = w_in.shape[1:]
    feat = width_enc // count
    text = MAX_PROMPT
    width = scale.shape[1]
    rows = text // count
    kinds, image_rows, _ = image.shape
    head_width = width // count
    own_cols = proj.shape[1]
    scaled_rows = proj.shape[0] + up.shape[0]
    tile = tile_of(hidden, 256)
    slots = 3
    wires = wires_needed(count, devices // 4, feat // tile_of(feat, 512))
    any_ = pl.BlockSpec(memory_space=pl.ANY)
    gathered_shape = column_shape(devices, scaled_rows, own_cols)
    outs = pl.pallas_call(
        front_kernel,
        out_shape=[
            jax.ShapeDtypeStruct((count, kinds, image_rows, head_width), bf16),
            jax.ShapeDtypeStruct((text, kv.shape[1]), f32),
            jax.ShapeDtypeStruct(gathered_shape, bf16),
            jax.ShapeDtypeStruct((1, own_cols), f32),
        ],
        in_specs=[SMEM, any_, VMEM, any_, any_, VMEM, any_, any_, any_] + [VMEM] * 6,
        out_specs=[VMEM] * 4,
        scratch_shapes=[
            pltpu.VMEM((text, width_enc), bf16),
            pltpu.VMEM((text, width_enc), bf16),
            pltpu.VMEM((slots, 2, width_enc, tile), bf16),
            pltpu.VMEM((hidden, width_enc), bf16),
            pltpu.VMEM((text, hidden), bf16),
            pltpu.VMEM((count, text, feat), bf16),
            pltpu.VMEM((count - 1, text, feat), bf16),
            pltpu.VMEM((text, feat), bf16),
            pltpu.VMEM(column_shape(devices, context.shape[0], own_cols), bf16),
            pltpu.VMEM((kv.shape[0] * devices, kv.shape[1]), bf16),
            pltpu.VMEM((text, width), bf16),
            pltpu.VMEM((count - 1, rows, width), bf16),
            pltpu.VMEM((rows, width), bf16),
            pltpu.VMEM((devices // 2 - 1, rows, width), bf16),
            pltpu.VMEM((devices // 2, rows, width), bf16),
            pltpu.VMEM((rows, width), bf16),
            pltpu.VMEM((text, width), bf16),
            pltpu.VMEM(proj.shape, f32),
            pltpu.VMEM((1, own_cols), f32),
            pltpu.VMEM((count - 1, 1, own_cols), f32),
            pltpu.VMEM((scaled_rows, own_cols), bf16),
            pltpu.SemaphoreType.DMA((slots,)),
            pltpu.SemaphoreType.DMA((6,)),
            pltpu.SemaphoreType.DMA((wires,)),
            pltpu.SemaphoreType.DMA((wires,)),
        ],
        compiler_params=pltpu.CompilerParams(
            collective_id=1, has_side_effects=True, vmem_limit_bytes=62 * 2**20
        ),
    )(owner, enc, gain, w_in, w_out, final_gain, context, kv, image, proj, down, up, magnitude, scale, shift)
    image_all, key_value, gathered, ratio = outs
    if not flat_columns(own_cols):
        gathered = gathered.transpose(1, 0, 2).reshape(scaled_rows, -1)
    return image_all, key_value, gathered, ratio


def finish_kernel(
    att_ref, weight_ref, dora_ref, down_ref, grad_ref, grad_blocks_ref,
    image_out, size_out, cols_out, down_out,
    parts, stage_r, stage_l, got_r, got_l, up, up_slots, down_slots,
    cols, col_slots, col_stage, col_sums, rows_all, row_slots, row_stage, row_sums,
    size, size_slots, size_stage, size_sums,
    r_s, r_r, l_s, l_r, us, ur, ws, wr, cs, cr, c2s, c2r, as_, ar, a2s, a2r, gs, gr, g2s, g2r,
):
    count = lax.axis_size("seq")
    rank, data_rank = lax.axis_index("seq"), lax.axis_index("dp")
    rows, width = image_out.shape
    depth = att_ref.shape[1]
    half = width // 2
    f32, bf16 = jnp.float32, jnp.bfloat16
    over_rows = (((0,), (0,)), ((), ()))

    def product(k):
        block = att_ref[k * rows : (k + 1) * rows, :]
        for h in range(2):
            columns = slice(h * half, (h + 1) * half)
            parts[k, h] = jnp.dot(block, weight_ref[:depth, columns], preferred_element_type=f32).astype(bf16)

    def link(right, t, h):
        stage, got, ss, rs = (stage_r, got_r, r_s, r_r) if right else (stage_l, got_l, l_s, l_r)
        target = lax.rem(rank + (1 if right else count - 1), count)
        return pltpu.make_async_remote_copy(
            src_ref=stage.at[t - 1, h],
            dst_ref=got.at[t - 1, h],
            send_sem=ss.at[t - 1, h],
            recv_sem=rs.at[t - 1, h],
            device_id={"seq": target},
            device_id_type=pl.DeviceIdType.MESH,
        )

    def chain(t, h):
        for right in (True, False):
            stage, got = (stage_r, got_r) if right else (stage_l, got_l)
            place = rank if right else count - 1 - rank
            part = t if right else count - t

            if t == 1:

                @pl.when(place == 0)
                def _():
                    stage[0, h] = parts[part, h]
                    link(right, 1, h).start()

            else:

                @pl.when(place == 0)
                def _():
                    stage[t - 1, h] = parts[part, h]
                    link(right, t, h).start()

                @pl.when((place >= 1) & (place <= t - 1))
                def _():
                    link(right, t - 1, h).wait_recv()
                    stage[t - 1, h] = (
                        parts[part, h].astype(f32) + got[t - 2, h].astype(f32)
                    ).astype(bf16)
                    link(right, t, h).start()

    greet("seq", "dp")
    done = {0}
    for k in (1, count - 1):
        if k not in done:
            product(k)
            done.add(k)
    for h in range(2):
        chain(1, h)

    ups = jnp.dot(att_ref[...], dora_ref[...], preferred_element_type=f32).astype(bf16)
    for k in range(count):
        up[k] = ups[k * rows : (k + 1) * rows]
    small = []
    for k in range(1, count):
        before = lax.rem(rank + count - k, count)
        small.append(send(up.at[k], up_slots.at[k - 1], us.at[k - 1], ur.at[k - 1], "seq", before))
        after = lax.rem(rank + k, count)
        small.append(send(down_ref, down_slots.at[k - 1], ws.at[k - 1], wr.at[k - 1], "seq", after))
    for t in range(2, count):
        for k in (t, count - t):
            if k not in done:
                product(k)
                done.add(k)
    product(0)
    finish(small)
    up_total = up[0].astype(f32)
    for k in range(1, count):
        up_total = up_total + up_slots[k - 1].astype(f32)
    up_total = up_total.astype(bf16)
    blocks, block_rows = rows_all.shape[0], rows_all.shape[1]
    for j in range(blocks):
        cols[j] = lax.dot_general(
            up_total, grad_blocks_ref[j], over_rows, preferred_element_type=f32
        ).astype(bf16)
    grad_rows = lax.dot_general(att_ref[:rows, :], down_ref[...], over_rows, preferred_element_type=f32)
    for k in range(1, count):
        grad_rows = grad_rows + lax.dot_general(
            att_ref[k * rows : (k + 1) * rows, :], down_slots[k - 1], over_rows, preferred_element_type=f32
        )
    for j in range(blocks):
        rows_all[j] = grad_rows[j * block_rows : (j + 1) * block_rows].astype(bf16)
    first = []
    for k, peer in peers("dp"):
        first.append(send(cols.at[peer], col_slots.at[k - 1], cs.at[k - 1], cr.at[k - 1], "dp", peer))
        first.append(send(rows_all.at[peer], row_slots.at[k - 1], as_.at[k - 1], ar.at[k - 1], "dp", peer))
    second = []
    for t in range(2, count):
        for h in range(2):
            chain(t, h)
        if t == 2:
            finish(first)
            col_total = cols[data_rank].astype(f32)
            row_total = rows_all[data_rank].astype(f32)
            for k, _ in peers("dp"):
                col_total = col_total + col_slots[k - 1].astype(f32)
                row_total = row_total + row_slots[k - 1].astype(f32)
            col_stage[...] = col_total.astype(bf16)
            row_stage[...] = row_total.astype(bf16)
            for k, peer in peers("seq"):
                second.append(send(col_stage, col_sums.at[k - 1], c2s.at[k - 1], c2r.at[k - 1], "seq", peer))
            for k, peer in peers("dp"):
                second.append(
                    send(row_stage, row_sums.at[data_rank], a2s.at[k - 1], a2r.at[k - 1], "dp", peer)
                )
            row_sums[data_rank] = row_stage[...]

    for h in range(2):

        @pl.when(rank >= 1)
        def _():
            link(True, count - 1, h).wait_recv()

        @pl.when(rank <= count - 2)
        def _():
            link(False, count - 1, h).wait_recv()

        columns = slice(h * half, (h + 1) * half)
        total = parts[0, h].astype(f32)
        total = total + jnp.where(rank >= 1, got_r[count - 2, h].astype(f32), 0.0)
        total = total + jnp.where(rank <= count - 2, got_l[count - 2, h].astype(f32), 0.0)
        image_out[:, columns] = total.astype(bf16)
        size[:, columns] = jnp.sum(grad_ref[:, columns].astype(f32) * total, 0, keepdims=True)
    last = [
        send(size, size_slots.at[k - 1], gs.at[k - 1], gr.at[k - 1], "dp", peer) for k, peer in peers("dp")
    ]
    finish(second)
    col_total = col_stage[...].astype(f32)
    for k, _ in peers("seq"):
        col_total = col_total + col_sums[k - 1].astype(f32)
    cols_out[...] = col_total
    down_out[...] = row_sums[...].astype(f32)
    finish(last)
    size_total = size[...]
    for k, _ in peers("dp"):
        size_total = size_total + size_slots[k - 1]
    size_stage[...] = size_total
    finish(
        [
            send(size_stage, size_sums.at[k - 1], g2s.at[k - 1], g2r.at[k - 1], "seq", peer)
            for k, peer in peers("seq")
        ]
    )
    for k, _ in peers("seq"):
        size_total = size_total + size_sums[k - 1]
    size_out[...] = size_total
    for t in range(1, count):
        for h in range(2):

            @pl.when(rank <= t - 1)
            def _():
                link(True, t, h).wait_send()

            @pl.when(count - 1 - rank <= t - 1)
            def _():
                link(False, t, h).wait_send()


def finish_step(attended, gathered, dora, down, grad, grad_blocks):
    count, data_devices = lax.axis_size("seq"), lax.axis_size("dp")
    depth, (rows, width) = attended.shape[1], grad.shape
    rank, own_cols = down.shape[1], grad_blocks.shape[2]
    block_rows = depth // data_devices
    f32, bf16 = jnp.float32, jnp.bfloat16
    halves = (rows, width // 2)
    return pl.pallas_call(
        finish_kernel,
        out_shape=[
            jax.ShapeDtypeStruct((rows, width), bf16),
            jax.ShapeDtypeStruct((1, width), f32),
            jax.ShapeDtypeStruct((rank, own_cols), f32),
            jax.ShapeDtypeStruct((data_devices, block_rows, rank), f32),
        ],
        in_specs=[VMEM] * 6,
        out_specs=[VMEM] * 4,
        scratch_shapes=[
            pltpu.VMEM((count, 2) + halves, bf16),
        ]
        + [pltpu.VMEM((count - 1, 2) + halves, bf16)] * 4
        + [
            pltpu.VMEM((count, rows, rank), bf16),
            pltpu.VMEM((count - 1, rows, rank), bf16),
            pltpu.VMEM((count - 1, rows, rank), bf16),
            pltpu.VMEM((data_devices, rank, own_cols), bf16),
            pltpu.VMEM((data_devices - 1, rank, own_cols), bf16),
            pltpu.VMEM((rank, own_cols), bf16),
            pltpu.VMEM((count - 1, rank, own_cols), bf16),
            pltpu.VMEM((data_devices, block_rows, rank), bf16),
            pltpu.VMEM((data_devices - 1, block_rows, rank), bf16),
            pltpu.VMEM((block_rows, rank), bf16),
            pltpu.VMEM((data_devices, block_rows, rank), bf16),
            pltpu.VMEM((1, width), f32),
            pltpu.VMEM((data_devices - 1, 1, width), f32),
            pltpu.VMEM((1, width), f32),
            pltpu.VMEM((count - 1, 1, width), f32),
        ]
        + [pltpu.SemaphoreType.DMA((count - 1, 2))] * 4
        + sems(count - 1) * 2
        + sems(data_devices - 1)
        + sems(count - 1)
        + sems(data_devices - 1) * 2
        + sems(data_devices - 1)
        + sems(count - 1),
        compiler_params=pltpu.CompilerParams(
            collective_id=3, has_side_effects=True, vmem_limit_bytes=58 * 2**20
        ),
    )(attended, gathered, dora, down, grad, grad_blocks)


def on_device(
    enc_states,
    lengths,
    prompt_owner_sample,
    t5_gain,
    t5_in_weight,
    t5_out_weight,
    t5_final_gain,
    context_weight,
    text_shift,
    text_scale,
    kv_weight,
    text_key_gain,
    image_query_key_value,
    image_qk_gain,
    proj_weight,
    dora_a,
    dora_b,
    magnitude,
    grad_out,
):
    data_rank = lax.axis_index("dp")
    bf16, f32 = jnp.bfloat16, jnp.float32
    image_all, key_value, gathered, ratio = front(
        prompt_owner_sample,
        enc_states,
        t5_gain[None],
        t5_in_weight,
        t5_out_weight,
        t5_final_gain[None],
        context_weight,
        kv_weight.reshape(kv_weight.shape[0], -1),
        jnp.transpose(image_query_key_value[0], (1, 0, 2)),
        proj_weight,
        dora_a.T,
        dora_b,
        magnitude[None],
        text_scale,
        text_shift,
    )
    ratio = ratio[0]
    scaled_up = gathered[dora_a.shape[0] :]
    diffusion_length = jnp.sum(jnp.where(prompt_owner_sample == data_rank, lengths, 0))
    attended = attention(diffusion_length, text_key_gain, image_qk_gain, key_value, image_all)

    down = lax.dot_general(
        grad_out[0], scaled_up, (((1,), (1,)), ((), ())), preferred_element_type=f32
    ).astype(bf16)
    data_devices = lax.axis_size("dp")
    grad_blocks = grad_out[0].reshape(grad_out.shape[1], data_devices, -1).transpose(1, 0, 2)
    image_out, sizes, column_sums, grad_a = finish_step(
        attended, gathered, dora_a.astype(bf16), down, grad_out[0], grad_blocks
    )
    grad_a = grad_a.reshape(-1, dora_b.shape[0])
    grad_b = column_sums * ratio
    own_cols = magnitude.shape[0]
    grad_magnitude = lax.dynamic_slice_in_dim(sizes[0], data_rank * own_cols, own_cols, 0) / magnitude
    return (image_out[None], grad_a, grad_b, grad_magnitude)


def solution(mesh):
    mapped = jax.shard_map(
        on_device,
        mesh=mesh,
        in_specs=(
            P("dp", None, None),
            P(),
            P(),
            P(),
            P(None, None, "seq"),
            P("seq", None),
            P(),
            P("seq", "dp"),
            P("dp", None),
            P("dp", None),
            P("dp", None, "seq"),
            P(),
            P("dp", "seq", None, None),
            P(),
            P("seq", "dp"),
            P("seq", None),
            P(None, "dp"),
            P("dp"),
            P("dp", "seq", None),
        ),
        out_specs=(P("dp", "seq", None), P("seq", None), P(None, "dp"), P("dp")),
        check_vma=False,
    )
    return mapped
```

```python
import math

import jax
import jax.numpy as jnp
from jax import lax
from jax.experimental import pallas as pl
from jax.experimental.pallas import tpu as pltpu
from jax.sharding import PartitionSpec as P

HD = 128
MAX_PROMPT = 128
EPSILON = 1e-06


def rms_scale(values, gain):
    return values * lax.rsqrt(jnp.mean(values * values, -1, keepdims=True) + EPSILON) * gain


def peers(axis):
    size, rank = lax.axis_size(axis), lax.axis_index(axis)
    return [(k, lax.rem(rank + k, size)) for k in range(1, size)]


def greet(*axes):
    barrier = pltpu.get_barrier_semaphore()
    count = 0
    for axis in axes:
        for _, peer in peers(axis):
            pl.semaphore_signal(
                barrier, inc=1, device_id={axis: peer}, device_id_type=pl.DeviceIdType.MESH
            )
            count += 1
    pl.semaphore_wait(barrier, count)


VMEM = pl.BlockSpec(memory_space=pltpu.VMEM)
SMEM = pl.BlockSpec(memory_space=pltpu.SMEM)


MESH = pl.DeviceIdType.MESH


class Wires:
    def __init__(self, send_sems, recv_sems):
        self.send_sems, self.recv_sems, self.copies = send_sems, recv_sems, []

    def send(self, source, target, axis, peer):
        index = len(self.copies)
        copy = pltpu.make_async_remote_copy(
            src_ref=source,
            dst_ref=target,
            send_sem=self.send_sems.at[index],
            recv_sem=self.recv_sems.at[index],
            device_id={axis: peer},
            device_id_type=MESH,
        )
        copy.start()
        self.copies.append(copy)
        return copy

    def drain(self):
        for copy in self.copies:
            copy.wait_send()


class Place:
    def __init__(self):
        self.pairs = lax.axis_size("dp") // 4
        index = lax.axis_index("dp")
        self.index = index
        self.core = lax.rem(index, 2)
        self.low = lax.rem(lax.div(index, 2), 2)
        self.high = lax.div(index, 4)

    def at(self, step=0, other_low=False, other_core=False):
        high = lax.rem(self.high + step + self.pairs, self.pairs) if step else self.high
        low = 1 - self.low if other_low else self.low
        core = 1 - self.core if other_core else self.core
        return (high * 2 + low) * 2 + core


class Gather:
    def __init__(self, wires, place, own, full, view):
        self.wires, self.place, self.own, self.full, self.view = wires, place, own, full, view
        self.sibling = place.at(other_core=True)
        self.late = []

    def share(self, owner, half=None):
        where = self.view(self.full, owner, half)
        self.late.append(self.wires.send(where, where, "dp", self.sibling))

    def first(self):
        place = self.place
        mine = self.view(self.full, place.index, None)
        send = self.wires.send
        self.low = send(self.own, mine, "dp", place.at(other_low=True))
        self.high = [send(self.own, mine, "dp", place.at(j)) for j in range(1, place.pairs)]
        self.late.append(send(self.own, mine, "dp", self.sibling))

    def second(self):
        place = self.place
        send = self.wires.send
        self.relayed = []
        self.low.wait_recv()
        owner = place.at(other_low=True)
        for j in range(1, place.pairs):
            where = self.view(self.full, owner, 0)
            self.relayed.append((j, 0, send(where, where, "dp", place.at(j))))
        self.share(owner)
        for j in range(1, place.pairs):
            self.high[j - 1].wait_recv()
            owner = place.at(-j)
            where = self.view(self.full, owner, 1)
            self.relayed.append((j, 1, send(where, where, "dp", place.at(other_low=True))))
            self.share(owner)

    def third(self):
        for j, half, copy in self.relayed:
            copy.wait_recv()
            self.share(self.place.at(-j, other_low=True), half)

    def done(self):
        for copy in self.late:
            copy.wait_recv()


def by_rows(rows):
    def view(full, owner, half):
        start, size = owner * rows, rows
        if half is not None:
            size = rows // 2
            start = start + half * size
        return full.at[pl.ds(pl.multiple_of(start, 16), size)]

    return view


def by_columns(rows, width, flat):
    def view(full, owner, half):
        part = pl.ds(0, rows) if half is None else pl.ds(half * (rows // 2), rows // 2)
        if flat:
            return full.at[part, pl.ds(pl.multiple_of(owner * width, 128), width)]
        return full.at[owner, part]

    return view


def flat_columns(width):
    return width % 128 == 0


def column_shape(devices, rows, width):
    return (rows, devices * width) if flat_columns(width) else (devices, rows, width)


def tile_of(width, largest):
    return next(t for t in (largest, largest // 2, 256, 128, width) if width % t == 0)


def front_kernel(
    owner_ref, enc_ref, gain_ref, in_ref, out_ref, final_ref, context_ref, kv_ref, image_ref,
    proj_ref, down_ref, up_ref, magnitude_ref, scale_ref, shift_ref,
    image_all, key_value, gathered, ratio_ref,
    tokens, normed, in_tiles, out_all, hidden, part, sum_slots, encoded, context_all, kv_all,
    context_part, row_slots, stage, prompts, sibling_prompts, final, text_all,
    direction, squares, square_slots, own_scaled,
    in_sems, local_sems, send_sems, recv_sems,
):
    f32, bf16 = jnp.float32, jnp.bfloat16
    count, devices = lax.axis_size("seq"), lax.axis_size("dp")
    rank, data_rank = lax.axis_index("seq"), lax.axis_index("dp")
    place = Place()
    wires = Wires(send_sems, recv_sems)
    text, width_enc = tokens.shape
    feat = encoded.shape[1]
    width = context_part.shape[1]
    rows = stage.shape[0]
    slots, _, _, tile = in_tiles.shape
    tiles = hidden.shape[1] // tile
    depth, own_cols = proj_ref.shape
    flat = flat_columns(own_cols)
    late = count // 2

    def in_copy(i, slot):
        return pltpu.make_async_copy(
            in_ref.at[:, :, pl.ds(pl.multiple_of(i * tile, 128), tile)], in_tiles.at[slot], in_sems.at[slot]
        )

    def local(source, target, index):
        return pltpu.make_async_copy(source, target, local_sems.at[index])

    token_copy = local(enc_ref.at[0, pl.ds(0, text)], tokens, 0)
    token_copy.start()
    for i in range(min(slots, tiles)):
        in_copy(i, i).start()
    out_copy = local(out_ref, out_all, 1)
    out_copy.start()

    def heads_of(owner):
        head_width = image_all.shape[3]
        return pl.ds(pl.multiple_of(owner * head_width, 128), head_width)

    context_view = by_columns(context_ref.shape[0], own_cols, flat)
    scaled_view = by_columns(own_scaled.shape[0], own_cols, flat)
    kv_view = by_rows(kv_ref.shape[0])
    context_gather = Gather(wires, place, context_ref, context_all, context_view)
    kv_gather = Gather(wires, place, kv_ref, kv_all, kv_view)
    scaled_gather = Gather(wires, place, own_scaled, gathered, scaled_view)

    locals_ = [
        local(image_ref.at[:, :, heads_of(rank)], image_all.at[0], 2),
        local(context_ref, context_view(context_all, data_rank, None), 3),
        local(kv_ref, kv_view(kv_all, data_rank, None), 4),
    ]
    greet("seq", "dp")
    context_gather.first()
    image_copies = [
        wires.send(image_ref.at[:, :, heads_of(peer)], image_all.at[k], "seq", peer)
        for k, peer in peers("seq")
        if k != late
    ]

    def late_image(kind):
        peer = lax.rem(rank + late, count)
        image_copies.append(
            wires.send(image_ref.at[kind, :, heads_of(peer)], image_all.at[late, kind], "seq", peer)
        )

    for copy in locals_:
        copy.start()

    token_copy.wait()
    for r in range(0, text, 32):
        block = tokens[r : r + 32, :].astype(f32)
        normed[r : r + 32, :] = rms_scale(block, gain_ref[...]).astype(bf16)

    def in_step(i, carry):
        slot = lax.rem(i, slots)
        in_copy(i, slot).wait()
        gate = jnp.dot(normed[...], in_tiles[slot, 0], preferred_element_type=f32)
        upward = jnp.dot(normed[...], in_tiles[slot, 1], preferred_element_type=f32)
        columns = pl.ds(pl.multiple_of(i * tile, 128), tile)
        hidden[:, columns] = (jax.nn.gelu(gate, approximate=True) * upward).astype(bf16)

        @pl.when(i + slots < tiles)
        def _():
            in_copy(i + slots, slot).start()

        return carry

    lax.fori_loop(0, tiles, in_step, 0)

    out_copy.wait()
    out_tile = tile_of(feat, 512)
    sums = []
    for k in [late] + [k for k in range(1, count) if k != late] + [0]:
        owner = lax.rem(rank + k, count)
        for t in range(0, feat, out_tile):
            columns = pl.ds(pl.multiple_of(owner * feat + t, 128), out_tile)
            part[k, :, t : t + out_tile] = jnp.dot(
                hidden[...], out_all[:, columns], preferred_element_type=f32
            ).astype(bf16)
            if k:
                sums.append(
                    wires.send(
                        part.at[k, :, t : t + out_tile], sum_slots.at[k - 1, :, t : t + out_tile], "seq", owner
                    )
                )

    context_gather.second()
    kv_gather.first()

    total = jnp.zeros((1, own_cols), f32)
    for r in range(0, depth, 128):
        block = proj_ref[r : r + 128, :].astype(f32) + lax.dot_general(
            down_ref[:, r : r + 128],
            up_ref[...],
            (((0,), (0,)), ((), ())),
            precision=lax.Precision.HIGHEST,
            preferred_element_type=f32,
        )
        direction[r : r + 128, :] = block
        total = total + jnp.sum(block * block, 0, keepdims=True)
    squares[...] = total
    square_copies = [wires.send(squares, square_slots.at[k - 1], "seq", peer) for k, peer in peers("seq")]

    context_gather.third()
    for copy in sums:
        copy.wait_recv()
    late_image(0)
    own = pl.ds(pl.multiple_of(rank * feat, 128), feat)
    for r in range(0, text, 32):
        total = part[0, r : r + 32, :].astype(f32)
        for k in range(1, count):
            total = total + sum_slots[k - 1, r : r + 32, :].astype(f32)
        encoded[r : r + 32, :] = (
            (tokens[r : r + 32, own].astype(f32) + total) * final_ref[:, own]
        ).astype(bf16)

    locals_[1].wait()
    context_gather.done()
    if flat:
        step = tile_of(width, 512)
        for c in range(0, width, step):
            context_part[:, c : c + step] = jnp.dot(
                encoded[...], context_all[:, c : c + step], preferred_element_type=f32
            ).astype(bf16)
    else:
        for d in range(devices):
            context_part[:, d * own_cols : (d + 1) * own_cols] = jnp.dot(
                encoded[...], context_all[d], preferred_element_type=f32
            ).astype(bf16)

    def block_of(index):
        return pl.ds(pl.multiple_of(index * rows, 16), rows)

    row_copies = [
        wires.send(context_part.at[block_of(peer)], row_slots.at[k - 1], "seq", peer) for k, peer in peers("seq")
    ]
    kv_gather.second()
    for copy in square_copies:
        copy.wait_recv()
    total = squares[...]
    for k in range(1, count):
        total = total + square_slots[k - 1]
    ratio = magnitude_ref[...] / jnp.sqrt(total + EPSILON)
    ratio_ref[...] = ratio
    for r in range(0, depth, 128):
        own_scaled[r : r + 128, :] = (direction[r : r + 128, :] * ratio).astype(bf16)
    own_scaled[depth:, :] = (up_ref[...] * ratio).astype(bf16)

    for copy in row_copies:
        copy.wait_recv()
    total = context_part[block_of(rank), :].astype(f32)
    for k in range(1, count):
        total = total + row_slots[k - 1].astype(f32)
    stage[...] = total.astype(bf16)

    chips = devices // 2
    chip = lax.div(data_rank, 2)
    sibling = place.at(other_core=True)
    prompt_copies = [
        wires.send(stage, prompts.at[j - 1], "dp", lax.rem(chip + j, chips) * 2 + place.core)
        for j in range(1, chips)
    ]
    shared = [wires.send(stage, sibling_prompts.at[0], "dp", sibling)]
    scaled_gather.first()
    local_scaled = local(own_scaled, scaled_view(gathered, data_rank, None), 5)
    local_scaled.start()
    late_image(1)
    for j in range(1, chips):
        prompt_copies[j - 1].wait_recv()
        shared.append(wires.send(prompts.at[j - 1], sibling_prompts.at[j], "dp", sibling))
    routed = jnp.where(owner_ref[data_rank] == data_rank, stage[...].astype(f32), 0.0)
    for j in range(1, chips):
        prompt = lax.rem(chip + chips - j, chips) * 2 + place.core
        routed = routed + jnp.where(owner_ref[prompt] == data_rank, prompts[j - 1].astype(f32), 0.0)
    for j in range(chips):
        shared[j].wait_recv()
        prompt = lax.rem(chip + chips - j, chips) * 2 + 1 - place.core
        routed = routed + jnp.where(owner_ref[prompt] == data_rank, sibling_prompts[j].astype(f32), 0.0)
    centre = jnp.mean(routed, -1, keepdims=True)
    spread = jnp.mean((routed - centre) * (routed - centre), -1, keepdims=True)
    layer_normed = (routed - centre) * lax.rsqrt(spread + EPSILON)
    final[...] = ((1.0 + scale_ref[...]) * layer_normed + shift_ref[...]).astype(bf16)
    text_copies = [wires.send(final, text_all.at[block_of(rank)], "seq", peer) for _, peer in peers("seq")]
    text_all[block_of(rank), :] = final[...]
    late_image(2)
    kv_gather.third()
    scaled_gather.second()
    locals_[2].wait()
    kv_gather.done()
    for copy in text_copies:
        copy.wait_recv()
    step = tile_of(kv_all.shape[1], 512)
    for c in range(0, kv_all.shape[1], step):
        key_value[:, c : c + step] = jnp.dot(
            text_all[...], kv_all[:, c : c + step], preferred_element_type=f32
        )
    scaled_gather.third()
    locals_[0].wait()
    local_scaled.wait()
    for copy in image_copies:
        copy.wait_recv()
    scaled_gather.done()
    wires.drain()


def wires_needed(count, pairs, sum_tiles):
    others = count - 1
    gathers = 3 * (pairs + 4 * (pairs - 1) + pairs + 2)
    return others + 3 + others * (sum_tiles + 3) + 4 * pairs + gathers


def front(owner, enc, gain, w_in, w_out, final_gain, context, kv, image, proj, down, up, magnitude, scale, shift):
    count, devices = lax.axis_size("seq"), lax.axis_size("dp")
    bf16, f32 = jnp.bfloat16, jnp.float32
    width_enc, hidden = w_in.shape[1:]
    feat = width_enc // count
    text = MAX_PROMPT
    width = scale.shape[1]
    rows = text // count
    kinds, image_rows, _ = image.shape
    head_width = width // count
    own_cols = proj.shape[1]
    scaled_rows = proj.shape[0] + up.shape[0]
    tile = tile_of(hidden, 256)
    slots = 3
    wires = wires_needed(count, devices // 4, feat // tile_of(feat, 512))
    any_ = pl.BlockSpec(memory_space=pl.ANY)
    gathered_shape = column_shape(devices, scaled_rows, own_cols)
    outs = pl.pallas_call(
        front_kernel,
        out_shape=[
            jax.ShapeDtypeStruct((count, kinds, image_rows, head_width), bf16),
            jax.ShapeDtypeStruct((text, kv.shape[1]), f32),
            jax.ShapeDtypeStruct(gathered_shape, bf16),
            jax.ShapeDtypeStruct((1, own_cols), f32),
        ],
        in_specs=[SMEM, any_, VMEM, any_, any_, VMEM, any_, any_, any_] + [VMEM] * 6,
        out_specs=[VMEM] * 4,
        scratch_shapes=[
            pltpu.VMEM((text, width_enc), bf16),
            pltpu.VMEM((text, width_enc), bf16),
            pltpu.VMEM((slots, 2, width_enc, tile), bf16),
            pltpu.VMEM((hidden, width_enc), bf16),
            pltpu.VMEM((text, hidden), bf16),
            pltpu.VMEM((count, text, feat), bf16),
            pltpu.VMEM((count - 1, text, feat), bf16),
            pltpu.VMEM((text, feat), bf16),
            pltpu.VMEM(column_shape(devices, context.shape[0], own_cols), bf16),
            pltpu.VMEM((kv.shape[0] * devices, kv.shape[1]), bf16),
            pltpu.VMEM((text, width), bf16),
            pltpu.VMEM((count - 1, rows, width), bf16),
            pltpu.VMEM((rows, width), bf16),
            pltpu.VMEM((devices // 2 - 1, rows, width), bf16),
            pltpu.VMEM((devices // 2, rows, width), bf16),
            pltpu.VMEM((rows, width), bf16),
            pltpu.VMEM((text, width), bf16),
            pltpu.VMEM(proj.shape, f32),
            pltpu.VMEM((1, own_cols), f32),
            pltpu.VMEM((count - 1, 1, own_cols), f32),
            pltpu.VMEM((scaled_rows, own_cols), bf16),
            pltpu.SemaphoreType.DMA((slots,)),
            pltpu.SemaphoreType.DMA((6,)),
            pltpu.SemaphoreType.DMA((wires,)),
            pltpu.SemaphoreType.DMA((wires,)),
        ],
        compiler_params=pltpu.CompilerParams(
            collective_id=1, has_side_effects=True, vmem_limit_bytes=62 * 2**20
        ),
    )(owner, enc, gain, w_in, w_out, final_gain, context, kv, image, proj, down, up, magnitude, scale, shift)
    image_all, key_value, gathered, ratio = outs
    if not flat_columns(own_cols):
        gathered = gathered.transpose(1, 0, 2).reshape(scaled_rows, -1)
    return image_all, key_value, gathered, ratio


def back_kernel(
    owner_ref, lengths_ref, text_gain_ref, image_gain_ref, key_value_ref, image_ref, weight_ref, dora_ref,
    grad_ref, ratio_ref, magnitude_ref,
    image_out, down_out, cols_out, size_out,
    keys, values, attended, parts, slots, down, up, up_slots, down_slots,
    cols, col_slots, col_stage, col_sums, rows_all, row_slots, row_stage, row_sums,
    size, size_slots, size_stage, size_sums,
    chain_send, chain_recv, send_sems, recv_sems,
):
    count, devices = lax.axis_size("seq"), lax.axis_size("dp")
    rank, data_rank = lax.axis_index("seq"), lax.axis_index("dp")
    rows, width = image_out.shape
    depth = image_ref.shape[3]
    text = key_value_ref.shape[0]
    heads = depth // HD
    half = width // 2
    own_cols = ratio_ref.shape[1]
    block_rows = depth // devices
    f32, bf16 = jnp.float32, jnp.bfloat16
    over_rows = (((0,), (0,)), ((), ()))
    over_columns = (((1,), (1,)), ((), ()))
    wires = Wires(send_sems, recv_sems)
    near = 1 - lax.div(rank, count // 2)

    def target_of(step, right):
        return right * (count - 1 - step) + (1 - right) * step

    def block_of(owner):
        return lax.rem(rank + count - owner, count)

    def link(owner, h, right):
        index = (right * count + owner) * 2 + h
        return pltpu.make_async_remote_copy(
            src_ref=parts.at[owner, h],
            dst_ref=slots.at[right, owner, h],
            send_sem=chain_send.at[owner * 2 + h],
            recv_sem=chain_recv.at[index],
            device_id={"seq": jnp.clip(rank + 2 * right - 1, 0, count - 1)},
            device_id_type=MESH,
        )

    def begin(step):
        owner = target_of(step, near)

        @pl.when((rank == 0) | (rank == count - 1))
        def _():
            for h in range(2):
                link(owner, h, near).start()

    def forward(step, right):
        owner = target_of(step, right)
        ahead = right * (owner - rank) + (1 - right) * (rank - owner)
        behind = right * rank + (1 - right) * (count - 1 - rank)

        @pl.when((ahead > 0) & (behind > 0))
        def _():
            for h in range(2):
                link(owner, h, right).wait_recv()
                parts[owner, h] = (parts[owner, h].astype(f32) + slots[right, owner, h].astype(f32)).astype(bf16)
                link(owner, h, right).start()

    greet("seq", "dp")
    down[...] = lax.dot_general(
        grad_ref[...], weight_ref[depth:, :], over_columns, preferred_element_type=f32
    ).astype(bf16)
    small = []
    for k, peer in peers("seq"):
        small.append(wires.send(down, down_slots.at[k - 1], "seq", peer))

    length = jnp.int32(0)
    for p in range(devices):
        length = length + jnp.where(owner_ref[p] == data_rank, lengths_ref[p], 0)

    def head(h):
        return pl.ds(pl.multiple_of(h * HD, HD), HD)

    def key_step(h, carry):
        keys[:text, head(h)] = rms_scale(key_value_ref[:, head(h)], text_gain_ref[...]).astype(bf16)
        for k in range(count):
            start = text + k * rows
            keys[start : start + rows, head(h)] = rms_scale(
                image_ref[k, 1, :, head(h)].astype(f32), image_gain_ref[1:2, :]
            ).astype(bf16)
        return carry

    lax.fori_loop(0, heads, key_step, 0)
    values[:text, :] = key_value_ref[:, depth:].astype(bf16)
    for k in range(count):
        start = text + k * rows
        values[start : start + rows, :] = image_ref[k, 2]
    scale = 1.0 / math.sqrt(HD)

    for step in range(count):
        owner = target_of(step, near)
        block = block_of(owner)
        block_slice = pl.ds(pl.multiple_of(block * rows, 16), rows)

        def head_step(h, carry):
            queries = rms_scale(
                image_ref[block, 0, :, head(h)].astype(f32), image_gain_ref[0:1, :]
            ).astype(bf16)
            scores = lax.dot_general(queries, keys[:, head(h)], over_columns, preferred_element_type=f32) * scale
            position = lax.broadcasted_iota(jnp.int32, scores.shape, 1)
            weight = jnp.where((position < length) | (position >= text), jnp.exp(scores), 0.0)
            denominator = jnp.sum(weight, -1, keepdims=True)
            mixture = jnp.dot(weight.astype(bf16), values[:, head(h)], preferred_element_type=f32)
            attended[block_slice, head(h)] = (mixture / denominator).astype(bf16)
            return carry

        lax.fori_loop(0, heads, head_step, 0)
        for h in range(2):
            columns = slice(h * half, (h + 1) * half)
            parts[owner, h] = jnp.dot(
                attended[block_slice, :], weight_ref[:depth, columns], preferred_element_type=f32
            ).astype(bf16)
        if step == 0:
            begin(0)

    dora = dora_ref[...].astype(bf16)
    ups = lax.dot_general(attended[...], dora, over_columns, preferred_element_type=f32).astype(bf16)
    for k in range(count):
        up[k] = ups[k * rows : (k + 1) * rows]
    for k in range(1, count):
        before = lax.rem(rank + count - k, count)
        small.append(wires.send(up.at[k], up_slots.at[k - 1], "seq", before))
    for step in range(1, count - 2):
        begin(step)
    forward(0, near)
    for copy in small:
        copy.wait_recv()
    up_total = up[0].astype(f32)
    for k in range(1, count):
        up_total = up_total + up_slots[k - 1].astype(f32)
    up_total = up_total.astype(bf16)
    column_grad = lax.dot_general(up_total, grad_ref[...], over_rows, preferred_element_type=f32).astype(bf16)
    for j in range(devices):
        cols[j] = column_grad[:, j * own_cols : (j + 1) * own_cols]
    row_grad = lax.dot_general(down[...], attended[:rows, :], over_rows, preferred_element_type=f32)
    for k in range(1, count):
        row_grad = row_grad + lax.dot_general(
            down_slots[k - 1], attended[k * rows : (k + 1) * rows, :], over_rows, preferred_element_type=f32
        )
    for j in range(devices):
        rows_all[j] = row_grad[:, j * block_rows : (j + 1) * block_rows].astype(bf16)
    first = []
    for k, peer in peers("dp"):
        first.append(wires.send(cols.at[peer], col_slots.at[k - 1], "dp", peer))
        first.append(wires.send(rows_all.at[peer], row_slots.at[k - 1], "dp", peer))
    for copy in first:
        copy.wait_recv()
    col_total = cols[data_rank].astype(f32)
    row_total = rows_all[data_rank].astype(f32)
    for k, _ in peers("dp"):
        col_total = col_total + col_slots[k - 1].astype(f32)
        row_total = row_total + row_slots[k - 1].astype(f32)
    col_stage[...] = col_total.astype(bf16)
    row_stage[...] = row_total.astype(bf16)
    second = []
    for k, peer in peers("seq"):
        second.append(wires.send(col_stage, col_sums.at[k - 1], "seq", peer))
    for k, peer in peers("dp"):
        second.append(wires.send(row_stage, row_sums.at[data_rank], "dp", peer))
    row_sums[data_rank] = row_stage[...]
    begin(count - 2)
    forward(0, 1 - near)
    for step in range(1, count - 1):
        forward(step, near)
        forward(step, 1 - near)

    sums = []
    for h in range(2):

        @pl.when(rank >= 1)
        def _():
            link(rank, h, 1).wait_recv()

        @pl.when(rank <= count - 2)
        def _():
            link(rank, h, 0).wait_recv()

        columns = slice(h * half, (h + 1) * half)
        total = parts[rank, h].astype(f32)
        total = total + jnp.where(rank >= 1, slots[1, rank, h].astype(f32), 0.0)
        total = total + jnp.where(rank <= count - 2, slots[0, rank, h].astype(f32), 0.0)
        image_out[:, columns] = total.astype(bf16)
        sums.append(jnp.sum(grad_ref[:, columns].astype(f32) * total, 0, keepdims=True))
    per_half = devices // 2
    for d in range(devices):
        start = (d % per_half) * own_cols
        size[d] = sums[d // per_half][:, start : start + own_cols]
    last = [wires.send(size.at[peer], size_slots.at[k - 1], "dp", peer) for k, peer in peers("dp")]
    for copy in second:
        copy.wait_recv()
    col_total = col_stage[...].astype(f32)
    for k, _ in peers("seq"):
        col_total = col_total + col_sums[k - 1].astype(f32)
    cols_out[...] = col_total * ratio_ref[...]
    for d in range(devices):
        down_out[:, d * block_rows : (d + 1) * block_rows] = row_sums[d].astype(f32)
    for copy in last:
        copy.wait_recv()
    size_total = size[data_rank]
    for k, _ in peers("dp"):
        size_total = size_total + size_slots[k - 1]
    size_stage[...] = size_total
    last = [wires.send(size_stage, size_sums.at[k - 1], "seq", peer) for k, peer in peers("seq")]
    for copy in last:
        copy.wait_recv()
    for k, _ in peers("seq"):
        size_total = size_total + size_sums[k - 1]
    size_out[...] = size_total / magnitude_ref[...]
    for owner in range(count):

        @pl.when(rank != owner)
        def _():
            for h in range(2):
                link(owner, h, 0).wait_send()

    wires.drain()


def back(owner, lengths, text_gain, image_gain, key_value, image, gathered, dora, grad, ratio, magnitude):
    count, devices = lax.axis_size("seq"), lax.axis_size("dp")
    rows, width = grad.shape
    rank, depth = dora.shape
    text = key_value.shape[0]
    own_cols = ratio.shape[1]
    block_rows = depth // devices
    f32, bf16 = jnp.float32, jnp.bfloat16
    others, data_others = count - 1, devices - 1
    wires = 4 * others + 4 * data_others
    return pl.pallas_call(
        back_kernel,
        out_shape=[
            jax.ShapeDtypeStruct((rows, width), bf16),
            jax.ShapeDtypeStruct((rank, depth), f32),
            jax.ShapeDtypeStruct((rank, own_cols), f32),
            jax.ShapeDtypeStruct((1, own_cols), f32),
        ],
        in_specs=[SMEM] * 2 + [VMEM] * 9,
        out_specs=[VMEM] * 4,
        scratch_shapes=[
            pltpu.VMEM((text + count * rows, depth), bf16),
            pltpu.VMEM((text + count * rows, depth), bf16),
            pltpu.VMEM((count * rows, depth), bf16),
            pltpu.VMEM((count, 2, rows, width // 2), bf16),
            pltpu.VMEM((2, count, 2, rows, width // 2), bf16),
            pltpu.VMEM((rows, rank), bf16),
            pltpu.VMEM((count, rows, rank), bf16),
            pltpu.VMEM((others, rows, rank), bf16),
            pltpu.VMEM((others, rows, rank), bf16),
            pltpu.VMEM((devices, rank, own_cols), bf16),
            pltpu.VMEM((data_others, rank, own_cols), bf16),
            pltpu.VMEM((rank, own_cols), bf16),
            pltpu.VMEM((others, rank, own_cols), bf16),
            pltpu.VMEM((devices, rank, block_rows), bf16),
            pltpu.VMEM((data_others, rank, block_rows), bf16),
            pltpu.VMEM((rank, block_rows), bf16),
            pltpu.VMEM((devices, rank, block_rows), bf16),
            pltpu.VMEM((devices, 1, own_cols), f32),
            pltpu.VMEM((data_others, 1, own_cols), f32),
            pltpu.VMEM((1, own_cols), f32),
            pltpu.VMEM((others, 1, own_cols), f32),
            pltpu.SemaphoreType.DMA((count * 2,)),
            pltpu.SemaphoreType.DMA((count * 4,)),
            pltpu.SemaphoreType.DMA((wires,)),
            pltpu.SemaphoreType.DMA((wires,)),
        ],
        compiler_params=pltpu.CompilerParams(
            collective_id=3, has_side_effects=True, vmem_limit_bytes=58 * 2**20
        ),
    )(owner, lengths, text_gain, image_gain, key_value, image, gathered, dora, grad, ratio, magnitude)


def on_device(
    enc_states,
    lengths,
    prompt_owner_sample,
    t5_gain,
    t5_in_weight,
    t5_out_weight,
    t5_final_gain,
    context_weight,
    text_shift,
    text_scale,
    kv_weight,
    text_key_gain,
    image_query_key_value,
    image_qk_gain,
    proj_weight,
    dora_a,
    dora_b,
    magnitude,
    grad_out,
):
    down = dora_a.T
    image_all, key_value, gathered, ratio = front(
        prompt_owner_sample,
        enc_states,
        t5_gain[None],
        t5_in_weight,
        t5_out_weight,
        t5_final_gain[None],
        context_weight,
        kv_weight.reshape(kv_weight.shape[0], -1),
        jnp.transpose(image_query_key_value[0], (1, 0, 2)),
        proj_weight,
        down,
        dora_b,
        magnitude[None],
        text_scale,
        text_shift,
    )
    image_out, grad_a, grad_b, grad_magnitude = back(
        prompt_owner_sample,
        lengths,
        text_key_gain[None],
        image_qk_gain,
        key_value,
        image_all,
        gathered,
        down,
        grad_out[0],
        ratio,
        magnitude[None],
    )
    return (image_out[None], grad_a.T, grad_b, grad_magnitude[0])


def solution(mesh):
    mapped = jax.shard_map(
        on_device,
        mesh=mesh,
        in_specs=(
            P("dp", None, None),
            P(),
            P(),
            P(),
            P(None, None, "seq"),
            P("seq", None),
            P(),
            P("seq", "dp"),
            P("dp", None),
            P("dp", None),
            P("dp", None, "seq"),
            P(),
            P("dp", "seq", None, None),
            P(),
            P("seq", "dp"),
            P("seq", None),
            P(None, "dp"),
            P("dp"),
            P("dp", "seq", None),
        ),
        out_specs=(P("dp", "seq", None), P("seq", None), P(None, "dp"), P("dp")),
        check_vma=False,
    )
    return mapped
```

```python
import math

import jax
import jax.numpy as jnp
from jax import lax
from jax.experimental import pallas as pl
from jax.experimental.pallas import tpu as pltpu
from jax.sharding import PartitionSpec as P

HD = 128
MAX_PROMPT = 128
EPSILON = 1e-06


def rms_scale(values, gain):
    return values * lax.rsqrt(jnp.mean(values * values, -1, keepdims=True) + EPSILON) * gain


def peers(axis):
    size, rank = lax.axis_size(axis), lax.axis_index(axis)
    return [(k, lax.rem(rank + k, size)) for k in range(1, size)]


def greet(*axes):
    barrier = pltpu.get_barrier_semaphore()
    count = 0
    for axis in axes:
        for _, peer in peers(axis):
            pl.semaphore_signal(
                barrier, inc=1, device_id={axis: peer}, device_id_type=pl.DeviceIdType.MESH
            )
            count += 1
    pl.semaphore_wait(barrier, count)


VMEM = pl.BlockSpec(memory_space=pltpu.VMEM)
SMEM = pl.BlockSpec(memory_space=pltpu.SMEM)


MESH = pl.DeviceIdType.MESH


class Wires:
    def __init__(self, send_sems, recv_sems):
        self.send_sems, self.recv_sems, self.copies = send_sems, recv_sems, []

    def send(self, source, target, axis, peer):
        index = len(self.copies)
        copy = pltpu.make_async_remote_copy(
            src_ref=source,
            dst_ref=target,
            send_sem=self.send_sems.at[index],
            recv_sem=self.recv_sems.at[index],
            device_id={axis: peer},
            device_id_type=MESH,
        )
        copy.start()
        self.copies.append(copy)
        return copy

    def drain(self):
        for copy in self.copies:
            copy.wait_send()


class Place:
    def __init__(self):
        self.pairs = lax.axis_size("dp") // 4
        index = lax.axis_index("dp")
        self.index = index
        self.core = lax.rem(index, 2)
        self.low = lax.rem(lax.div(index, 2), 2)
        self.high = lax.div(index, 4)

    def at(self, step=0, other_low=False, other_core=False):
        high = lax.rem(self.high + step + self.pairs, self.pairs) if step else self.high
        low = 1 - self.low if other_low else self.low
        core = 1 - self.core if other_core else self.core
        return (high * 2 + low) * 2 + core


class Gather:
    def __init__(self, wires, place, own, full, view):
        self.wires, self.place, self.own, self.full, self.view = wires, place, own, full, view
        self.sibling = place.at(other_core=True)
        self.late = []

    def share(self, owner, half=None):
        where = self.view(self.full, owner, half)
        self.late.append(self.wires.send(where, where, "dp", self.sibling))

    def first(self):
        place = self.place
        mine = self.view(self.full, place.index, None)
        send = self.wires.send
        self.low = send(self.own, mine, "dp", place.at(other_low=True))
        self.high = [send(self.own, mine, "dp", place.at(j)) for j in range(1, place.pairs)]
        self.late.append(send(self.own, mine, "dp", self.sibling))

    def second(self):
        place = self.place
        send = self.wires.send
        self.relayed = []
        self.low.wait_recv()
        owner = place.at(other_low=True)
        for j in range(1, place.pairs):
            where = self.view(self.full, owner, 0)
            self.relayed.append((j, 0, send(where, where, "dp", place.at(j))))
        self.share(owner)
        for j in range(1, place.pairs):
            self.high[j - 1].wait_recv()
            owner = place.at(-j)
            where = self.view(self.full, owner, 1)
            self.relayed.append((j, 1, send(where, where, "dp", place.at(other_low=True))))
            self.share(owner)

    def third(self):
        for j, half, copy in self.relayed:
            copy.wait_recv()
            self.share(self.place.at(-j, other_low=True), half)

    def done(self):
        for copy in self.late:
            copy.wait_recv()


def by_rows(rows):
    def view(full, owner, half):
        start, size = owner * rows, rows
        if half is not None:
            size = rows // 2
            start = start + half * size
        return full.at[pl.ds(pl.multiple_of(start, 16), size)]

    return view


def by_columns(rows, width, flat):
    def view(full, owner, half):
        part = pl.ds(0, rows) if half is None else pl.ds(half * (rows // 2), rows // 2)
        if flat:
            return full.at[part, pl.ds(pl.multiple_of(owner * width, 128), width)]
        return full.at[owner, part]

    return view


def flat_columns(width):
    return width % 128 == 0


def column_shape(devices, rows, width):
    return (rows, devices * width) if flat_columns(width) else (devices, rows, width)


def tile_of(width, largest):
    return next(t for t in (largest, largest // 2, 256, 128, width) if width % t == 0)


class Chain:
    def __init__(self, part, slot, send_sems, recv_sems, chunks):
        self.part, self.slot, self.chunks = part, slot, chunks
        self.send_sems, self.recv_sems = send_sems, recv_sems
        self.count, self.rank = lax.axis_size("seq"), lax.axis_index("seq")
        self.near = 1 - lax.div(self.rank, self.count // 2)
        self.far = 1 - self.near

    def target(self, step, right):
        return right * (self.count - 1 - step) + (1 - right) * step

    def link(self, owner, c, right):
        return pltpu.make_async_remote_copy(
            src_ref=self.part(owner, c),
            dst_ref=self.slot(right, owner, c),
            send_sem=self.send_sems.at[owner * self.chunks + c],
            recv_sem=self.recv_sems.at[(right * self.count + owner) * self.chunks + c],
            device_id={"seq": jnp.clip(self.rank + 2 * right - 1, 0, self.count - 1)},
            device_id_type=MESH,
        )

    def begin(self, step, chunks=None):
        owner = self.target(step, self.near)

        @pl.when((self.rank == 0) | (self.rank == self.count - 1))
        def _():
            for c in range(self.chunks) if chunks is None else chunks:
                self.link(owner, c, self.near).start()

    def forward(self, step, right, chunks=None):
        owner = self.target(step, right)
        ahead = right * (owner - self.rank) + (1 - right) * (self.rank - owner)
        behind = right * self.rank + (1 - right) * (self.count - 1 - self.rank)

        @pl.when((ahead > 0) & (behind > 0))
        def _():
            for c in range(self.chunks) if chunks is None else chunks:
                self.link(owner, c, right).wait_recv()
                part = self.part(owner, c)
                part[...] = (
                    part[...].astype(jnp.float32) + self.slot(right, owner, c)[...].astype(jnp.float32)
                ).astype(part.dtype)
                self.link(owner, c, right).start()

    def arrive(self, c):
        @pl.when(self.rank >= 1)
        def _():
            self.link(self.rank, c, 1).wait_recv()

        @pl.when(self.rank <= self.count - 2)
        def _():
            self.link(self.rank, c, 0).wait_recv()

    def total(self, part, from_left, from_right):
        total = part.astype(jnp.float32)
        total = total + jnp.where(self.rank >= 1, from_left.astype(jnp.float32), 0.0)
        return total + jnp.where(self.rank <= self.count - 2, from_right.astype(jnp.float32), 0.0)

    def drain(self):
        for owner in range(self.count):

            @pl.when(self.rank != owner)
            def _():
                for c in range(self.chunks):
                    self.link(owner, c, 0).wait_send()


class Relay:
    def __init__(self, block, send_sems, recv_sems):
        self.block, self.send_sems, self.recv_sems = block, send_sems, recv_sems
        self.count, self.rank = lax.axis_size("seq"), lax.axis_index("seq")

    def link(self, owner, hop, right):
        index = right * (self.count - 1) + hop
        where = self.block(owner)
        return pltpu.make_async_remote_copy(
            src_ref=where,
            dst_ref=where,
            send_sem=self.send_sems.at[index],
            recv_sem=self.recv_sems.at[index],
            device_id={"seq": jnp.clip(self.rank + 2 * right - 1, 0, self.count - 1)},
            device_id_type=MESH,
        )

    def reaches(self, right):
        return self.rank < self.count - 1 if right else self.rank > 0

    def begin(self):
        for right in (1, 0):

            @pl.when(self.reaches(right))
            def _():
                self.link(self.rank, 0, right).start()

    def forward(self, hop):
        for right in (1, 0):
            owner = self.rank - hop if right else self.rank + hop
            there = owner >= 0 if right else owner < self.count
            owner = jnp.clip(owner, 0, self.count - 1)

            @pl.when(there)
            def _():
                self.link(owner, hop - 1, right).wait_recv()

            if hop < self.count - 1:

                @pl.when(there & self.reaches(right))
                def _():
                    self.link(owner, hop, right).start()

    def drain(self):
        for hop in range(self.count - 1):
            for right in (1, 0):
                owner = self.rank - hop if right else self.rank + hop
                there = owner >= 0 if right else owner < self.count

                @pl.when(there & self.reaches(right))
                def _():
                    self.link(self.rank, hop, right).wait_send()


def front_kernel(
    owner_ref, enc_ref, gain_ref, in_ref, out_ref, final_ref, context_ref, kv_ref, image_ref,
    proj_ref, down_ref, up_ref, magnitude_ref, scale_ref, shift_ref,
    image_all, key_value, gathered, ratio_ref,
    tokens, normed, in_tiles, out_all, hidden, part, sum_slots, encoded, context_all, kv_all,
    context_part, row_slots, stage, prompts, sibling_prompts, text_all,
    direction, squares, square_slots, own_scaled,
    in_sems, local_sems, send_sems, recv_sems, sum_send, sum_recv, row_send, row_recv, text_send, text_recv,
):
    f32, bf16 = jnp.float32, jnp.bfloat16
    count, devices = lax.axis_size("seq"), lax.axis_size("dp")
    rank, data_rank = lax.axis_index("seq"), lax.axis_index("dp")
    place = Place()
    wires = Wires(send_sems, recv_sems)
    text, width_enc = tokens.shape
    feat = encoded.shape[1]
    width = context_part.shape[1]
    rows = stage.shape[0]
    slots, _, _, tile = in_tiles.shape
    tiles = hidden.shape[1] // tile
    depth, own_cols = proj_ref.shape
    flat = flat_columns(own_cols)
    late = count // 2

    def in_copy(i, slot):
        return pltpu.make_async_copy(
            in_ref.at[:, :, pl.ds(pl.multiple_of(i * tile, 128), tile)], in_tiles.at[slot], in_sems.at[slot]
        )

    def local(source, target, index):
        return pltpu.make_async_copy(source, target, local_sems.at[index])

    token_copy = local(enc_ref.at[0, pl.ds(0, text)], tokens, 0)
    token_copy.start()
    for i in range(min(slots, tiles)):
        in_copy(i, i).start()
    out_copy = local(out_ref, out_all, 1)
    out_copy.start()

    def heads_of(owner):
        head_width = image_all.shape[3]
        return pl.ds(pl.multiple_of(owner * head_width, 128), head_width)

    context_view = by_columns(context_ref.shape[0], own_cols, flat)
    scaled_view = by_columns(own_scaled.shape[0], own_cols, flat)
    kv_view = by_rows(kv_ref.shape[0])
    context_gather = Gather(wires, place, context_ref, context_all, context_view)
    kv_gather = Gather(wires, place, kv_ref, kv_all, kv_view)
    scaled_gather = Gather(wires, place, own_scaled, gathered, scaled_view)

    locals_ = [
        local(image_ref.at[:, :, heads_of(rank)], image_all.at[0], 2),
        local(context_ref, context_view(context_all, data_rank, None), 3),
        local(kv_ref, kv_view(kv_all, data_rank, None), 4),
    ]
    greet("seq", "dp")
    context_gather.first()
    image_copies = []

    def image(k, kind):
        peer = lax.rem(rank + k, count)
        image_copies.append(wires.send(image_ref.at[kind, :, heads_of(peer)], image_all.at[k, kind], "seq", peer))

    def images(kinds):
        for k in range(2, count):
            if k != late:
                for kind in kinds:
                    image(k, kind)

    for kind in range(3):
        image(1, kind)

    for copy in locals_:
        copy.start()

    token_copy.wait()
    for r in range(0, text, 32):
        block = tokens[r : r + 32, :].astype(f32)
        normed[r : r + 32, :] = rms_scale(block, gain_ref[...]).astype(bf16)

    def in_step(i, carry):
        slot = lax.rem(i, slots)
        in_copy(i, slot).wait()
        gate = jnp.dot(normed[...], in_tiles[slot, 0], preferred_element_type=f32)
        upward = jnp.dot(normed[...], in_tiles[slot, 1], preferred_element_type=f32)
        columns = pl.ds(pl.multiple_of(i * tile, 128), tile)
        hidden[:, columns] = (jax.nn.gelu(gate, approximate=True) * upward).astype(bf16)

        @pl.when(i + slots < tiles)
        def _():
            in_copy(i + slots, slot).start()

        return carry

    lax.fori_loop(0, tiles, in_step, 0)

    out_copy.wait()
    out_tile = tile_of(feat, 512)

    def piece(c):
        return slice(c * out_tile, (c + 1) * out_tile)

    sums = Chain(
        lambda owner, c: part.at[owner, :, piece(c)],
        lambda right, owner, c: sum_slots.at[right, owner, :, piece(c)],
        sum_send,
        sum_recv,
        feat // out_tile,
    )
    if late > 1:
        image(late, 0)
    for step in range(count):
        owner = sums.target(step, sums.near)
        for c in range(sums.chunks):
            columns = pl.ds(pl.multiple_of(owner * feat + c * out_tile, 128), out_tile)
            part[owner, :, piece(c)] = jnp.dot(
                hidden[...], out_all[:, columns], preferred_element_type=f32
            ).astype(bf16)
            if step < count - 1:
                sums.begin(step, (c,))

    context_gather.second()
    kv_gather.first()

    total = jnp.zeros((1, own_cols), f32)
    for r in range(0, depth, 128):
        block = proj_ref[r : r + 128, :].astype(f32) + lax.dot_general(
            down_ref[:, r : r + 128],
            up_ref[...],
            (((0,), (0,)), ((), ())),
            precision=lax.Precision.HIGHEST,
            preferred_element_type=f32,
        )
        direction[r : r + 128, :] = block
        total = total + jnp.sum(block * block, 0, keepdims=True)
    squares[...] = total
    square_copies = [wires.send(squares, square_slots.at[k - 1], "seq", peer) for k, peer in peers("seq")]

    for step in range(count - 1):
        sums.forward(step, sums.near)
        sums.forward(step, sums.far)
    context_gather.third()
    for c in range(sums.chunks):
        sums.arrive(c)
    images((0,))
    own = pl.ds(pl.multiple_of(rank * feat, 128), feat)
    for r in range(0, text, 32):
        block = slice(r, r + 32)
        total = sums.total(part[rank, block, :], sum_slots[1, rank, block, :], sum_slots[0, rank, block, :])
        encoded[block, :] = ((tokens[block, own].astype(f32) + total) * final_ref[:, own]).astype(bf16)

    locals_[1].wait()
    context_gather.done()
    if late > 1:
        image(late, 1)

    def block_of(index):
        return pl.ds(pl.multiple_of(index * rows, 16), rows)

    half = width // 2
    row_sums = Chain(
        lambda owner, c: context_part.at[block_of(owner), c * half : (c + 1) * half],
        lambda right, owner, c: row_slots.at[right, owner, :, c * half : (c + 1) * half],
        row_send,
        row_recv,
        2,
    )
    for c in range(2):
        if flat:
            step = tile_of(half, 512)
            for start in range(c * half, (c + 1) * half, step):
                context_part[:, start : start + step] = jnp.dot(
                    encoded[...], context_all[:, start : start + step], preferred_element_type=f32
                ).astype(bf16)
        else:
            for d in range(c * devices // 2, (c + 1) * devices // 2):
                context_part[:, d * own_cols : (d + 1) * own_cols] = jnp.dot(
                    encoded[...], context_all[d], preferred_element_type=f32
                ).astype(bf16)
        for step in range(count - 1):
            row_sums.begin(step, (c,))
    for copy in square_copies:
        copy.wait_recv()
    total = squares[...]
    for k in range(1, count):
        total = total + square_slots[k - 1]
    ratio = magnitude_ref[...] / jnp.sqrt(total + EPSILON)
    ratio_ref[...] = ratio
    for r in range(0, depth, 128):
        own_scaled[r : r + 128, :] = (direction[r : r + 128, :] * ratio).astype(bf16)
    own_scaled[depth:, :] = (up_ref[...] * ratio).astype(bf16)

    for c in range(2):
        for step in range(count - 1):
            row_sums.forward(step, row_sums.near, (c,))
            row_sums.forward(step, row_sums.far, (c,))
    for c in range(2):
        row_sums.arrive(c)
    stage[...] = row_sums.total(
        context_part[block_of(rank), :], row_slots[1, rank], row_slots[0, rank]
    ).astype(bf16)

    chips = devices // 2
    chip = lax.div(data_rank, 2)
    sibling = place.at(other_core=True)
    prompt_copies = [
        wires.send(stage, prompts.at[j - 1], "dp", lax.rem(chip + j, chips) * 2 + place.core)
        for j in range(1, chips)
    ]
    shared = [wires.send(stage, sibling_prompts.at[0], "dp", sibling)]
    images((1, 2))
    kv_gather.second()
    local_scaled = local(own_scaled, scaled_view(gathered, data_rank, None), 5)
    local_scaled.start()
    for j in range(1, chips):
        prompt_copies[j - 1].wait_recv()
        shared.append(wires.send(prompts.at[j - 1], sibling_prompts.at[j], "dp", sibling))
    routed = jnp.where(owner_ref[data_rank] == data_rank, stage[...].astype(f32), 0.0)
    for j in range(1, chips):
        prompt = lax.rem(chip + chips - j, chips) * 2 + place.core
        routed = routed + jnp.where(owner_ref[prompt] == data_rank, prompts[j - 1].astype(f32), 0.0)
    for j in range(chips):
        shared[j].wait_recv()
        prompt = lax.rem(chip + chips - j, chips) * 2 + 1 - place.core
        routed = routed + jnp.where(owner_ref[prompt] == data_rank, sibling_prompts[j].astype(f32), 0.0)
    centre = jnp.mean(routed, -1, keepdims=True)
    spread = jnp.mean((routed - centre) * (routed - centre), -1, keepdims=True)
    layer_normed = (routed - centre) * lax.rsqrt(spread + EPSILON)
    text_all[block_of(rank), :] = ((1.0 + scale_ref[...]) * layer_normed + shift_ref[...]).astype(bf16)
    scaled_gather.first()
    if late > 1:
        image(late, 2)
    texts = Relay(lambda owner: text_all.at[block_of(owner)], text_send, text_recv)
    texts.begin()
    for hop in range(1, count):
        texts.forward(hop)
    kv_gather.third()
    locals_[2].wait()
    kv_gather.done()
    step = tile_of(kv_all.shape[1], 512)
    for c in range(0, kv_all.shape[1], step):
        key_value[:, c : c + step] = jnp.dot(
            text_all[...], kv_all[:, c : c + step], preferred_element_type=f32
        )
    scaled_gather.second()
    scaled_gather.third()
    locals_[0].wait()
    local_scaled.wait()
    for copy in image_copies:
        copy.wait_recv()
    scaled_gather.done()
    sums.drain()
    row_sums.drain()
    texts.drain()
    wires.drain()


def wires_needed(count, pairs):
    others = count - 1
    gathers = 3 * (pairs + 4 * (pairs - 1) + pairs + 2)
    return 4 * others + 4 * pairs + gathers


def front(owner, enc, gain, w_in, w_out, final_gain, context, kv, image, proj, down, up, magnitude, scale, shift):
    count, devices = lax.axis_size("seq"), lax.axis_size("dp")
    bf16, f32 = jnp.bfloat16, jnp.float32
    width_enc, hidden = w_in.shape[1:]
    feat = width_enc // count
    text = MAX_PROMPT
    width = scale.shape[1]
    rows = text // count
    kinds, image_rows, _ = image.shape
    head_width = width // count
    own_cols = proj.shape[1]
    scaled_rows = proj.shape[0] + up.shape[0]
    tile = tile_of(hidden, 256)
    slots = 3
    pieces = feat // tile_of(feat, 512)
    wires = wires_needed(count, devices // 4)
    any_ = pl.BlockSpec(memory_space=pl.ANY)
    gathered_shape = column_shape(devices, scaled_rows, own_cols)
    outs = pl.pallas_call(
        front_kernel,
        out_shape=[
            jax.ShapeDtypeStruct((count, kinds, image_rows, head_width), bf16),
            jax.ShapeDtypeStruct((text, kv.shape[1]), f32),
            jax.ShapeDtypeStruct(gathered_shape, bf16),
            jax.ShapeDtypeStruct((1, own_cols), f32),
        ],
        in_specs=[SMEM, any_, VMEM, any_, any_, VMEM, any_, any_, any_] + [VMEM] * 6,
        out_specs=[VMEM] * 4,
        scratch_shapes=[
            pltpu.VMEM((text, width_enc), bf16),
            pltpu.VMEM((text, width_enc), bf16),
            pltpu.VMEM((slots, 2, width_enc, tile), bf16),
            pltpu.VMEM((hidden, width_enc), bf16),
            pltpu.VMEM((text, hidden), bf16),
            pltpu.VMEM((count, text, feat), bf16),
            pltpu.VMEM((2, count, text, feat), bf16),
            pltpu.VMEM((text, feat), bf16),
            pltpu.VMEM(column_shape(devices, context.shape[0], own_cols), bf16),
            pltpu.VMEM((kv.shape[0] * devices, kv.shape[1]), bf16),
            pltpu.VMEM((text, width), bf16),
            pltpu.VMEM((2, count, rows, width), bf16),
            pltpu.VMEM((rows, width), bf16),
            pltpu.VMEM((devices // 2 - 1, rows, width), bf16),
            pltpu.VMEM((devices // 2, rows, width), bf16),
            pltpu.VMEM((text, width), bf16),
            pltpu.VMEM(proj.shape, f32),
            pltpu.VMEM((1, own_cols), f32),
            pltpu.VMEM((count - 1, 1, own_cols), f32),
            pltpu.VMEM((scaled_rows, own_cols), bf16),
            pltpu.SemaphoreType.DMA((slots,)),
            pltpu.SemaphoreType.DMA((6,)),
            pltpu.SemaphoreType.DMA((wires,)),
            pltpu.SemaphoreType.DMA((wires,)),
            pltpu.SemaphoreType.DMA((count * pieces,)),
            pltpu.SemaphoreType.DMA((count * 2 * pieces,)),
            pltpu.SemaphoreType.DMA((count * 2,)),
            pltpu.SemaphoreType.DMA((count * 4,)),
            pltpu.SemaphoreType.DMA((count * 2,)),
            pltpu.SemaphoreType.DMA((count * 2,)),
        ],
        compiler_params=pltpu.CompilerParams(
            collective_id=1, has_side_effects=True, vmem_limit_bytes=62 * 2**20
        ),
    )(owner, enc, gain, w_in, w_out, final_gain, context, kv, image, proj, down, up, magnitude, scale, shift)
    image_all, key_value, gathered, ratio = outs
    if not flat_columns(own_cols):
        gathered = gathered.transpose(1, 0, 2).reshape(scaled_rows, -1)
    return image_all, key_value, gathered, ratio


def back_kernel(
    owner_ref, lengths_ref, text_gain_ref, image_gain_ref, key_value_ref, image_ref, weight_ref, dora_ref,
    grad_ref, ratio_ref, magnitude_ref,
    image_out, down_out, cols_out, size_out,
    keys, values, attended, parts, slots, down, up, up_slots, down_slots,
    cols, col_slots, col_stage, col_sums, rows_all, row_slots, row_stage, row_sums,
    size, size_slots, size_stage, size_sums,
    chain_send, chain_recv, send_sems, recv_sems,
):
    count, devices = lax.axis_size("seq"), lax.axis_size("dp")
    rank, data_rank = lax.axis_index("seq"), lax.axis_index("dp")
    rows, width = image_out.shape
    depth = image_ref.shape[3]
    text = key_value_ref.shape[0]
    heads = depth // HD
    half = width // 2
    own_cols = ratio_ref.shape[1]
    block_rows = depth // devices
    f32, bf16 = jnp.float32, jnp.bfloat16
    over_rows = (((0,), (0,)), ((), ()))
    over_columns = (((1,), (1,)), ((), ()))
    wires = Wires(send_sems, recv_sems)

    def block_of(owner):
        return lax.rem(rank + count - owner, count)

    chain = Chain(
        lambda owner, h: parts.at[owner, h],
        lambda right, owner, h: slots.at[right, owner, h],
        chain_send,
        chain_recv,
        2,
    )
    near, far = chain.near, chain.far

    greet("seq", "dp")
    down[...] = lax.dot_general(
        grad_ref[...], weight_ref[depth:, :], over_columns, preferred_element_type=f32
    ).astype(bf16)
    small = []
    for k, peer in peers("seq"):
        small.append(wires.send(down, down_slots.at[k - 1], "seq", peer))

    length = jnp.int32(0)
    for p in range(devices):
        length = length + jnp.where(owner_ref[p] == data_rank, lengths_ref[p], 0)

    def head(h):
        return pl.ds(pl.multiple_of(h * HD, HD), HD)

    def key_step(h, carry):
        keys[:text, head(h)] = rms_scale(key_value_ref[:, head(h)], text_gain_ref[...]).astype(bf16)
        for k in range(count):
            start = text + k * rows
            keys[start : start + rows, head(h)] = rms_scale(
                image_ref[k, 1, :, head(h)].astype(f32), image_gain_ref[1:2, :]
            ).astype(bf16)
        return carry

    lax.fori_loop(0, heads, key_step, 0)
    values[:text, :] = key_value_ref[:, depth:].astype(bf16)
    for k in range(count):
        start = text + k * rows
        values[start : start + rows, :] = image_ref[k, 2]
    scale = 1.0 / math.sqrt(HD)

    for step in range(count):
        owner = chain.target(step, near)
        block = block_of(owner)
        block_slice = pl.ds(pl.multiple_of(block * rows, 16), rows)

        def head_step(h, carry):
            queries = rms_scale(
                image_ref[block, 0, :, head(h)].astype(f32), image_gain_ref[0:1, :]
            ).astype(bf16)
            scores = lax.dot_general(queries, keys[:, head(h)], over_columns, preferred_element_type=f32) * scale
            position = lax.broadcasted_iota(jnp.int32, scores.shape, 1)
            weight = jnp.where((position < length) | (position >= text), jnp.exp(scores), 0.0)
            denominator = jnp.sum(weight, -1, keepdims=True)
            mixture = jnp.dot(weight.astype(bf16), values[:, head(h)], preferred_element_type=f32)
            attended[block_slice, head(h)] = (mixture / denominator).astype(bf16)
            return carry

        lax.fori_loop(0, heads, head_step, 0)
        for h in range(2):
            columns = slice(h * half, (h + 1) * half)
            parts[owner, h] = jnp.dot(
                attended[block_slice, :], weight_ref[:depth, columns], preferred_element_type=f32
            ).astype(bf16)
        if step == 0:
            chain.begin(0)

    dora = dora_ref[...].astype(bf16)
    ups = lax.dot_general(attended[...], dora, over_columns, preferred_element_type=f32).astype(bf16)
    for k in range(count):
        up[k] = ups[k * rows : (k + 1) * rows]
    for k in range(1, count):
        before = lax.rem(rank + count - k, count)
        small.append(wires.send(up.at[k], up_slots.at[k - 1], "seq", before))
    for step in range(1, count - 2):
        chain.begin(step)
    chain.forward(0, near)
    for copy in small:
        copy.wait_recv()
    up_total = up[0].astype(f32)
    for k in range(1, count):
        up_total = up_total + up_slots[k - 1].astype(f32)
    up_total = up_total.astype(bf16)
    column_grad = lax.dot_general(up_total, grad_ref[...], over_rows, preferred_element_type=f32).astype(bf16)
    for j in range(devices):
        cols[j] = column_grad[:, j * own_cols : (j + 1) * own_cols]
    row_grad = lax.dot_general(down[...], attended[:rows, :], over_rows, preferred_element_type=f32)
    for k in range(1, count):
        row_grad = row_grad + lax.dot_general(
            down_slots[k - 1], attended[k * rows : (k + 1) * rows, :], over_rows, preferred_element_type=f32
        )
    for j in range(devices):
        rows_all[j] = row_grad[:, j * block_rows : (j + 1) * block_rows].astype(bf16)
    first = []
    for k, peer in peers("dp"):
        first.append(wires.send(cols.at[peer], col_slots.at[k - 1], "dp", peer))
        first.append(wires.send(rows_all.at[peer], row_slots.at[k - 1], "dp", peer))
    for copy in first:
        copy.wait_recv()
    col_total = cols[data_rank].astype(f32)
    row_total = rows_all[data_rank].astype(f32)
    for k, _ in peers("dp"):
        col_total = col_total + col_slots[k - 1].astype(f32)
        row_total = row_total + row_slots[k - 1].astype(f32)
    col_stage[...] = col_total.astype(bf16)
    row_stage[...] = row_total.astype(bf16)
    second = []
    for k, peer in peers("seq"):
        second.append(wires.send(col_stage, col_sums.at[k - 1], "seq", peer))
    for k, peer in peers("dp"):
        second.append(wires.send(row_stage, row_sums.at[data_rank], "dp", peer))
    row_sums[data_rank] = row_stage[...]
    chain.begin(count - 2)
    chain.forward(0, far)
    for step in range(1, count - 1):
        chain.forward(step, near)
        chain.forward(step, far)

    sums = []
    for h in range(2):
        chain.arrive(h)
        columns = slice(h * half, (h + 1) * half)
        total = chain.total(parts[rank, h], slots[1, rank, h], slots[0, rank, h])
        image_out[:, columns] = total.astype(bf16)
        sums.append(jnp.sum(grad_ref[:, columns].astype(f32) * total, 0, keepdims=True))
    per_half = devices // 2
    for d in range(devices):
        start = (d % per_half) * own_cols
        size[d] = sums[d // per_half][:, start : start + own_cols]
    last = [wires.send(size.at[peer], size_slots.at[k - 1], "dp", peer) for k, peer in peers("dp")]
    for copy in second:
        copy.wait_recv()
    col_total = col_stage[...].astype(f32)
    for k, _ in peers("seq"):
        col_total = col_total + col_sums[k - 1].astype(f32)
    cols_out[...] = col_total * ratio_ref[...]
    for d in range(devices):
        down_out[:, d * block_rows : (d + 1) * block_rows] = row_sums[d].astype(f32)
    for copy in last:
        copy.wait_recv()
    size_total = size[data_rank]
    for k, _ in peers("dp"):
        size_total = size_total + size_slots[k - 1]
    size_stage[...] = size_total
    last = [wires.send(size_stage, size_sums.at[k - 1], "seq", peer) for k, peer in peers("seq")]
    for copy in last:
        copy.wait_recv()
    for k, _ in peers("seq"):
        size_total = size_total + size_sums[k - 1]
    size_out[...] = size_total / magnitude_ref[...]
    chain.drain()
    wires.drain()


def back(owner, lengths, text_gain, image_gain, key_value, image, gathered, dora, grad, ratio, magnitude):
    count, devices = lax.axis_size("seq"), lax.axis_size("dp")
    rows, width = grad.shape
    rank, depth = dora.shape
    text = key_value.shape[0]
    own_cols = ratio.shape[1]
    block_rows = depth // devices
    f32, bf16 = jnp.float32, jnp.bfloat16
    others, data_others = count - 1, devices - 1
    wires = 4 * others + 4 * data_others
    return pl.pallas_call(
        back_kernel,
        out_shape=[
            jax.ShapeDtypeStruct((rows, width), bf16),
            jax.ShapeDtypeStruct((rank, depth), f32),
            jax.ShapeDtypeStruct((rank, own_cols), f32),
            jax.ShapeDtypeStruct((1, own_cols), f32),
        ],
        in_specs=[SMEM] * 2 + [VMEM] * 9,
        out_specs=[VMEM] * 4,
        scratch_shapes=[
            pltpu.VMEM((text + count * rows, depth), bf16),
            pltpu.VMEM((text + count * rows, depth), bf16),
            pltpu.VMEM((count * rows, depth), bf16),
            pltpu.VMEM((count, 2, rows, width // 2), bf16),
            pltpu.VMEM((2, count, 2, rows, width // 2), bf16),
            pltpu.VMEM((rows, rank), bf16),
            pltpu.VMEM((count, rows, rank), bf16),
            pltpu.VMEM((others, rows, rank), bf16),
            pltpu.VMEM((others, rows, rank), bf16),
            pltpu.VMEM((devices, rank, own_cols), bf16),
            pltpu.VMEM((data_others, rank, own_cols), bf16),
            pltpu.VMEM((rank, own_cols), bf16),
            pltpu.VMEM((others, rank, own_cols), bf16),
            pltpu.VMEM((devices, rank, block_rows), bf16),
            pltpu.VMEM((data_others, rank, block_rows), bf16),
            pltpu.VMEM((rank, block_rows), bf16),
            pltpu.VMEM((devices, rank, block_rows), bf16),
            pltpu.VMEM((devices, 1, own_cols), f32),
            pltpu.VMEM((data_others, 1, own_cols), f32),
            pltpu.VMEM((1, own_cols), f32),
            pltpu.VMEM((others, 1, own_cols), f32),
            pltpu.SemaphoreType.DMA((count * 2,)),
            pltpu.SemaphoreType.DMA((count * 4,)),
            pltpu.SemaphoreType.DMA((wires,)),
            pltpu.SemaphoreType.DMA((wires,)),
        ],
        compiler_params=pltpu.CompilerParams(
            collective_id=3, has_side_effects=True, vmem_limit_bytes=58 * 2**20
        ),
    )(owner, lengths, text_gain, image_gain, key_value, image, gathered, dora, grad, ratio, magnitude)


def on_device(
    enc_states,
    lengths,
    prompt_owner_sample,
    t5_gain,
    t5_in_weight,
    t5_out_weight,
    t5_final_gain,
    context_weight,
    text_shift,
    text_scale,
    kv_weight,
    text_key_gain,
    image_query_key_value,
    image_qk_gain,
    proj_weight,
    dora_a,
    dora_b,
    magnitude,
    grad_out,
):
    down = dora_a.T
    image_all, key_value, gathered, ratio = front(
        prompt_owner_sample,
        enc_states,
        t5_gain[None],
        t5_in_weight,
        t5_out_weight,
        t5_final_gain[None],
        context_weight,
        kv_weight.reshape(kv_weight.shape[0], -1),
        jnp.transpose(image_query_key_value[0], (1, 0, 2)),
        proj_weight,
        down,
        dora_b,
        magnitude[None],
        text_scale,
        text_shift,
    )
    image_out, grad_a, grad_b, grad_magnitude = back(
        prompt_owner_sample,
        lengths,
        text_key_gain[None],
        image_qk_gain,
        key_value,
        image_all,
        gathered,
        down,
        grad_out[0],
        ratio,
        magnitude[None],
    )
    return (image_out[None], grad_a.T, grad_b, grad_magnitude[0])


def solution(mesh):
    mapped = jax.shard_map(
        on_device,
        mesh=mesh,
        in_specs=(
            P("dp", None, None),
            P(),
            P(),
            P(),
            P(None, None, "seq"),
            P("seq", None),
            P(),
            P("seq", "dp"),
            P("dp", None),
            P("dp", None),
            P("dp", None, "seq"),
            P(),
            P("dp", "seq", None, None),
            P(),
            P("seq", "dp"),
            P("seq", None),
            P(None, "dp"),
            P("dp"),
            P("dp", "seq", None),
        ),
        out_specs=(P("dp", "seq", None), P("seq", None), P(None, "dp"), P("dp")),
        check_vma=False,
    )
    return mapped
```

```python
import functools
import math

import jax
import jax.numpy as jnp
from jax import lax
from jax.experimental import pallas as pl
from jax.experimental.pallas import tpu as pltpu
from jax.sharding import PartitionSpec as P

HD = 128
MAX_PROMPT = 128
EPSILON = 1e-06


def rms_scale(values, gain):
    return values * lax.rsqrt(jnp.mean(values * values, -1, keepdims=True) + EPSILON) * gain


def peers(axis):
    size, rank = lax.axis_size(axis), lax.axis_index(axis)
    return [(k, lax.rem(rank + k, size)) for k in range(1, size)]


def greet(*axes):
    barrier = pltpu.get_barrier_semaphore()
    count = 0
    for axis in axes:
        for _, peer in peers(axis):
            pl.semaphore_signal(
                barrier, inc=1, device_id={axis: peer}, device_id_type=pl.DeviceIdType.MESH
            )
            count += 1
    pl.semaphore_wait(barrier, count)


VMEM = pl.BlockSpec(memory_space=pltpu.VMEM)
SMEM = pl.BlockSpec(memory_space=pltpu.SMEM)


MESH = pl.DeviceIdType.MESH


class Wires:
    def __init__(self, send_sems, recv_sems):
        self.send_sems, self.recv_sems, self.copies = send_sems, recv_sems, []

    def send(self, source, target, axis, peer):
        index = len(self.copies)
        copy = pltpu.make_async_remote_copy(
            src_ref=source,
            dst_ref=target,
            send_sem=self.send_sems.at[index],
            recv_sem=self.recv_sems.at[index],
            device_id={axis: peer},
            device_id_type=MESH,
        )
        copy.start()
        self.copies.append(copy)
        return copy

    def drain(self):
        for copy in self.copies:
            copy.wait_send()


class Place:
    def __init__(self):
        self.pairs = lax.axis_size("dp") // 4
        index = lax.axis_index("dp")
        self.index = index
        self.core = lax.rem(index, 2)
        self.low = lax.rem(lax.div(index, 2), 2)
        self.high = lax.div(index, 4)

    def at(self, step=0, other_low=False, other_core=False):
        high = lax.rem(self.high + step + self.pairs, self.pairs) if step else self.high
        low = 1 - self.low if other_low else self.low
        core = 1 - self.core if other_core else self.core
        return (high * 2 + low) * 2 + core


class Gather:
    def __init__(self, wires, place, own, full, view):
        self.wires, self.place, self.own, self.full, self.view = wires, place, own, full, view
        self.sibling = place.at(other_core=True)
        self.late = []

    def share(self, owner, half=None):
        where = self.view(self.full, owner, half)
        self.late.append(self.wires.send(where, where, "dp", self.sibling))

    def first(self):
        place = self.place
        mine = self.view(self.full, place.index, None)
        send = self.wires.send
        self.low = send(self.own, mine, "dp", place.at(other_low=True))
        self.high = [send(self.own, mine, "dp", place.at(j)) for j in range(1, place.pairs)]
        self.late.append(send(self.own, mine, "dp", self.sibling))

    def second(self):
        place = self.place
        send = self.wires.send
        self.relayed = []
        self.low.wait_recv()
        owner = place.at(other_low=True)
        for j in range(1, place.pairs):
            where = self.view(self.full, owner, 0)
            self.relayed.append((j, 0, send(where, where, "dp", place.at(j))))
        self.share(owner)
        for j in range(1, place.pairs):
            self.high[j - 1].wait_recv()
            owner = place.at(-j)
            where = self.view(self.full, owner, 1)
            self.relayed.append((j, 1, send(where, where, "dp", place.at(other_low=True))))
            self.share(owner)

    def third(self):
        for j, half, copy in self.relayed:
            copy.wait_recv()
            self.share(self.place.at(-j, other_low=True), half)

    def done(self):
        for copy in self.late:
            copy.wait_recv()


def by_rows(rows):
    def view(full, owner, half):
        start, size = owner * rows, rows
        if half is not None:
            size = rows // 2
            start = start + half * size
        return full.at[pl.ds(pl.multiple_of(start, 16), size)]

    return view


def by_columns(rows, width, flat):
    def view(full, owner, half):
        part = pl.ds(0, rows) if half is None else pl.ds(half * (rows // 2), rows // 2)
        if flat:
            return full.at[part, pl.ds(pl.multiple_of(owner * width, 128), width)]
        return full.at[owner, part]

    return view


def flat_columns(width):
    return width % 128 == 0


def column_shape(devices, rows, width):
    return (rows, devices * width) if flat_columns(width) else (devices, rows, width)


def tile_of(width, largest):
    return next(t for t in (largest, largest // 2, 256, 128, width) if width % t == 0)


def exp_scores(queries, keys):
    scores = lax.dot_general(queries, keys, (((1,), (1,)), ((), ())), preferred_element_type=jnp.float32)
    return jnp.exp(scores * (1.0 / math.sqrt(HD)))


def pieces_of(own_cols):
    return own_cols // 128 if flat_columns(own_cols) else 1


def scaled_pieces(scaled, up_weight, weight, own_cols):
    adapter = up_weight.shape[-2]
    depth = scaled.shape[0] - adapter
    pieces = pieces_of(own_cols)
    piece = own_cols // pieces
    flat = flat_columns(own_cols)
    triples = [(scaled.at[pl.ds(depth, adapter)], up_weight, by_columns(adapter, own_cols, flat))]
    for p in range(pieces):
        source = scaled.at[pl.ds(0, depth), pl.ds(p * piece, piece)]
        triples.append((source, weight.at[p], by_columns(depth, piece, flat)))
    return triples


class Chain:
    def __init__(self, part, slot, send_sems, recv_sems, chunks):
        self.part, self.slot, self.chunks = part, slot, chunks
        self.send_sems, self.recv_sems = send_sems, recv_sems
        self.count, self.rank = lax.axis_size("seq"), lax.axis_index("seq")
        self.near = 1 - lax.div(self.rank, self.count // 2)
        self.far = 1 - self.near

    def target(self, step, right):
        return right * (self.count - 1 - step) + (1 - right) * step

    def link(self, owner, c, right):
        return pltpu.make_async_remote_copy(
            src_ref=self.part(owner, c),
            dst_ref=self.slot(right, owner, c),
            send_sem=self.send_sems.at[owner * self.chunks + c],
            recv_sem=self.recv_sems.at[(right * self.count + owner) * self.chunks + c],
            device_id={"seq": jnp.clip(self.rank + 2 * right - 1, 0, self.count - 1)},
            device_id_type=MESH,
        )

    def begin(self, step, chunks=None):
        owner = self.target(step, self.near)

        @pl.when((self.rank == 0) | (self.rank == self.count - 1))
        def _():
            for c in range(self.chunks) if chunks is None else chunks:
                self.link(owner, c, self.near).start()

    def forward(self, step, right, chunks=None):
        owner = self.target(step, right)
        ahead = right * (owner - self.rank) + (1 - right) * (self.rank - owner)
        behind = right * self.rank + (1 - right) * (self.count - 1 - self.rank)

        @pl.when((ahead > 0) & (behind > 0))
        def _():
            for c in range(self.chunks) if chunks is None else chunks:
                self.link(owner, c, right).wait_recv()
                part = self.part(owner, c)
                part[...] = (
                    part[...].astype(jnp.float32) + self.slot(right, owner, c)[...].astype(jnp.float32)
                ).astype(part.dtype)
                self.link(owner, c, right).start()

    def arrive(self, c):
        @pl.when(self.rank >= 1)
        def _():
            self.link(self.rank, c, 1).wait_recv()

        @pl.when(self.rank <= self.count - 2)
        def _():
            self.link(self.rank, c, 0).wait_recv()

    def total(self, part, from_left, from_right):
        total = part.astype(jnp.float32)
        total = total + jnp.where(self.rank >= 1, from_left.astype(jnp.float32), 0.0)
        return total + jnp.where(self.rank <= self.count - 2, from_right.astype(jnp.float32), 0.0)

    def drain(self):
        for owner in range(self.count):

            @pl.when(self.rank != owner)
            def _():
                for c in range(self.chunks):
                    self.link(owner, c, 0).wait_send()


class Relay:
    def __init__(self, block, send_sems, recv_sems):
        self.block, self.send_sems, self.recv_sems = block, send_sems, recv_sems
        self.count, self.rank = lax.axis_size("seq"), lax.axis_index("seq")

    def link(self, owner, hop, right):
        index = right * (self.count - 1) + hop
        where = self.block(owner)
        return pltpu.make_async_remote_copy(
            src_ref=where,
            dst_ref=where,
            send_sem=self.send_sems.at[index],
            recv_sem=self.recv_sems.at[index],
            device_id={"seq": jnp.clip(self.rank + 2 * right - 1, 0, self.count - 1)},
            device_id_type=MESH,
        )

    def reaches(self, right):
        return self.rank < self.count - 1 if right else self.rank > 0

    def begin(self):
        for right in (1, 0):

            @pl.when(self.reaches(right))
            def _():
                self.link(self.rank, 0, right).start()

    def forward(self, hop):
        for right in (1, 0):
            owner = self.rank - hop if right else self.rank + hop
            there = owner >= 0 if right else owner < self.count
            owner = jnp.clip(owner, 0, self.count - 1)

            @pl.when(there)
            def _():
                self.link(owner, hop - 1, right).wait_recv()

            if hop < self.count - 1:

                @pl.when(there & self.reaches(right))
                def _():
                    self.link(owner, hop, right).start()

    def drain(self):
        for hop in range(self.count - 1):
            for right in (1, 0):
                owner = self.rank - hop if right else self.rank + hop
                there = owner >= 0 if right else owner < self.count

                @pl.when(there & self.reaches(right))
                def _():
                    self.link(self.rank, hop, right).wait_send()


def front_part(
    owner_ref, enc_ref, gain_ref, in_ref, out_ref, final_ref, context_ref, kv_ref, image_ref,
    proj_ref, down_ref, up_ref, magnitude_ref, scale_ref, shift_ref, image_gain_ref,
    queries, mixture, denominator, key_value, own_scaled, weight, up_weight, ratio_ref,
    image_all, tokens, normed, in_tiles, out_tiles, hidden, part, sum_slots, encoded, context_all, kv_all,
    context_part, row_slots, stage, prompts, sibling_prompts, text_all,
    direction, squares, square_slots,
    in_sems, out_sems, local_sems, send_sems, recv_sems, sum_send, sum_recv, row_send, row_recv, text_send, text_recv,
):
    f32, bf16 = jnp.float32, jnp.bfloat16
    count, devices = lax.axis_size("seq"), lax.axis_size("dp")
    rank, data_rank = lax.axis_index("seq"), lax.axis_index("dp")
    place = Place()
    wires = Wires(send_sems, recv_sems)
    text, width_enc = tokens.shape
    feat = encoded.shape[1]
    width = context_part.shape[1]
    rows = stage.shape[0]
    slots = in_tiles.shape[0]
    tile = in_tiles.shape[2] // 2
    tiles = hidden.shape[1] // tile
    depth, own_cols = proj_ref.shape
    flat = flat_columns(own_cols)
    late = count // 2

    class in_copy:
        def __init__(self, i, slot):
            columns = pl.ds(pl.multiple_of(i * tile, 128), tile)
            self.copies = [
                pltpu.make_async_copy(
                    in_ref.at[side, :, columns],
                    in_tiles.at[slot, :, side * tile : (side + 1) * tile],
                    in_sems.at[slot * 2 + side],
                )
                for side in range(2)
            ]

        def start(self):
            for copy in self.copies:
                copy.start()

        def wait(self):
            for copy in self.copies:
                copy.wait()

    near = 1 - lax.div(rank, count // 2)
    out_slots, _, out_tile = out_tiles.shape
    chunks = feat // out_tile

    def out_copy(i):
        step, c = divmod(i, chunks)
        owner = near * (count - 1 - step) + (1 - near) * step
        columns = pl.ds(pl.multiple_of(owner * feat + c * out_tile, 128), out_tile)
        slot = i % out_slots
        return pltpu.make_async_copy(out_ref.at[:, columns], out_tiles.at[slot], out_sems.at[slot])

    def local(source, target, index):
        return pltpu.make_async_copy(source, target, local_sems.at[index])

    token_copy = local(enc_ref.at[0, pl.ds(0, text)], tokens, 0)
    token_copy.start()
    for i in range(min(slots, tiles)):
        in_copy(i, i).start()
    for i in range(min(out_slots, count * chunks)):
        out_copy(i).start()

    def heads_of(owner):
        head_width = image_all.shape[3]
        return pl.ds(pl.multiple_of(owner * head_width, 128), head_width)

    context_view = by_columns(context_ref.shape[0], own_cols, flat)
    kv_view = by_rows(kv_ref.shape[0])
    context_gather = Gather(wires, place, context_ref, context_all, context_view)
    kv_gather = Gather(wires, place, kv_ref, kv_all, kv_view)

    locals_ = [
        local(image_ref.at[:, :, heads_of(rank)], image_all.at[0], 2),
        local(context_ref, context_view(context_all, data_rank, None), 3),
        local(kv_ref, kv_view(kv_all, data_rank, None), 4),
    ]
    scaled_gathers, scaled_locals = [], []
    for source, target, view in scaled_pieces(own_scaled, up_weight, weight, own_cols)[:2]:
        scaled_gathers.append(Gather(wires, place, source, target, view))
        scaled_locals.append(local(source, view(target, data_rank, None), 5 + len(scaled_locals)))
    image_rows = image_all.shape[2]
    heads = image_all.shape[3] // HD

    def head(h):
        return pl.ds(pl.multiple_of(h * HD, HD), HD)

    def query_step(h, carry):
        for k in range(count):
            queries[k * image_rows : (k + 1) * image_rows, head(h)] = rms_scale(
                image_all[k, 0, :, head(h)].astype(f32), image_gain_ref[0:1, :]
            ).astype(bf16)
        return carry

    def attend(k):
        def head_step(h, carry):
            keys = rms_scale(image_all[k, 1, :, head(h)].astype(f32), image_gain_ref[1:2, :]).astype(bf16)
            share = exp_scores(queries[:, head(h)], keys)
            total = jnp.broadcast_to(jnp.sum(share, -1, keepdims=True), (share.shape[0], HD))
            mixed = jnp.dot(share.astype(bf16), image_all[k, 2, :, head(h)], preferred_element_type=f32)
            if k:
                total = total + denominator[:, head(h)]
                mixed = mixed + mixture[:, head(h)]
            denominator[:, head(h)] = total
            mixture[:, head(h)] = mixed
            return carry

        if k:
            image_copies[k, 1].wait_recv()
            image_copies[k, 2].wait_recv()
        lax.fori_loop(0, heads, head_step, 0)

    greet("seq", "dp")
    context_gather.first()
    image_copies = {}

    def image(k, kind):
        peer = lax.rem(rank + k, count)
        image_copies[k, kind] = wires.send(
            image_ref.at[kind, :, heads_of(peer)], image_all.at[k, kind], "seq", peer
        )

    def images(kinds):
        for k in range(2, count):
            if k != late:
                for kind in kinds:
                    image(k, kind)

    for kind in range(3):
        image(1, kind)

    for copy in locals_:
        copy.start()

    token_copy.wait()
    for r in range(0, text, 32):
        block = tokens[r : r + 32, :].astype(f32)
        normed[r : r + 32, :] = rms_scale(block, gain_ref[...]).astype(bf16)

    def in_step(i, carry):
        slot = lax.rem(i, slots)
        in_copy(i, slot).wait()
        both = jnp.dot(normed[...], in_tiles[slot], preferred_element_type=f32)
        gate, upward = both[:, :tile], both[:, tile:]
        columns = pl.ds(pl.multiple_of(i * tile, 128), tile)
        hidden[:, columns] = (jax.nn.gelu(gate, approximate=True) * upward).astype(bf16)

        @pl.when(i + slots < tiles)
        def _():
            in_copy(i + slots, slot).start()

        return carry

    lax.fori_loop(0, tiles, in_step, 0)

    def piece(c):
        return slice(c * out_tile, (c + 1) * out_tile)

    sums = Chain(
        lambda owner, c: part.at[owner, :, piece(c)],
        lambda right, owner, c: sum_slots.at[owner + right, :, piece(c)],
        sum_send,
        sum_recv,
        chunks,
    )
    if late > 1:
        image(late, 0)
    for step in range(count):
        owner = sums.target(step, sums.near)
        for c in range(sums.chunks):
            index = step * chunks + c
            out_copy(index).wait()
            part[owner, :, piece(c)] = jnp.dot(
                hidden[...], out_tiles[index % out_slots], preferred_element_type=f32
            ).astype(bf16)
            if index + out_slots < count * chunks:
                out_copy(index + out_slots).start()
            if step < count - 1:
                sums.begin(step, (c,))

    context_gather.second()
    kv_gather.first()

    total = jnp.zeros((1, own_cols), f32)
    for r in range(0, depth, 128):
        block = proj_ref[r : r + 128, :].astype(f32) + lax.dot_general(
            down_ref[:, r : r + 128],
            up_ref[...],
            (((0,), (0,)), ((), ())),
            precision=lax.Precision.HIGHEST,
            preferred_element_type=f32,
        )
        direction[r : r + 128, :] = block
        total = total + jnp.sum(block * block, 0, keepdims=True)
    squares[...] = total
    square_copies = [wires.send(squares, square_slots.at[k - 1], "seq", peer) for k, peer in peers("seq")]

    for step in range(count - 1):
        sums.forward(step, sums.near)
        sums.forward(step, sums.far)
    context_gather.third()
    for c in range(sums.chunks):
        sums.arrive(c)
    images((0,))
    own = pl.ds(pl.multiple_of(rank * feat, 128), feat)
    for r in range(0, text, 32):
        block = slice(r, r + 32)
        total = sums.total(part[rank, block, :], sum_slots[rank + 1, block, :], sum_slots[rank, block, :])
        encoded[block, :] = ((tokens[block, own].astype(f32) + total) * final_ref[:, own]).astype(bf16)

    locals_[1].wait()
    context_gather.done()
    if late > 1:
        image(late, 1)

    def block_of(index):
        return pl.ds(pl.multiple_of(index * rows, 16), rows)

    half = width // 2
    row_sums = Chain(
        lambda owner, c: context_part.at[block_of(owner), c * half : (c + 1) * half],
        lambda right, owner, c: row_slots.at[owner + right, :, c * half : (c + 1) * half],
        row_send,
        row_recv,
        2,
    )
    for c in range(2):
        if flat:
            step = tile_of(half, 512)
            for start in range(c * half, (c + 1) * half, step):
                context_part[:, start : start + step] = jnp.dot(
                    encoded[...], context_all[:, start : start + step], preferred_element_type=f32
                ).astype(bf16)
        else:
            for d in range(c * devices // 2, (c + 1) * devices // 2):
                context_part[:, d * own_cols : (d + 1) * own_cols] = jnp.dot(
                    encoded[...], context_all[d], preferred_element_type=f32
                ).astype(bf16)
        for step in range(count - 1):
            row_sums.begin(step, (c,))
    kv_gather.second()
    for copy in square_copies:
        copy.wait_recv()
    total = squares[...]
    for k in range(1, count):
        total = total + square_slots[k - 1]
    ratio = magnitude_ref[...] / jnp.sqrt(total + EPSILON)
    ratio_ref[...] = ratio
    for r in range(0, depth, 128):
        own_scaled[r : r + 128, :] = (direction[r : r + 128, :] * ratio).astype(bf16)
    own_scaled[depth:, :] = (up_ref[...] * ratio).astype(bf16)

    for c in range(2):
        for step in range(count - 1):
            row_sums.forward(step, row_sums.near, (c,))
            row_sums.forward(step, row_sums.far, (c,))
    for c in range(2):
        row_sums.arrive(c)
    stage[...] = row_sums.total(
        context_part[block_of(rank), :], row_slots[rank + 1], row_slots[rank]
    ).astype(bf16)

    chips = devices // 2
    chip = lax.div(data_rank, 2)
    sibling = place.at(other_core=True)
    prompt_copies = [
        wires.send(stage, prompts.at[j - 1], "dp", lax.rem(chip + j, chips) * 2 + place.core)
        for j in range(1, chips)
    ]
    shared = [wires.send(stage, sibling_prompts.at[0], "dp", sibling)]
    images((1, 2))
    for gather, copy in zip(scaled_gathers, scaled_locals):
        gather.first()
        copy.start()
    locals_[0].wait()
    for k in range(1, count):
        image_copies[k, 0].wait_recv()
    lax.fori_loop(0, heads, query_step, 0)
    attend(0)
    attend(1)
    for j in range(1, chips):
        prompt_copies[j - 1].wait_recv()
        shared.append(wires.send(prompts.at[j - 1], sibling_prompts.at[j], "dp", sibling))
    routed = jnp.where(owner_ref[data_rank] == data_rank, stage[...].astype(f32), 0.0)
    for j in range(1, chips):
        prompt = lax.rem(chip + chips - j, chips) * 2 + place.core
        routed = routed + jnp.where(owner_ref[prompt] == data_rank, prompts[j - 1].astype(f32), 0.0)
    for j in range(chips):
        shared[j].wait_recv()
        prompt = lax.rem(chip + chips - j, chips) * 2 + 1 - place.core
        routed = routed + jnp.where(owner_ref[prompt] == data_rank, sibling_prompts[j].astype(f32), 0.0)
    centre = jnp.mean(routed, -1, keepdims=True)
    spread = jnp.mean((routed - centre) * (routed - centre), -1, keepdims=True)
    layer_normed = (routed - centre) * lax.rsqrt(spread + EPSILON)
    text_all[block_of(rank), :] = ((1.0 + scale_ref[...]) * layer_normed + shift_ref[...]).astype(bf16)
    if late > 1:
        image(late, 2)
    texts = Relay(lambda owner: text_all.at[block_of(owner)], text_send, text_recv)
    texts.begin()
    for k in [k for k in range(2, count) if k != late] + [late] * (late > 1):
        attend(k)
    for gather in scaled_gathers:
        gather.second()
    for hop in range(1, count):
        texts.forward(hop)
    kv_gather.third()
    for gather in scaled_gathers:
        gather.third()
    locals_[2].wait()
    kv_gather.done()
    step = tile_of(kv_all.shape[1], 512)
    for c in range(0, kv_all.shape[1], step):
        key_value[:, c : c + step] = jnp.dot(
            text_all[...], kv_all[:, c : c + step], preferred_element_type=f32
        )
    for gather, copy in zip(scaled_gathers, scaled_locals):
        gather.done()
        copy.wait()
    return sums, row_sums, texts, wires


def back_part(
    owner_ref, lengths_ref, text_gain_ref, key_value_ref, queries_ref, mixture_ref, denominator_ref,
    scaled_ref, weight, up_weight_ref, dora_ref, grad_ref, ratio_ref, magnitude_ref,
    image_out, down_out, cols_out, size_out,
    attended, parts, slots, down, up, up_slots, down_slots,
    cols, col_slots, col_stage, col_sums, rows_all, row_slots, row_stage, row_sums,
    size, size_slots, size_stage, size_sums,
    local_sems, chain_send, chain_recv, send_sems, recv_sems,
):
    count, devices = lax.axis_size("seq"), lax.axis_size("dp")
    rank, data_rank = lax.axis_index("seq"), lax.axis_index("dp")
    rows, width = image_out.shape
    depth = queries_ref.shape[1]
    text = key_value_ref.shape[0]
    heads = depth // HD
    own_cols = ratio_ref.shape[1]
    adapter = dora_ref.shape[0]
    pieces = pieces_of(own_cols)
    piece = own_cols // pieces
    flat = flat_columns(own_cols)
    block_rows = depth // devices
    f32, bf16 = jnp.float32, jnp.bfloat16
    over_rows = (((0,), (0,)), ((), ()))
    over_columns = (((1,), (1,)), ((), ()))
    wires = Wires(send_sems, recv_sems)
    place = Place()

    def block_of(owner):
        return lax.rem(rank + count - owner, count)

    chain = Chain(
        lambda owner, p: parts.at[owner, p],
        lambda right, owner, p: slots.at[owner + right, p],
        chain_send,
        chain_recv,
        pieces,
    )
    near, far = chain.near, chain.far
    gathers, owns = [None], [None]
    for source, target, view in scaled_pieces(scaled_ref, up_weight_ref, weight, own_cols)[2:]:
        gathers.append(Gather(wires, place, source, target, view))
        owns.append(
            pltpu.make_async_copy(source, view(target, data_rank, None), local_sems.at[len(owns) - 1])
        )
    if pieces > 1:
        gathers[1].first()
    for copy in owns[1:]:
        copy.start()

    length = jnp.int32(0)
    for p in range(devices):
        length = length + jnp.where(owner_ref[p] == data_rank, lengths_ref[p], 0)

    def head(h):
        return pl.ds(pl.multiple_of(h * HD, HD), HD)

    def head_step(h, carry):
        keys = rms_scale(key_value_ref[:, head(h)], text_gain_ref[...]).astype(bf16)
        values = key_value_ref[:, pl.ds(pl.multiple_of(depth + h * HD, HD), HD)].astype(bf16)
        share = exp_scores(queries_ref[:, head(h)], keys)
        position = lax.broadcasted_iota(jnp.int32, share.shape, 1)
        share = jnp.where(position < length, share, 0.0)
        denominator = denominator_ref[:, head(h)] + jnp.sum(share, -1, keepdims=True)
        mixture = mixture_ref[:, head(h)] + jnp.dot(share.astype(bf16), values, preferred_element_type=f32)
        attended[:, head(h)] = (mixture / denominator).astype(bf16)
        return carry

    lax.fori_loop(0, heads, head_step, 0)

    def products(p, begin=True):
        if p:
            gathers[p].done()
            owns[p].wait()
        source = weight.at[p]
        for step in range(count):
            owner = chain.target(step, near)
            block = attended[pl.ds(pl.multiple_of(block_of(owner) * rows, 16), rows), :]
            if flat:
                parts[owner, p] = jnp.dot(block, source[...], preferred_element_type=f32).astype(bf16)
            else:
                for d in range(devices):
                    parts[owner, p, :, d * piece : (d + 1) * piece] = jnp.dot(
                        block, source[d], preferred_element_type=f32
                    ).astype(bf16)
            if begin and step < count - 1:
                chain.begin(step, (p,))

    if flat:
        down_total = lax.dot_general(grad_ref[...], up_weight_ref[...], over_columns, preferred_element_type=f32)
    else:
        down_total = jnp.zeros((rows, adapter), f32)
        for d in range(devices):
            down_total = down_total + lax.dot_general(
                grad_ref[:, d * own_cols : (d + 1) * own_cols],
                up_weight_ref[d],
                over_columns,
                preferred_element_type=f32,
            )
    down[...] = down_total.astype(bf16)
    ups = lax.dot_general(
        attended[...], dora_ref[...].astype(bf16), over_columns, preferred_element_type=f32
    ).astype(bf16)
    for k in range(count):
        up[k] = ups[k * rows : (k + 1) * rows]
    small = []
    for k, peer in peers("seq"):
        small.append(wires.send(down, down_slots.at[k - 1], "seq", peer))
        before = lax.rem(rank + count - k, count)
        small.append(wires.send(up.at[k], up_slots.at[k - 1], "seq", before))
    products(0)
    if pieces > 1:
        gathers[1].second()
    if pieces > 2:
        gathers[2].first()

    for copy in small:
        copy.wait_recv()
    up_total = up[0].astype(f32)
    for k in range(1, count):
        up_total = up_total + up_slots[k - 1].astype(f32)
    up_total = up_total.astype(bf16)
    column_grad = lax.dot_general(up_total, grad_ref[...], over_rows, preferred_element_type=f32).astype(bf16)
    for j in range(devices):
        cols[j] = column_grad[:, j * own_cols : (j + 1) * own_cols]
    row_grad = lax.dot_general(down[...], attended[:rows, :], over_rows, preferred_element_type=f32)
    for k in range(1, count):
        row_grad = row_grad + lax.dot_general(
            down_slots[k - 1], attended[k * rows : (k + 1) * rows, :], over_rows, preferred_element_type=f32
        )
    for j in range(devices):
        rows_all[j] = row_grad[:, j * block_rows : (j + 1) * block_rows].astype(bf16)
    first = []
    for k, peer in peers("dp"):
        first.append(wires.send(cols.at[peer], col_slots.at[k - 1], "dp", peer))
        first.append(wires.send(rows_all.at[peer], row_slots.at[k - 1], "dp", peer))

    for p in range(1, pieces):
        if p > 1:
            gathers[p].second()
            if p + 1 < pieces:
                gathers[p + 1].first()
        gathers[p].third()
        products(p, p + 1 < pieces)
        chain.forward(p - 1, near, (0,))
    moves = [(p, step, side) for p in range(pieces) for step in range(count - 1) for side in (0, 1)]
    moves = [m for m in moves if m not in [(0, p - 1, 0) for p in range(1, pieces)]]
    for copy in first:
        copy.wait_recv()
    col_total = cols[data_rank].astype(f32)
    row_total = rows_all[data_rank].astype(f32)
    for k, _ in peers("dp"):
        col_total = col_total + col_slots[k - 1].astype(f32)
        row_total = row_total + row_slots[k - 1].astype(f32)
    col_stage[...] = col_total.astype(bf16)
    row_stage[...] = row_total.astype(bf16)
    second = []
    for k, peer in peers("seq"):
        second.append(wires.send(col_stage, col_sums.at[k - 1], "seq", peer))
    for k, peer in peers("dp"):
        second.append(wires.send(row_stage, row_sums.at[data_rank], "dp", peer))
    row_sums[data_rank] = row_stage[...]
    if pieces > 1:
        for step in range(count - 1):
            chain.begin(step, (pieces - 1,))
    for p, step, side in moves:
        chain.forward(step, far if side else near, (p,))

    for p in range(pieces):
        chain.arrive(p)
        total = chain.total(parts[rank, p], slots[rank + 1, p], slots[rank, p])
        for d in range(devices):
            own = slice(d * own_cols + p * piece, d * own_cols + (p + 1) * piece)
            block = total[:, d * piece : (d + 1) * piece]
            image_out[:, own] = block.astype(bf16)
            size[d, :, p * piece : (p + 1) * piece] = jnp.sum(
                grad_ref[:, own].astype(f32) * block, 0, keepdims=True
            )
    last = [wires.send(size.at[peer], size_slots.at[k - 1], "dp", peer) for k, peer in peers("dp")]
    for copy in second:
        copy.wait_recv()
    col_total = col_stage[...].astype(f32)
    for k, _ in peers("seq"):
        col_total = col_total + col_sums[k - 1].astype(f32)
    cols_out[...] = col_total * ratio_ref[...]
    for d in range(devices):
        down_out[:, d * block_rows : (d + 1) * block_rows] = row_sums[d].astype(f32)
    for copy in last:
        copy.wait_recv()
    size_total = size[data_rank]
    for k, _ in peers("dp"):
        size_total = size_total + size_slots[k - 1]
    size_stage[...] = size_total
    last = [wires.send(size_stage, size_sums.at[k - 1], "seq", peer) for k, peer in peers("seq")]
    for copy in last:
        copy.wait_recv()
    for k, _ in peers("seq"):
        size_total = size_total + size_sums[k - 1]
    size_out[...] = size_total / magnitude_ref[...]
    chain.drain()
    wires.drain()


def program_kernel(counts, *refs):
    names = []
    for n in counts:
        names.append(refs[:n])
        refs = refs[n:]
    front_in, back_in, outs, shared, front_scratch, back_scratch = names
    key_value, queries, mixture, denominator, own_scaled, weight, up_weight, ratio = shared
    owner, down, magnitude = front_in[0], front_in[10], front_in[12]
    waits = front_part(
        *front_in, queries, mixture, denominator, key_value, own_scaled, weight, up_weight, ratio, *front_scratch
    )
    lengths, text_gain, grad = back_in
    back_part(
        owner, lengths, text_gain, key_value, queries, mixture, denominator,
        own_scaled, weight, up_weight, down, grad, ratio, magnitude,
        *outs, *back_scratch,
    )
    for wait in waits:
        wait.drain()


def program(
    owner, enc, gain, w_in, w_out, final_gain, context, kv, image, proj, down, up, magnitude, scale, shift,
    image_gain, lengths, text_gain, grad,
):
    count, devices = lax.axis_size("seq"), lax.axis_size("dp")
    bf16, f32 = jnp.bfloat16, jnp.float32
    width_enc, hidden = w_in.shape[1:]
    feat = width_enc // count
    text = MAX_PROMPT
    width = scale.shape[1]
    text_rows = text // count
    kinds, rows, _ = image.shape
    head_width = width // count
    depth, own_cols = proj.shape
    rank = up.shape[0]
    block_rows = depth // devices
    pieces = pieces_of(own_cols)
    piece = own_cols // pieces
    others, data_others, pairs = count - 1, devices - 1, devices // 4
    tile, out_tile = tile_of(hidden, 128), tile_of(feat, 512)
    slots = 3
    sum_chunks = feat // out_tile
    per_gather = 6 * pairs - 3
    front_wires = 4 * others + 4 * pairs + 4 * per_gather
    back_wires = 4 * others + 4 * data_others + pieces * per_gather
    any_ = pl.BlockSpec(memory_space=pl.ANY)
    vmem, sems = pltpu.VMEM, pltpu.SemaphoreType.DMA
    shared = [
        vmem((text, kv.shape[1]), f32),
        vmem((count * rows, head_width), bf16),
        vmem((count * rows, head_width), f32),
        vmem((count * rows, head_width), f32),
        vmem((depth + rank, own_cols), bf16),
        vmem((pieces,) + column_shape(devices, depth, piece), bf16),
        vmem(column_shape(devices, rank, own_cols), bf16),
        vmem((1, own_cols), f32),
    ]
    front_scratch = [
        vmem((count, kinds, rows, head_width), bf16),
        vmem((text, width_enc), bf16),
        vmem((text, width_enc), bf16),
        vmem((slots, width_enc, 2 * tile), bf16),
        vmem((slots, hidden, out_tile), bf16),
        vmem((text, hidden), bf16),
        vmem((count, text, feat), bf16),
        vmem((count + 1, text, feat), bf16),
        vmem((text, feat), bf16),
        vmem(column_shape(devices, context.shape[0], own_cols), bf16),
        vmem((kv.shape[0] * devices, kv.shape[1]), bf16),
        vmem((text, width), bf16),
        vmem((count + 1, text_rows, width), bf16),
        vmem((text_rows, width), bf16),
        vmem((devices // 2 - 1, text_rows, width), bf16),
        vmem((devices // 2, text_rows, width), bf16),
        vmem((text, width), bf16),
        vmem((depth, own_cols), f32),
        vmem((1, own_cols), f32),
        vmem((others, 1, own_cols), f32),
        sems((slots * 2,)),
        sems((slots,)),
        sems((7,)),
        sems((front_wires,)),
        sems((front_wires,)),
        sems((count * sum_chunks,)),
        sems((count * 2 * sum_chunks,)),
        sems((count * 2,)),
        sems((count * 4,)),
        sems((count * 2,)),
        sems((count * 2,)),
    ]
    back_scratch = [
        vmem((count * rows, head_width), bf16),
        vmem((count, pieces, rows, devices * piece), bf16),
        vmem((count + 1, pieces, rows, devices * piece), bf16),
        vmem((rows, rank), bf16),
        vmem((count, rows, rank), bf16),
        vmem((others, rows, rank), bf16),
        vmem((others, rows, rank), bf16),
        vmem((devices, rank, own_cols), bf16),
        vmem((data_others, rank, own_cols), bf16),
        vmem((rank, own_cols), bf16),
        vmem((others, rank, own_cols), bf16),
        vmem((devices, rank, block_rows), bf16),
        vmem((data_others, rank, block_rows), bf16),
        vmem((rank, block_rows), bf16),
        vmem((devices, rank, block_rows), bf16),
        vmem((devices, 1, own_cols), f32),
        vmem((data_others, 1, own_cols), f32),
        vmem((1, own_cols), f32),
        vmem((others, 1, own_cols), f32),
        sems((pieces + 1,)),
        sems((count * pieces,)),
        sems((count * 2 * pieces,)),
        sems((back_wires,)),
        sems((back_wires,)),
    ]
    front_in = (
        owner, enc, gain, w_in, w_out, final_gain, context, kv, image, proj, down, up, magnitude, scale, shift,
        image_gain,
    )
    back_in = (lengths, text_gain, grad)
    counts = (len(front_in), len(back_in), 4, len(shared), len(front_scratch), len(back_scratch))
    return pl.pallas_call(
        functools.partial(program_kernel, counts),
        out_shape=[
            jax.ShapeDtypeStruct(grad.shape, bf16),
            jax.ShapeDtypeStruct((rank, depth), f32),
            jax.ShapeDtypeStruct((rank, own_cols), f32),
            jax.ShapeDtypeStruct((1, own_cols), f32),
        ],
        in_specs=[SMEM, any_, VMEM, any_, any_, VMEM, any_, any_, any_] + [VMEM] * 7 + [SMEM, VMEM, VMEM],
        out_specs=[VMEM] * 4,
        scratch_shapes=shared + front_scratch + back_scratch,
        compiler_params=pltpu.CompilerParams(
            collective_id=1, has_side_effects=True, vmem_limit_bytes=63 * 2**20
        ),
    )(*front_in, *back_in)


def on_device(
    enc_states,
    lengths,
    prompt_owner_sample,
    t5_gain,
    t5_in_weight,
    t5_out_weight,
    t5_final_gain,
    context_weight,
    text_shift,
    text_scale,
    kv_weight,
    text_key_gain,
    image_query_key_value,
    image_qk_gain,
    proj_weight,
    dora_a,
    dora_b,
    magnitude,
    grad_out,
):
    image_out, grad_a, grad_b, grad_magnitude = program(
        prompt_owner_sample,
        enc_states,
        t5_gain[None],
        t5_in_weight,
        t5_out_weight,
        t5_final_gain[None],
        context_weight,
        kv_weight.reshape(kv_weight.shape[0], -1),
        jnp.transpose(image_query_key_value[0], (1, 0, 2)),
        proj_weight,
        dora_a.T,
        dora_b,
        magnitude[None],
        text_scale,
        text_shift,
        image_qk_gain,
        lengths,
        text_key_gain[None],
        grad_out[0],
    )
    return (image_out[None], grad_a.T, grad_b, grad_magnitude[0])


def solution(mesh):
    mapped = jax.shard_map(
        on_device,
        mesh=mesh,
        in_specs=(
            P("dp", None, None),
            P(),
            P(),
            P(),
            P(None, None, "seq"),
            P("seq", None),
            P(),
            P("seq", "dp"),
            P("dp", None),
            P("dp", None),
            P("dp", None, "seq"),
            P(),
            P("dp", "seq", None, None),
            P(),
            P("seq", "dp"),
            P("seq", None),
            P(None, "dp"),
            P("dp"),
            P("dp", "seq", None),
        ),
        out_specs=(P("dp", "seq", None), P("seq", None), P(None, "dp"), P("dp")),
        check_vma=False,
    )
    return mapped
```

```python
import functools
import math

import jax
import jax.numpy as jnp
from jax import lax
from jax.experimental import pallas as pl
from jax.experimental.pallas import tpu as pltpu
from jax.sharding import PartitionSpec as P

HD = 128
MAX_PROMPT = 128
EPSILON = 1e-06


def rms_scale(values, gain):
    return values * lax.rsqrt(jnp.mean(values * values, -1, keepdims=True) + EPSILON) * gain


def peers(axis):
    size, rank = lax.axis_size(axis), lax.axis_index(axis)
    return [(k, lax.rem(rank + k, size)) for k in range(1, size)]


def greet(*axes):
    barrier = pltpu.get_barrier_semaphore()
    count = 0
    for axis in axes:
        for _, peer in peers(axis):
            pl.semaphore_signal(
                barrier, inc=1, device_id={axis: peer}, device_id_type=pl.DeviceIdType.MESH
            )
            count += 1
    pl.semaphore_wait(barrier, count)


VMEM = pl.BlockSpec(memory_space=pltpu.VMEM)
SMEM = pl.BlockSpec(memory_space=pltpu.SMEM)


MESH = pl.DeviceIdType.MESH


class Wires:
    def __init__(self, send_sems, recv_sems):
        self.send_sems, self.recv_sems, self.copies = send_sems, recv_sems, []

    def send(self, source, target, axis, peer):
        index = len(self.copies)
        copy = pltpu.make_async_remote_copy(
            src_ref=source,
            dst_ref=target,
            send_sem=self.send_sems.at[index],
            recv_sem=self.recv_sems.at[index],
            device_id={axis: peer},
            device_id_type=MESH,
        )
        copy.start()
        self.copies.append(copy)
        return copy

    def drain(self):
        for copy in self.copies:
            copy.wait_send()


class Place:
    def __init__(self):
        self.pairs = lax.axis_size("dp") // 4
        index = lax.axis_index("dp")
        self.index = index
        self.core = lax.rem(index, 2)
        self.low = lax.rem(lax.div(index, 2), 2)
        self.high = lax.div(index, 4)

    def at(self, step=0, other_low=False, other_core=False):
        high = lax.rem(self.high + step + self.pairs, self.pairs) if step else self.high
        low = 1 - self.low if other_low else self.low
        core = 1 - self.core if other_core else self.core
        return (high * 2 + low) * 2 + core


class Gather:
    def __init__(self, wires, place, own, full, view):
        self.wires, self.place, self.own, self.full, self.view = wires, place, own, full, view
        self.sibling = place.at(other_core=True)
        self.late = []

    def share(self, owner, half=None):
        where = self.view(self.full, owner, half)
        self.late.append(self.wires.send(where, where, "dp", self.sibling))

    def first(self):
        place = self.place
        mine = self.view(self.full, place.index, None)
        send = self.wires.send
        self.low = send(self.own, mine, "dp", place.at(other_low=True))
        self.high = [send(self.own, mine, "dp", place.at(j)) for j in range(1, place.pairs)]
        self.late.append(send(self.own, mine, "dp", self.sibling))

    def second(self):
        place = self.place
        send = self.wires.send
        self.relayed = []
        self.low.wait_recv()
        owner = place.at(other_low=True)
        for j in range(1, place.pairs):
            where = self.view(self.full, owner, 0)
            self.relayed.append((j, 0, send(where, where, "dp", place.at(j))))
        self.share(owner)
        for j in range(1, place.pairs):
            self.high[j - 1].wait_recv()
            owner = place.at(-j)
            where = self.view(self.full, owner, 1)
            self.relayed.append((j, 1, send(where, where, "dp", place.at(other_low=True))))
            self.share(owner)

    def third(self):
        for j, half, copy in self.relayed:
            copy.wait_recv()
            self.share(self.place.at(-j, other_low=True), half)

    def done(self):
        for copy in self.late:
            copy.wait_recv()


def by_rows(rows):
    def view(full, owner, half):
        start, size = owner * rows, rows
        if half is not None:
            size = rows // 2
            start = start + half * size
        return full.at[pl.ds(pl.multiple_of(start, 16), size)]

    return view


def by_columns(rows, width, flat):
    def view(full, owner, half):
        part = pl.ds(0, rows) if half is None else pl.ds(half * (rows // 2), rows // 2)
        if flat:
            return full.at[part, pl.ds(pl.multiple_of(owner * width, 128), width)]
        return full.at[owner, part]

    return view


def flat_columns(width):
    return width % 128 == 0


def column_shape(devices, rows, width):
    return (rows, devices * width) if flat_columns(width) else (devices, rows, width)


def tile_of(width, largest):
    return next(t for t in (largest, largest // 2, 256, 128, width) if width % t == 0)


def exp_scores(queries, keys):
    scores = lax.dot_general(queries, keys, (((1,), (1,)), ((), ())), preferred_element_type=jnp.float32)
    return jnp.exp(scores * (1.0 / math.sqrt(HD)))


def pieces_of(own_cols):
    return own_cols // 128 if flat_columns(own_cols) else 1


def scaled_pieces(scaled, up_weight, weight, own_cols):
    adapter = up_weight.shape[-2]
    depth = scaled.shape[0] - adapter
    pieces = pieces_of(own_cols)
    piece = own_cols // pieces
    flat = flat_columns(own_cols)
    triples = [(scaled.at[pl.ds(depth, adapter)], up_weight, by_columns(adapter, own_cols, flat))]
    for p in range(pieces):
        source = scaled.at[pl.ds(0, depth), pl.ds(p * piece, piece)]
        triples.append((source, weight.at[p], by_columns(depth, piece, flat)))
    return triples


class Chain:
    def __init__(self, part, slot, send_sems, recv_sems, chunks):
        self.part, self.slot, self.chunks = part, slot, chunks
        self.send_sems, self.recv_sems = send_sems, recv_sems
        self.count, self.rank = lax.axis_size("seq"), lax.axis_index("seq")
        self.near = 1 - lax.div(self.rank, self.count // 2)
        self.far = 1 - self.near

    def target(self, step, right):
        return right * (self.count - 1 - step) + (1 - right) * step

    def link(self, owner, c, right):
        return pltpu.make_async_remote_copy(
            src_ref=self.part(owner, c),
            dst_ref=self.slot(right, owner, c),
            send_sem=self.send_sems.at[owner * self.chunks + c],
            recv_sem=self.recv_sems.at[(right * self.count + owner) * self.chunks + c],
            device_id={"seq": jnp.clip(self.rank + 2 * right - 1, 0, self.count - 1)},
            device_id_type=MESH,
        )

    def begin(self, step, chunks=None):
        owner = self.target(step, self.near)

        @pl.when((self.rank == 0) | (self.rank == self.count - 1))
        def _():
            for c in range(self.chunks) if chunks is None else chunks:
                self.link(owner, c, self.near).start()

    def forward(self, step, right, chunks=None):
        owner = self.target(step, right)
        ahead = right * (owner - self.rank) + (1 - right) * (self.rank - owner)
        behind = right * self.rank + (1 - right) * (self.count - 1 - self.rank)

        @pl.when((ahead > 0) & (behind > 0))
        def _():
            for c in range(self.chunks) if chunks is None else chunks:
                self.link(owner, c, right).wait_recv()
                part = self.part(owner, c)
                part[...] = (
                    part[...].astype(jnp.float32) + self.slot(right, owner, c)[...].astype(jnp.float32)
                ).astype(part.dtype)
                self.link(owner, c, right).start()

    def arrive(self, c):
        @pl.when(self.rank >= 1)
        def _():
            self.link(self.rank, c, 1).wait_recv()

        @pl.when(self.rank <= self.count - 2)
        def _():
            self.link(self.rank, c, 0).wait_recv()

    def total(self, part, from_left, from_right):
        total = part.astype(jnp.float32)
        total = total + jnp.where(self.rank >= 1, from_left.astype(jnp.float32), 0.0)
        return total + jnp.where(self.rank <= self.count - 2, from_right.astype(jnp.float32), 0.0)

    def drain(self):
        for owner in range(self.count):

            @pl.when(self.rank != owner)
            def _():
                for c in range(self.chunks):
                    self.link(owner, c, 0).wait_send()


class Relay:
    def __init__(self, block, send_sems, recv_sems):
        self.block, self.send_sems, self.recv_sems = block, send_sems, recv_sems
        self.count, self.rank = lax.axis_size("seq"), lax.axis_index("seq")

    def link(self, owner, hop, right):
        index = right * (self.count - 1) + hop
        where = self.block(owner)
        return pltpu.make_async_remote_copy(
            src_ref=where,
            dst_ref=where,
            send_sem=self.send_sems.at[index],
            recv_sem=self.recv_sems.at[index],
            device_id={"seq": jnp.clip(self.rank + 2 * right - 1, 0, self.count - 1)},
            device_id_type=MESH,
        )

    def reaches(self, right):
        return self.rank < self.count - 1 if right else self.rank > 0

    def begin(self):
        for right in (1, 0):

            @pl.when(self.reaches(right))
            def _():
                self.link(self.rank, 0, right).start()

    def forward(self, hop):
        for right in (1, 0):
            owner = self.rank - hop if right else self.rank + hop
            there = owner >= 0 if right else owner < self.count
            owner = jnp.clip(owner, 0, self.count - 1)

            @pl.when(there)
            def _():
                self.link(owner, hop - 1, right).wait_recv()

            if hop < self.count - 1:

                @pl.when(there & self.reaches(right))
                def _():
                    self.link(owner, hop, right).start()

    def drain(self):
        for hop in range(self.count - 1):
            for right in (1, 0):
                owner = self.rank - hop if right else self.rank + hop
                there = owner >= 0 if right else owner < self.count

                @pl.when(there & self.reaches(right))
                def _():
                    self.link(self.rank, hop, right).wait_send()


def front_part(
    owner_ref, enc_ref, gain_ref, in_ref, out_ref, final_ref, context_ref, kv_ref, image_ref,
    proj_ref, down_ref, up_ref, magnitude_ref, scale_ref, shift_ref, image_gain_ref,
    queries, mixture, denominator, key_value, own_scaled, weight, up_weight, ratio_ref,
    image_all, tokens, normed, in_tiles, out_tiles, hidden, part, sum_slots, encoded, context_all, kv_all,
    context_part, row_slots, stage, prompts, sibling_prompts, text_all,
    direction, squares, square_slots,
    in_sems, out_sems, local_sems, send_sems, recv_sems, sum_send, sum_recv, row_send, row_recv, text_send, text_recv,
):
    f32, bf16 = jnp.float32, jnp.bfloat16
    count, devices = lax.axis_size("seq"), lax.axis_size("dp")
    rank, data_rank = lax.axis_index("seq"), lax.axis_index("dp")
    place = Place()
    wires = Wires(send_sems, recv_sems)
    text, width_enc = tokens.shape
    feat = encoded.shape[1]
    width = context_part.shape[1]
    rows = stage.shape[0]
    slots = in_tiles.shape[0]
    tile = in_tiles.shape[2] // 2
    tiles = hidden.shape[1] // tile
    depth, own_cols = proj_ref.shape
    flat = flat_columns(own_cols)
    late = count // 2

    class in_copy:
        def __init__(self, i, slot):
            columns = pl.ds(pl.multiple_of(i * tile, 128), tile)
            self.copies = [
                pltpu.make_async_copy(
                    in_ref.at[side, :, columns],
                    in_tiles.at[slot, :, side * tile : (side + 1) * tile],
                    in_sems.at[slot * 2 + side],
                )
                for side in range(2)
            ]

        def start(self):
            for copy in self.copies:
                copy.start()

        def wait(self):
            for copy in self.copies:
                copy.wait()

    near = 1 - lax.div(rank, count // 2)
    out_slots, _, out_tile = out_tiles.shape
    chunks = feat // out_tile

    def out_copy(i):
        step, c = divmod(i, chunks)
        owner = near * (count - 1 - step) + (1 - near) * step
        columns = pl.ds(pl.multiple_of(owner * feat + c * out_tile, 128), out_tile)
        slot = i % out_slots
        return pltpu.make_async_copy(out_ref.at[:, columns], out_tiles.at[slot], out_sems.at[slot])

    def local(source, target, index):
        return pltpu.make_async_copy(source, target, local_sems.at[index])

    token_copy = local(enc_ref.at[0, pl.ds(0, text)], tokens, 0)
    token_copy.start()
    for i in range(min(slots, tiles)):
        in_copy(i, i).start()
    for i in range(min(out_slots, count * chunks)):
        out_copy(i).start()

    def heads_of(owner):
        head_width = image_all.shape[3]
        return pl.ds(pl.multiple_of(owner * head_width, 128), head_width)

    context_view = by_columns(context_ref.shape[0], own_cols, flat)
    kv_view = by_rows(kv_ref.shape[0])
    context_gather = Gather(wires, place, context_ref, context_all, context_view)
    kv_gather = Gather(wires, place, kv_ref, kv_all, kv_view)

    locals_ = [
        local(image_ref.at[:, :, heads_of(rank)], image_all.at[0], 2),
        local(context_ref, context_view(context_all, data_rank, None), 3),
        local(kv_ref, kv_view(kv_all, data_rank, None), 4),
    ]
    scaled_gathers, scaled_locals = [], []
    for source, target, view in scaled_pieces(own_scaled, up_weight, weight, own_cols)[:2]:
        scaled_gathers.append(Gather(wires, place, source, target, view))
        scaled_locals.append(local(source, view(target, data_rank, None), 5 + len(scaled_locals)))
    image_rows = image_all.shape[2]
    heads = image_all.shape[3] // HD

    def head(h):
        return pl.ds(pl.multiple_of(h * HD, HD), HD)

    def query_step(h, carry):
        for k in range(count):
            queries[k * image_rows : (k + 1) * image_rows, head(h)] = rms_scale(
                image_all[k, 0, :, head(h)].astype(f32), image_gain_ref[0:1, :]
            ).astype(bf16)
        return carry

    def attend(k):
        def head_step(h, carry):
            keys = rms_scale(image_all[k, 1, :, head(h)].astype(f32), image_gain_ref[1:2, :]).astype(bf16)
            share = exp_scores(queries[:, head(h)], keys)
            total = jnp.broadcast_to(jnp.sum(share, -1, keepdims=True), (share.shape[0], HD))
            mixed = jnp.dot(share.astype(bf16), image_all[k, 2, :, head(h)], preferred_element_type=f32)
            if k:
                total = total + denominator[:, head(h)]
                mixed = mixed + mixture[:, head(h)]
            denominator[:, head(h)] = total
            mixture[:, head(h)] = mixed
            return carry

        if k:
            image_copies[k, 1].wait_recv()
            image_copies[k, 2].wait_recv()
        lax.fori_loop(0, heads, head_step, 0)

    greet("seq", "dp")
    context_gather.first()
    image_copies = {}

    def image(k, kind):
        peer = lax.rem(rank + k, count)
        image_copies[k, kind] = wires.send(
            image_ref.at[kind, :, heads_of(peer)], image_all.at[k, kind], "seq", peer
        )

    def images(kinds):
        for k in range(2, count):
            if k != late:
                for kind in kinds:
                    image(k, kind)

    for kind in range(3):
        image(1, kind)

    for copy in locals_:
        copy.start()

    token_copy.wait()
    for r in range(0, text, 32):
        block = tokens[r : r + 32, :].astype(f32)
        normed[r : r + 32, :] = rms_scale(block, gain_ref[...]).astype(bf16)

    def in_step(i, carry):
        slot = lax.rem(i, slots)
        in_copy(i, slot).wait()
        both = jnp.dot(normed[...], in_tiles[slot], preferred_element_type=f32)
        gate, upward = both[:, :tile], both[:, tile:]
        columns = pl.ds(pl.multiple_of(i * tile, 128), tile)
        hidden[:, columns] = (jax.nn.gelu(gate, approximate=True) * upward).astype(bf16)

        @pl.when(i + slots < tiles)
        def _():
            in_copy(i + slots, slot).start()

        return carry

    lax.fori_loop(0, tiles, in_step, 0)

    def piece(c):
        return slice(c * out_tile, (c + 1) * out_tile)

    sums = Chain(
        lambda owner, c: part.at[owner, :, piece(c)],
        lambda right, owner, c: sum_slots.at[owner + right, :, piece(c)],
        sum_send,
        sum_recv,
        chunks,
    )
    if late > 1:
        image(late, 0)
    for step in range(count):
        owner = sums.target(step, sums.near)
        for c in range(sums.chunks):
            index = step * chunks + c
            out_copy(index).wait()
            part[owner, :, piece(c)] = jnp.dot(
                hidden[...], out_tiles[index % out_slots], preferred_element_type=f32
            ).astype(bf16)
            if index + out_slots < count * chunks:
                out_copy(index + out_slots).start()
            if step < count - 1:
                sums.begin(step, (c,))

    context_gather.second()
    kv_gather.first()

    total = jnp.zeros((1, own_cols), f32)
    for r in range(0, depth, 128):
        block = proj_ref[r : r + 128, :].astype(f32) + lax.dot_general(
            down_ref[:, r : r + 128],
            up_ref[...],
            (((0,), (0,)), ((), ())),
            precision=lax.Precision.HIGHEST,
            preferred_element_type=f32,
        )
        direction[r : r + 128, :] = block
        total = total + jnp.sum(block * block, 0, keepdims=True)
    squares[...] = total
    square_copies = [wires.send(squares, square_slots.at[k - 1], "seq", peer) for k, peer in peers("seq")]

    for step in range(count - 1):
        sums.forward(step, sums.near)
        sums.forward(step, sums.far)
    context_gather.third()
    for c in range(sums.chunks):
        sums.arrive(c)
    images((0,))
    own = pl.ds(pl.multiple_of(rank * feat, 128), feat)
    for r in range(0, text, 32):
        block = slice(r, r + 32)
        total = sums.total(part[rank, block, :], sum_slots[rank + 1, block, :], sum_slots[rank, block, :])
        encoded[block, :] = ((tokens[block, own].astype(f32) + total) * final_ref[:, own]).astype(bf16)

    locals_[1].wait()
    context_gather.done()
    if late > 1:
        image(late, 1)

    def block_of(index):
        return pl.ds(pl.multiple_of(index * rows, 16), rows)

    half = width // 2
    row_sums = Chain(
        lambda owner, c: context_part.at[block_of(owner), c * half : (c + 1) * half],
        lambda right, owner, c: row_slots.at[owner + right, :, c * half : (c + 1) * half],
        row_send,
        row_recv,
        2,
    )
    for c in range(2):
        if flat:
            step = tile_of(half, 512)
            for start in range(c * half, (c + 1) * half, step):
                context_part[:, start : start + step] = jnp.dot(
                    encoded[...], context_all[:, start : start + step], preferred_element_type=f32
                ).astype(bf16)
        else:
            for d in range(c * devices // 2, (c + 1) * devices // 2):
                context_part[:, d * own_cols : (d + 1) * own_cols] = jnp.dot(
                    encoded[...], context_all[d], preferred_element_type=f32
                ).astype(bf16)
        for step in range(count - 1):
            row_sums.begin(step, (c,))
    for copy in square_copies:
        copy.wait_recv()
    total = squares[...]
    for k in range(1, count):
        total = total + square_slots[k - 1]
    ratio = magnitude_ref[...].reshape(1, own_cols) / jnp.sqrt(total + EPSILON)
    ratio_ref[...] = ratio
    for r in range(0, depth, 128):
        own_scaled[r : r + 128, :] = (direction[r : r + 128, :] * ratio).astype(bf16)
    own_scaled[depth:, :] = (up_ref[...] * ratio).astype(bf16)

    for c in range(2):
        for step in range(count - 1):
            row_sums.forward(step, row_sums.near, (c,))
            row_sums.forward(step, row_sums.far, (c,))
        if c == 0:
            kv_gather.second()
    for c in range(2):
        row_sums.arrive(c)
    stage[...] = row_sums.total(
        context_part[block_of(rank), :], row_slots[rank + 1], row_slots[rank]
    ).astype(bf16)

    chips = devices // 2
    chip = lax.div(data_rank, 2)
    sibling = place.at(other_core=True)
    prompt_copies = [
        wires.send(stage, prompts.at[j - 1], "dp", lax.rem(chip + j, chips) * 2 + place.core)
        for j in range(1, chips)
    ]
    shared = [wires.send(stage, sibling_prompts.at[0], "dp", sibling)]
    images((1, 2))
    for gather, copy in zip(scaled_gathers, scaled_locals):
        gather.first()
        copy.start()
    locals_[0].wait()
    for k in range(1, count):
        image_copies[k, 0].wait_recv()
    lax.fori_loop(0, heads, query_step, 0)
    attend(0)
    attend(1)
    for j in range(1, chips):
        prompt_copies[j - 1].wait_recv()
        shared.append(wires.send(prompts.at[j - 1], sibling_prompts.at[j], "dp", sibling))
    routed = jnp.where(owner_ref[data_rank] == data_rank, stage[...].astype(f32), 0.0)
    for j in range(1, chips):
        prompt = lax.rem(chip + chips - j, chips) * 2 + place.core
        routed = routed + jnp.where(owner_ref[prompt] == data_rank, prompts[j - 1].astype(f32), 0.0)
    for j in range(chips):
        shared[j].wait_recv()
        prompt = lax.rem(chip + chips - j, chips) * 2 + 1 - place.core
        routed = routed + jnp.where(owner_ref[prompt] == data_rank, sibling_prompts[j].astype(f32), 0.0)
    centre = jnp.mean(routed, -1, keepdims=True)
    spread = jnp.mean((routed - centre) * (routed - centre), -1, keepdims=True)
    layer_normed = (routed - centre) * lax.rsqrt(spread + EPSILON)
    text_all[block_of(rank), :] = ((1.0 + scale_ref[...]) * layer_normed + shift_ref[...]).astype(bf16)
    if late > 1:
        image(late, 2)
    texts = Relay(lambda owner: text_all.at[block_of(owner)], text_send, text_recv)
    texts.begin()
    for k in [k for k in range(2, count) if k != late] + [late] * (late > 1):
        attend(k)
    for gather in scaled_gathers:
        gather.second()
    for hop in range(1, count):
        texts.forward(hop)
    kv_gather.third()
    for gather in scaled_gathers:
        gather.third()
    locals_[2].wait()
    kv_gather.done()
    step = tile_of(kv_all.shape[1], 512)
    for c in range(0, kv_all.shape[1], step):
        key_value[:, c : c + step] = jnp.dot(
            text_all[...], kv_all[:, c : c + step], preferred_element_type=f32
        )
    for gather, copy in zip(scaled_gathers, scaled_locals):
        gather.done()
        copy.wait()
    return sums, row_sums, texts, wires


def back_part(
    owner_ref, lengths_ref, text_gain_ref, key_value_ref, queries_ref, mixture_ref, denominator_ref,
    scaled_ref, weight, up_weight_ref, dora_ref, grad_ref, ratio_ref, magnitude_ref,
    image_out, down_out, cols_out, size_out,
    attended, parts, slots, down, up, up_slots, down_slots,
    cols, col_slots, col_stage, col_sums, rows_all, row_slots, row_stage, row_sums,
    size, size_slots, size_stage, size_sums,
    local_sems, chain_send, chain_recv, send_sems, recv_sems,
):
    count, devices = lax.axis_size("seq"), lax.axis_size("dp")
    rank, data_rank = lax.axis_index("seq"), lax.axis_index("dp")
    rows, width = image_out.shape
    depth = queries_ref.shape[1]
    text = key_value_ref.shape[0]
    heads = depth // HD
    own_cols = ratio_ref.shape[1]
    adapter = dora_ref.shape[0]
    pieces = pieces_of(own_cols)
    piece = own_cols // pieces
    flat = flat_columns(own_cols)
    block_rows = depth // devices
    f32, bf16 = jnp.float32, jnp.bfloat16
    over_rows = (((0,), (0,)), ((), ()))
    over_columns = (((1,), (1,)), ((), ()))
    wires = Wires(send_sems, recv_sems)
    place = Place()

    def block_of(owner):
        return lax.rem(rank + count - owner, count)

    chain = Chain(
        lambda owner, p: parts.at[owner, p],
        lambda right, owner, p: slots.at[owner + right, p],
        chain_send,
        chain_recv,
        pieces,
    )
    near, far = chain.near, chain.far
    gathers, owns = [None], [None]
    for source, target, view in scaled_pieces(scaled_ref, up_weight_ref, weight, own_cols)[2:]:
        gathers.append(Gather(wires, place, source, target, view))
        owns.append(
            pltpu.make_async_copy(source, view(target, data_rank, None), local_sems.at[len(owns) - 1])
        )
    if pieces > 1:
        gathers[1].first()
    for copy in owns[1:]:
        copy.start()

    length = jnp.int32(0)
    for p in range(devices):
        length = length + jnp.where(owner_ref[p] == data_rank, lengths_ref[p], 0)

    def head(h):
        return pl.ds(pl.multiple_of(h * HD, HD), HD)

    def head_step(h, carry):
        keys = rms_scale(key_value_ref[:, head(h)], text_gain_ref[...]).astype(bf16)
        values = key_value_ref[:, pl.ds(pl.multiple_of(depth + h * HD, HD), HD)].astype(bf16)
        share = exp_scores(queries_ref[:, head(h)], keys)
        position = lax.broadcasted_iota(jnp.int32, share.shape, 1)
        share = jnp.where(position < length, share, 0.0)
        denominator = denominator_ref[:, head(h)] + jnp.sum(share, -1, keepdims=True)
        mixture = mixture_ref[:, head(h)] + jnp.dot(share.astype(bf16), values, preferred_element_type=f32)
        attended[:, head(h)] = (mixture / denominator).astype(bf16)
        return carry

    lax.fori_loop(0, heads, head_step, 0)

    def products(p, begin=True):
        if p:
            gathers[p].done()
            owns[p].wait()
        source = weight.at[p]
        for step in range(count):
            owner = chain.target(step, near)
            block = attended[pl.ds(pl.multiple_of(block_of(owner) * rows, 16), rows), :]
            if flat:
                parts[owner, p] = jnp.dot(block, source[...], preferred_element_type=f32).astype(bf16)
            else:
                for d in range(devices):
                    parts[owner, p, :, d * piece : (d + 1) * piece] = jnp.dot(
                        block, source[d], preferred_element_type=f32
                    ).astype(bf16)
            if begin and step < count - 1:
                chain.begin(step, (p,))

    if flat:
        down_total = lax.dot_general(grad_ref[...], up_weight_ref[...], over_columns, preferred_element_type=f32)
    else:
        down_total = jnp.zeros((rows, adapter), f32)
        for d in range(devices):
            down_total = down_total + lax.dot_general(
                grad_ref[:, d * own_cols : (d + 1) * own_cols],
                up_weight_ref[d],
                over_columns,
                preferred_element_type=f32,
            )
    down[...] = down_total.astype(bf16)
    ups = lax.dot_general(
        attended[...], dora_ref[...].astype(bf16), over_columns, preferred_element_type=f32
    ).astype(bf16)
    for k in range(count):
        up[k] = ups[k * rows : (k + 1) * rows]
    small = []
    for k, peer in peers("seq"):
        small.append(wires.send(down, down_slots.at[k - 1], "seq", peer))
        before = lax.rem(rank + count - k, count)
        small.append(wires.send(up.at[k], up_slots.at[k - 1], "seq", before))
    def forwards(p):
        for step in range(count - 1):
            chain.forward(step, near, (p,))
            chain.forward(step, far, (p,))

    def prepare(p):
        gathers[p].second()
        if p + 1 < pieces:
            gathers[p + 1].first()
        gathers[p].third()
        products(p, p + 1 < pieces)

    products(0)
    if pieces > 1:
        prepare(1)
        forwards(0)
    for p in range(2, pieces):
        prepare(p)
    for copy in small:
        copy.wait_recv()
    up_total = up[0].astype(f32)
    for k in range(1, count):
        up_total = up_total + up_slots[k - 1].astype(f32)
    up_total = up_total.astype(bf16)
    column_grad = lax.dot_general(up_total, grad_ref[...], over_rows, preferred_element_type=f32).astype(bf16)
    for j in range(devices):
        cols[j] = column_grad[:, j * own_cols : (j + 1) * own_cols]
    row_grad = lax.dot_general(down[...], attended[:rows, :], over_rows, preferred_element_type=f32)
    for k in range(1, count):
        row_grad = row_grad + lax.dot_general(
            down_slots[k - 1], attended[k * rows : (k + 1) * rows, :], over_rows, preferred_element_type=f32
        )
    for j in range(devices):
        rows_all[j] = row_grad[:, j * block_rows : (j + 1) * block_rows].astype(bf16)
    first = []
    for k, peer in peers("dp"):
        first.append(wires.send(cols.at[peer], col_slots.at[k - 1], "dp", peer))
        first.append(wires.send(rows_all.at[peer], row_slots.at[k - 1], "dp", peer))

    for p in range(1, pieces - 1):
        forwards(p)
    for copy in first:
        copy.wait_recv()
    col_total = cols[data_rank].astype(f32)
    row_total = rows_all[data_rank].astype(f32)
    for k, _ in peers("dp"):
        col_total = col_total + col_slots[k - 1].astype(f32)
        row_total = row_total + row_slots[k - 1].astype(f32)
    col_stage[...] = col_total.astype(bf16)
    row_stage[...] = row_total.astype(bf16)
    second = []
    for k, peer in peers("seq"):
        second.append(wires.send(col_stage, col_sums.at[k - 1], "seq", peer))
    for k, peer in peers("dp"):
        second.append(wires.send(row_stage, row_sums.at[data_rank], "dp", peer))
    row_sums[data_rank] = row_stage[...]
    if pieces > 1:
        for step in range(count - 1):
            chain.begin(step, (pieces - 1,))
    forwards(pieces - 1)

    for p in range(pieces):
        chain.arrive(p)
        total = chain.total(parts[rank, p], slots[rank + 1, p], slots[rank, p])
        for d in range(devices):
            own = slice(d * own_cols + p * piece, d * own_cols + (p + 1) * piece)
            block = total[:, d * piece : (d + 1) * piece]
            image_out[:, own] = block.astype(bf16)
            size[d, :, p * piece : (p + 1) * piece] = jnp.sum(
                grad_ref[:, own].astype(f32) * block, 0, keepdims=True
            )
    last = [wires.send(size.at[peer], size_slots.at[k - 1], "dp", peer) for k, peer in peers("dp")]
    for copy in second:
        copy.wait_recv()
    col_total = col_stage[...].astype(f32)
    for k, _ in peers("seq"):
        col_total = col_total + col_sums[k - 1].astype(f32)
    cols_out[...] = col_total * ratio_ref[...]
    for d in range(devices):
        down_out[:, d * block_rows : (d + 1) * block_rows] = row_sums[d].astype(f32)
    for copy in last:
        copy.wait_recv()
    size_total = size[data_rank]
    for k, _ in peers("dp"):
        size_total = size_total + size_slots[k - 1]
    size_stage[...] = size_total
    last = [wires.send(size_stage, size_sums.at[k - 1], "seq", peer) for k, peer in peers("seq")]
    for copy in last:
        copy.wait_recv()
    for k, _ in peers("seq"):
        size_total = size_total + size_sums[k - 1]
    size_out[...] = size_total / magnitude_ref[...].reshape(1, own_cols)
    chain.drain()
    wires.drain()


def program_kernel(counts, *refs):
    names = []
    for n in counts:
        names.append(refs[:n])
        refs = refs[n:]
    front_in, back_in, outs, shared, front_scratch, back_scratch = names
    key_value, queries, mixture, denominator, own_scaled, weight, up_weight, ratio = shared
    owner, down, magnitude = front_in[0], front_in[10], front_in[12]
    waits = front_part(
        *front_in, queries, mixture, denominator, key_value, own_scaled, weight, up_weight, ratio, *front_scratch
    )
    lengths, text_gain, grad = back_in
    back_part(
        owner, lengths, text_gain, key_value, queries, mixture, denominator,
        own_scaled, weight, up_weight, down, grad, ratio, magnitude,
        *outs, *back_scratch,
    )
    for wait in waits:
        wait.drain()


def program(
    owner, enc, gain, w_in, w_out, final_gain, context, kv, image, proj, down, up, magnitude, scale, shift,
    image_gain, lengths, text_gain, grad,
):
    count, devices = lax.axis_size("seq"), lax.axis_size("dp")
    bf16, f32 = jnp.bfloat16, jnp.float32
    width_enc, hidden = w_in.shape[1:]
    feat = width_enc // count
    text = MAX_PROMPT
    width = scale.shape[1]
    text_rows = text // count
    kinds, rows, _ = image.shape
    head_width = width // count
    depth, own_cols = proj.shape
    rank = up.shape[0]
    block_rows = depth // devices
    pieces = pieces_of(own_cols)
    piece = own_cols // pieces
    others, data_others, pairs = count - 1, devices - 1, devices // 4
    tile, out_tile = tile_of(hidden, 128), tile_of(feat, 512)
    slots = 3
    sum_chunks = feat // out_tile
    per_gather = 6 * pairs - 3
    front_wires = 4 * others + 4 * pairs + 4 * per_gather
    back_wires = 4 * others + 4 * data_others + pieces * per_gather
    any_ = pl.BlockSpec(memory_space=pl.ANY)
    vmem, sems = pltpu.VMEM, pltpu.SemaphoreType.DMA
    shared = [
        vmem((text, kv.shape[1]), f32),
        vmem((count * rows, head_width), bf16),
        vmem((count * rows, head_width), f32),
        vmem((count * rows, head_width), f32),
        vmem((depth + rank, own_cols), bf16),
        vmem((pieces,) + column_shape(devices, depth, piece), bf16),
        vmem(column_shape(devices, rank, own_cols), bf16),
        vmem((1, own_cols), f32),
    ]
    front_scratch = [
        vmem((count, kinds, rows, head_width), bf16),
        vmem((text, width_enc), bf16),
        vmem((text, width_enc), bf16),
        vmem((slots, width_enc, 2 * tile), bf16),
        vmem((slots, hidden, out_tile), bf16),
        vmem((text, hidden), bf16),
        vmem((count, text, feat), bf16),
        vmem((count + 1, text, feat), bf16),
        vmem((text, feat), bf16),
        vmem(column_shape(devices, context.shape[0], own_cols), bf16),
        vmem((kv.shape[0] * devices, kv.shape[1]), bf16),
        vmem((text, width), bf16),
        vmem((count + 1, text_rows, width), bf16),
        vmem((text_rows, width), bf16),
        vmem((devices // 2 - 1, text_rows, width), bf16),
        vmem((devices // 2, text_rows, width), bf16),
        vmem((text, width), bf16),
        vmem((depth, own_cols), f32),
        vmem((1, own_cols), f32),
        vmem((others, 1, own_cols), f32),
        sems((slots * 2,)),
        sems((slots,)),
        sems((7,)),
        sems((front_wires,)),
        sems((front_wires,)),
        sems((count * sum_chunks,)),
        sems((count * 2 * sum_chunks,)),
        sems((count * 2,)),
        sems((count * 4,)),
        sems((count * 2,)),
        sems((count * 2,)),
    ]
    back_scratch = [
        vmem((count * rows, head_width), bf16),
        vmem((count, pieces, rows, devices * piece), bf16),
        vmem((count + 1, pieces, rows, devices * piece), bf16),
        vmem((rows, rank), bf16),
        vmem((count, rows, rank), bf16),
        vmem((others, rows, rank), bf16),
        vmem((others, rows, rank), bf16),
        vmem((devices, rank, own_cols), bf16),
        vmem((data_others, rank, own_cols), bf16),
        vmem((rank, own_cols), bf16),
        vmem((others, rank, own_cols), bf16),
        vmem((devices, rank, block_rows), bf16),
        vmem((data_others, rank, block_rows), bf16),
        vmem((rank, block_rows), bf16),
        vmem((devices, rank, block_rows), bf16),
        vmem((devices, 1, own_cols), f32),
        vmem((data_others, 1, own_cols), f32),
        vmem((1, own_cols), f32),
        vmem((others, 1, own_cols), f32),
        sems((pieces + 1,)),
        sems((count * pieces,)),
        sems((count * 2 * pieces,)),
        sems((back_wires,)),
        sems((back_wires,)),
    ]
    front_in = (
        owner, enc, gain, w_in, w_out, final_gain, context, kv, image, proj, down, up, magnitude, scale, shift,
        image_gain,
    )
    back_in = (lengths, text_gain, grad)
    counts = (len(front_in), len(back_in), 4, len(shared), len(front_scratch), len(back_scratch))
    return pl.pallas_call(
        functools.partial(program_kernel, counts),
        out_shape=[
            jax.ShapeDtypeStruct(grad.shape, bf16),
            jax.ShapeDtypeStruct((rank, depth), f32),
            jax.ShapeDtypeStruct((rank, own_cols), f32),
            jax.ShapeDtypeStruct((1, own_cols), f32),
        ],
        in_specs=[SMEM, any_, VMEM, any_, any_, VMEM, any_, any_, any_] + [VMEM] * 7 + [SMEM, VMEM, VMEM],
        out_specs=[VMEM] * 4,
        scratch_shapes=shared + front_scratch + back_scratch,
        compiler_params=pltpu.CompilerParams(
            collective_id=1, has_side_effects=True, vmem_limit_bytes=63 * 2**20
        ),
    )(*front_in, *back_in)


def results_kernel(*refs):
    half = len(refs) // 2
    for source, target in zip(refs[:half], refs[half:]):
        target[...] = source[...].reshape(target.shape)


def results(*values):
    shapes = [jax.ShapeDtypeStruct(v.shape if v.shape[0] > 1 else v.shape[1:], v.dtype) for v in values]
    return pl.pallas_call(
        results_kernel, out_shape=shapes, in_specs=[VMEM] * len(values), out_specs=[VMEM] * len(values)
    )(*values)


def on_device(
    enc_states,
    lengths,
    prompt_owner_sample,
    t5_gain,
    t5_in_weight,
    t5_out_weight,
    t5_final_gain,
    context_weight,
    text_shift,
    text_scale,
    kv_weight,
    text_key_gain,
    image_query_key_value,
    image_qk_gain,
    proj_weight,
    dora_a,
    dora_b,
    magnitude,
    grad_out,
):
    outs = program(
        prompt_owner_sample,
        enc_states,
        t5_gain[None],
        t5_in_weight,
        t5_out_weight,
        t5_final_gain[None],
        context_weight,
        kv_weight.reshape(kv_weight.shape[0], -1),
        jnp.transpose(image_query_key_value[0], (1, 0, 2)),
        proj_weight,
        dora_a.T,
        dora_b,
        magnitude,
        text_scale,
        text_shift,
        image_qk_gain,
        lengths,
        text_key_gain[None],
        grad_out[0],
    )
    image_out, grad_a, grad_b, grad_magnitude = results(*outs)
    return (image_out[None], grad_a.T, grad_b, grad_magnitude)


def solution(mesh):
    mapped = jax.shard_map(
        on_device,
        mesh=mesh,
        in_specs=(
            P("dp", None, None),
            P(),
            P(),
            P(),
            P(None, None, "seq"),
            P("seq", None),
            P(),
            P("seq", "dp"),
            P("dp", None),
            P("dp", None),
            P("dp", None, "seq"),
            P(),
            P("dp", "seq", None, None),
            P(),
            P("seq", "dp"),
            P("seq", None),
            P(None, "dp"),
            P("dp"),
            P("dp", "seq", None),
        ),
        out_specs=(P("dp", "seq", None), P("seq", None), P(None, "dp"), P("dp")),
        check_vma=False,
    )
    return mapped
```

```python
import functools
import math

import jax
import jax.numpy as jnp
from jax import lax
from jax.experimental import pallas as pl
from jax.experimental.pallas import tpu as pltpu
from jax.sharding import PartitionSpec as P

HD = 128
MAX_PROMPT = 128
EPSILON = 1e-06


def rms_scale(values, gain):
    return values * lax.rsqrt(jnp.mean(values * values, -1, keepdims=True) + EPSILON) * gain


def peers(axis):
    size, rank = lax.axis_size(axis), lax.axis_index(axis)
    return [(k, lax.rem(rank + k, size)) for k in range(1, size)]


def greet(*axes):
    barrier = pltpu.get_barrier_semaphore()
    count = 0
    for axis in axes:
        for _, peer in peers(axis):
            pl.semaphore_signal(
                barrier, inc=1, device_id={axis: peer}, device_id_type=pl.DeviceIdType.MESH
            )
            count += 1
    pl.semaphore_wait(barrier, count)


VMEM = pl.BlockSpec(memory_space=pltpu.VMEM)
SMEM = pl.BlockSpec(memory_space=pltpu.SMEM)


MESH = pl.DeviceIdType.MESH


class Wires:
    def __init__(self, send_sems, recv_sems):
        self.send_sems, self.recv_sems, self.copies = send_sems, recv_sems, []

    def send(self, source, target, axis, peer):
        index = len(self.copies)
        copy = pltpu.make_async_remote_copy(
            src_ref=source,
            dst_ref=target,
            send_sem=self.send_sems.at[index],
            recv_sem=self.recv_sems.at[index],
            device_id={axis: peer},
            device_id_type=MESH,
        )
        copy.start()
        self.copies.append(copy)
        return copy

    def drain(self):
        for copy in self.copies:
            copy.wait_send()


class Place:
    def __init__(self):
        self.pairs = lax.axis_size("dp") // 4
        index = lax.axis_index("dp")
        self.index = index
        self.core = lax.rem(index, 2)
        self.low = lax.rem(lax.div(index, 2), 2)
        self.high = lax.div(index, 4)

    def at(self, step=0, other_low=False, other_core=False):
        high = lax.rem(self.high + step + self.pairs, self.pairs) if step else self.high
        low = 1 - self.low if other_low else self.low
        core = 1 - self.core if other_core else self.core
        return (high * 2 + low) * 2 + core


class Gather:
    def __init__(self, wires, place, own, full, view):
        self.wires, self.place, self.own, self.full, self.view = wires, place, own, full, view
        self.sibling = place.at(other_core=True)
        self.late = []

    def share(self, owner, half=None):
        where = self.view(self.full, owner, half)
        self.late.append(self.wires.send(where, where, "dp", self.sibling))

    def first(self):
        place = self.place
        mine = self.view(self.full, place.index, None)
        send = self.wires.send
        self.low = send(self.own, mine, "dp", place.at(other_low=True))
        self.high = [send(self.own, mine, "dp", place.at(j)) for j in range(1, place.pairs)]
        self.late.append(send(self.own, mine, "dp", self.sibling))

    def second(self):
        place = self.place
        send = self.wires.send
        self.relayed = []
        self.low.wait_recv()
        owner = place.at(other_low=True)
        for j in range(1, place.pairs):
            where = self.view(self.full, owner, 0)
            self.relayed.append((j, 0, send(where, where, "dp", place.at(j))))
        self.share(owner)
        for j in range(1, place.pairs):
            self.high[j - 1].wait_recv()
            owner = place.at(-j)
            where = self.view(self.full, owner, 1)
            self.relayed.append((j, 1, send(where, where, "dp", place.at(other_low=True))))
            self.share(owner)

    def third(self):
        for j, half, copy in self.relayed:
            copy.wait_recv()
            self.share(self.place.at(-j, other_low=True), half)

    def done(self):
        for copy in self.late:
            copy.wait_recv()


def by_rows(rows):
    def view(full, owner, half):
        start, size = owner * rows, rows
        if half is not None:
            size = rows // 2
            start = start + half * size
        return full.at[pl.ds(pl.multiple_of(start, 16), size)]

    return view


def by_columns(rows, width, flat):
    def view(full, owner, half):
        part = pl.ds(0, rows) if half is None else pl.ds(half * (rows // 2), rows // 2)
        if flat:
            return full.at[part, pl.ds(pl.multiple_of(owner * width, 128), width)]
        return full.at[owner, part]

    return view


def flat_columns(width):
    return width % 128 == 0


def column_shape(devices, rows, width):
    return (rows, devices * width) if flat_columns(width) else (devices, rows, width)


def tile_of(width, largest):
    return next(t for t in (largest, largest // 2, 256, 128, width) if width % t == 0)


def exp_scores(queries, keys):
    scores = lax.dot_general(queries, keys, (((1,), (1,)), ((), ())), preferred_element_type=jnp.float32)
    return jnp.exp(scores * (1.0 / math.sqrt(HD)))


def pieces_of(own_cols):
    return own_cols // 128 if flat_columns(own_cols) else 1


def scaled_pieces(scaled, up_weight, weight, own_cols):
    adapter = up_weight.shape[-2]
    depth = scaled.shape[0] - adapter
    pieces = pieces_of(own_cols)
    piece = own_cols // pieces
    flat = flat_columns(own_cols)
    triples = [(scaled.at[pl.ds(depth, adapter)], up_weight, by_columns(adapter, own_cols, flat))]
    for p in range(pieces):
        source = scaled.at[pl.ds(0, depth), pl.ds(p * piece, piece)]
        triples.append((source, weight.at[p], by_columns(depth, piece, flat)))
    return triples


class Chain:
    def __init__(self, part, slot, send_sems, recv_sems, chunks):
        self.part, self.slot, self.chunks = part, slot, chunks
        self.send_sems, self.recv_sems = send_sems, recv_sems
        self.count, self.rank = lax.axis_size("seq"), lax.axis_index("seq")
        self.near = 1 - lax.div(self.rank, self.count // 2)
        self.far = 1 - self.near

    def target(self, step, right):
        return right * (self.count - 1 - step) + (1 - right) * step

    def link(self, owner, c, right):
        return pltpu.make_async_remote_copy(
            src_ref=self.part(owner, c),
            dst_ref=self.slot(right, owner, c),
            send_sem=self.send_sems.at[owner * self.chunks + c],
            recv_sem=self.recv_sems.at[(right * self.count + owner) * self.chunks + c],
            device_id={"seq": jnp.clip(self.rank + 2 * right - 1, 0, self.count - 1)},
            device_id_type=MESH,
        )

    def begin(self, step, chunks=None):
        owner = self.target(step, self.near)

        @pl.when((self.rank == 0) | (self.rank == self.count - 1))
        def _():
            for c in range(self.chunks) if chunks is None else chunks:
                self.link(owner, c, self.near).start()

    def forward(self, step, right, chunks=None):
        owner = self.target(step, right)
        ahead = right * (owner - self.rank) + (1 - right) * (self.rank - owner)
        behind = right * self.rank + (1 - right) * (self.count - 1 - self.rank)

        @pl.when((ahead > 0) & (behind > 0))
        def _():
            for c in range(self.chunks) if chunks is None else chunks:
                self.link(owner, c, right).wait_recv()
                part = self.part(owner, c)
                part[...] = (
                    part[...].astype(jnp.float32) + self.slot(right, owner, c)[...].astype(jnp.float32)
                ).astype(part.dtype)
                self.link(owner, c, right).start()

    def arrive(self, c):
        @pl.when(self.rank >= 1)
        def _():
            self.link(self.rank, c, 1).wait_recv()

        @pl.when(self.rank <= self.count - 2)
        def _():
            self.link(self.rank, c, 0).wait_recv()

    def total(self, part, from_left, from_right):
        total = part.astype(jnp.float32)
        total = total + jnp.where(self.rank >= 1, from_left.astype(jnp.float32), 0.0)
        return total + jnp.where(self.rank <= self.count - 2, from_right.astype(jnp.float32), 0.0)

    def drain(self):
        for owner in range(self.count):

            @pl.when(self.rank != owner)
            def _():
                for c in range(self.chunks):
                    self.link(owner, c, 0).wait_send()


class Relay:
    def __init__(self, block, send_sems, recv_sems):
        self.block, self.send_sems, self.recv_sems = block, send_sems, recv_sems
        self.count, self.rank = lax.axis_size("seq"), lax.axis_index("seq")

    def link(self, owner, hop, right):
        index = right * (self.count - 1) + hop
        where = self.block(owner)
        return pltpu.make_async_remote_copy(
            src_ref=where,
            dst_ref=where,
            send_sem=self.send_sems.at[index],
            recv_sem=self.recv_sems.at[index],
            device_id={"seq": jnp.clip(self.rank + 2 * right - 1, 0, self.count - 1)},
            device_id_type=MESH,
        )

    def reaches(self, right):
        return self.rank < self.count - 1 if right else self.rank > 0

    def begin(self):
        for right in (1, 0):

            @pl.when(self.reaches(right))
            def _():
                self.link(self.rank, 0, right).start()

    def forward(self, hop):
        for right in (1, 0):
            owner = self.rank - hop if right else self.rank + hop
            there = owner >= 0 if right else owner < self.count
            owner = jnp.clip(owner, 0, self.count - 1)

            @pl.when(there)
            def _():
                self.link(owner, hop - 1, right).wait_recv()

            if hop < self.count - 1:

                @pl.when(there & self.reaches(right))
                def _():
                    self.link(owner, hop, right).start()

    def drain(self):
        for hop in range(self.count - 1):
            for right in (1, 0):
                owner = self.rank - hop if right else self.rank + hop
                there = owner >= 0 if right else owner < self.count

                @pl.when(there & self.reaches(right))
                def _():
                    self.link(self.rank, hop, right).wait_send()


def front_part(
    owner_ref, enc_ref, gain_ref, in_ref, out_ref, final_ref, context_ref, kv_ref, image_ref,
    proj_ref, down_ref, up_ref, magnitude_ref, scale_ref, shift_ref, image_gain_ref,
    queries, mixture, denominator, key_value, own_scaled, weight, up_weight, ratio_ref,
    image_all, tokens, normed, in_tiles, out_tiles, hidden, part, sum_slots, encoded, context_all, kv_all,
    context_part, row_slots, stage, prompts, sibling_prompts, text_all,
    direction, squares, square_slots,
    in_sems, out_sems, local_sems, send_sems, recv_sems, sum_send, sum_recv, row_send, row_recv, text_send, text_recv,
):
    f32, bf16 = jnp.float32, jnp.bfloat16
    count, devices = lax.axis_size("seq"), lax.axis_size("dp")
    rank, data_rank = lax.axis_index("seq"), lax.axis_index("dp")
    place = Place()
    wires = Wires(send_sems, recv_sems)
    text, width_enc = tokens.shape
    feat = encoded.shape[1]
    width = context_part.shape[1]
    rows = stage.shape[0]
    slots = in_tiles.shape[0]
    tile = in_tiles.shape[2] // 2
    tiles = hidden.shape[1] // tile
    depth, own_cols = proj_ref.shape
    flat = flat_columns(own_cols)
    late = count // 2

    class in_copy:
        def __init__(self, i, slot):
            columns = pl.ds(pl.multiple_of(i * tile, 128), tile)
            self.copies = [
                pltpu.make_async_copy(
                    in_ref.at[side, :, columns],
                    in_tiles.at[slot, :, side * tile : (side + 1) * tile],
                    in_sems.at[slot * 2 + side],
                )
                for side in range(2)
            ]

        def start(self):
            for copy in self.copies:
                copy.start()

        def wait(self):
            for copy in self.copies:
                copy.wait()

    near = 1 - lax.div(rank, count // 2)
    out_slots, _, out_tile = out_tiles.shape
    chunks = feat // out_tile

    def out_copy(i):
        step, c = divmod(i, chunks)
        owner = near * (count - 1 - step) + (1 - near) * step
        columns = pl.ds(pl.multiple_of(owner * feat + c * out_tile, 128), out_tile)
        slot = i % out_slots
        return pltpu.make_async_copy(out_ref.at[:, columns], out_tiles.at[slot], out_sems.at[slot])

    def local(source, target, index):
        return pltpu.make_async_copy(source, target, local_sems.at[index])

    token_copy = local(enc_ref.at[0, pl.ds(0, text)], tokens, 0)
    token_copy.start()
    for i in range(min(slots, tiles)):
        in_copy(i, i).start()
    for i in range(min(out_slots, count * chunks)):
        out_copy(i).start()

    def heads_of(owner):
        head_width = image_all.shape[3]
        return pl.ds(pl.multiple_of(owner * head_width, 128), head_width)

    context_view = by_columns(context_ref.shape[0], own_cols, flat)
    kv_view = by_rows(kv_ref.shape[0])
    context_gather = Gather(wires, place, context_ref, context_all, context_view)
    kv_gather = Gather(wires, place, kv_ref, kv_all, kv_view)

    locals_ = [
        local(image_ref.at[:, :, heads_of(rank)], image_all.at[0], 2),
        local(context_ref, context_view(context_all, data_rank, None), 3),
        local(kv_ref, kv_view(kv_all, data_rank, None), 4),
    ]
    scaled_gathers, scaled_locals = [], []
    for source, target, view in scaled_pieces(own_scaled, up_weight, weight, own_cols)[:2]:
        scaled_gathers.append(Gather(wires, place, source, target, view))
        scaled_locals.append(local(source, view(target, data_rank, None), 5 + len(scaled_locals)))
    image_rows = image_all.shape[2]
    heads = image_all.shape[3] // HD

    def head(h):
        return pl.ds(pl.multiple_of(h * HD, HD), HD)

    def query_step(h, carry):
        for k in range(count):
            queries[k * image_rows : (k + 1) * image_rows, head(h)] = rms_scale(
                image_all[k, 0, :, head(h)].astype(f32), image_gain_ref[0:1, :]
            ).astype(bf16)
        return carry

    def attend(k):
        def head_step(h, carry):
            keys = rms_scale(image_all[k, 1, :, head(h)].astype(f32), image_gain_ref[1:2, :]).astype(bf16)
            share = exp_scores(queries[:, head(h)], keys)
            total = jnp.broadcast_to(jnp.sum(share, -1, keepdims=True), (share.shape[0], HD))
            mixed = jnp.dot(share.astype(bf16), image_all[k, 2, :, head(h)], preferred_element_type=f32)
            if k:
                total = total + denominator[:, head(h)]
                mixed = mixed + mixture[:, head(h)]
            denominator[:, head(h)] = total
            mixture[:, head(h)] = mixed
            return carry

        if k:
            image_copies[k, 1].wait_recv()
            image_copies[k, 2].wait_recv()
        lax.fori_loop(0, heads, head_step, 0)

    greet("seq", "dp")
    context_gather.first()
    image_copies = {}

    def image(k, kind):
        peer = lax.rem(rank + k, count)
        image_copies[k, kind] = wires.send(
            image_ref.at[kind, :, heads_of(peer)], image_all.at[k, kind], "seq", peer
        )

    def images(kinds):
        for k in range(2, count):
            if k != late:
                for kind in kinds:
                    image(k, kind)

    for kind in range(3):
        image(1, kind)

    for copy in locals_:
        copy.start()

    token_copy.wait()
    for r in range(0, text, 32):
        block = tokens[r : r + 32, :].astype(f32)
        normed[r : r + 32, :] = rms_scale(block, gain_ref[...]).astype(bf16)

    def in_step(i, carry):
        slot = lax.rem(i, slots)
        in_copy(i, slot).wait()
        both = jnp.dot(normed[...], in_tiles[slot], preferred_element_type=f32)
        gate, upward = both[:, :tile], both[:, tile:]
        columns = pl.ds(pl.multiple_of(i * tile, 128), tile)
        hidden[:, columns] = (jax.nn.gelu(gate, approximate=True) * upward).astype(bf16)

        @pl.when(i + slots < tiles)
        def _():
            in_copy(i + slots, slot).start()

        return carry

    lax.fori_loop(0, tiles, in_step, 0)

    def piece(c):
        return slice(c * out_tile, (c + 1) * out_tile)

    sums = Chain(
        lambda owner, c: part.at[owner, :, piece(c)],
        lambda right, owner, c: sum_slots.at[owner + right, :, piece(c)],
        sum_send,
        sum_recv,
        chunks,
    )
    if late > 1:
        image(late, 0)
    for step in range(count):
        owner = sums.target(step, sums.near)
        for c in range(sums.chunks):
            index = step * chunks + c
            out_copy(index).wait()
            part[owner, :, piece(c)] = jnp.dot(
                hidden[...], out_tiles[index % out_slots], preferred_element_type=f32
            ).astype(bf16)
            if index + out_slots < count * chunks:
                out_copy(index + out_slots).start()
            if step < count - 1:
                sums.begin(step, (c,))

    context_gather.second()
    kv_gather.first()

    total = jnp.zeros((1, own_cols), f32)
    for r in range(0, depth, 128):
        block = proj_ref[r : r + 128, :].astype(f32) + lax.dot_general(
            down_ref[:, r : r + 128],
            up_ref[...],
            (((0,), (0,)), ((), ())),
            precision=lax.Precision.HIGHEST,
            preferred_element_type=f32,
        )
        direction[r : r + 128, :] = block
        total = total + jnp.sum(block * block, 0, keepdims=True)
    squares[...] = total
    square_copies = [wires.send(squares, square_slots.at[k - 1], "seq", peer) for k, peer in peers("seq")]

    for step in range(count - 1):
        sums.forward(step, sums.near)
        sums.forward(step, sums.far)
    context_gather.third()
    for c in range(sums.chunks):
        sums.arrive(c)
    images((0,))
    own = pl.ds(pl.multiple_of(rank * feat, 128), feat)
    for r in range(0, text, 32):
        block = slice(r, r + 32)
        total = sums.total(part[rank, block, :], sum_slots[rank + 1, block, :], sum_slots[rank, block, :])
        encoded[block, :] = ((tokens[block, own].astype(f32) + total) * final_ref[:, own]).astype(bf16)

    locals_[1].wait()
    context_gather.done()
    if late > 1:
        image(late, 1)
        image(late, 2)

    def block_of(index):
        return pl.ds(pl.multiple_of(index * rows, 16), rows)

    half = width // 2
    row_sums = Chain(
        lambda owner, c: context_part.at[block_of(owner), c * half : (c + 1) * half],
        lambda right, owner, c: row_slots.at[owner + right, :, c * half : (c + 1) * half],
        row_send,
        row_recv,
        2,
    )
    for c in range(2):
        if flat:
            step = tile_of(half, 512)
            for start in range(c * half, (c + 1) * half, step):
                context_part[:, start : start + step] = jnp.dot(
                    encoded[...], context_all[:, start : start + step], preferred_element_type=f32
                ).astype(bf16)
        else:
            for d in range(c * devices // 2, (c + 1) * devices // 2):
                context_part[:, d * own_cols : (d + 1) * own_cols] = jnp.dot(
                    encoded[...], context_all[d], preferred_element_type=f32
                ).astype(bf16)
        for step in range(count - 1):
            row_sums.begin(step, (c,))
    for copy in square_copies:
        copy.wait_recv()
    total = squares[...]
    for k in range(1, count):
        total = total + square_slots[k - 1]
    ratio = magnitude_ref[...].reshape(1, own_cols) / jnp.sqrt(total + EPSILON)
    ratio_ref[...] = ratio
    for r in range(0, depth, 128):
        own_scaled[r : r + 128, :] = (direction[r : r + 128, :] * ratio).astype(bf16)
    own_scaled[depth:, :] = (up_ref[...] * ratio).astype(bf16)

    for c in range(2):
        for step in range(count - 1):
            row_sums.forward(step, row_sums.near, (c,))
            row_sums.forward(step, row_sums.far, (c,))
    for c in range(2):
        row_sums.arrive(c)
    stage[...] = row_sums.total(
        context_part[block_of(rank), :], row_slots[rank + 1], row_slots[rank]
    ).astype(bf16)

    chips = devices // 2
    chip = lax.div(data_rank, 2)
    sibling = place.at(other_core=True)
    prompt_copies = [
        wires.send(stage, prompts.at[j - 1], "dp", lax.rem(chip + j, chips) * 2 + place.core)
        for j in range(1, chips)
    ]
    shared = [wires.send(stage, sibling_prompts.at[0], "dp", sibling)]
    images((1, 2))
    kv_gather.second()
    for gather, copy in zip(scaled_gathers, scaled_locals):
        gather.first()
        copy.start()
    locals_[0].wait()
    for k in range(1, count):
        image_copies[k, 0].wait_recv()
    lax.fori_loop(0, heads, query_step, 0)
    attend(0)
    attend(1)
    for j in range(1, chips):
        prompt_copies[j - 1].wait_recv()
        shared.append(wires.send(prompts.at[j - 1], sibling_prompts.at[j], "dp", sibling))
    routed = jnp.where(owner_ref[data_rank] == data_rank, stage[...].astype(f32), 0.0)
    for j in range(1, chips):
        prompt = lax.rem(chip + chips - j, chips) * 2 + place.core
        routed = routed + jnp.where(owner_ref[prompt] == data_rank, prompts[j - 1].astype(f32), 0.0)
    for j in range(chips):
        shared[j].wait_recv()
        prompt = lax.rem(chip + chips - j, chips) * 2 + 1 - place.core
        routed = routed + jnp.where(owner_ref[prompt] == data_rank, sibling_prompts[j].astype(f32), 0.0)
    centre = jnp.mean(routed, -1, keepdims=True)
    spread = jnp.mean((routed - centre) * (routed - centre), -1, keepdims=True)
    layer_normed = (routed - centre) * lax.rsqrt(spread + EPSILON)
    text_all[block_of(rank), :] = ((1.0 + scale_ref[...]) * layer_normed + shift_ref[...]).astype(bf16)
    texts = Relay(lambda owner: text_all.at[block_of(owner)], text_send, text_recv)
    texts.begin()
    for k in [k for k in range(2, count) if k != late] + [late] * (late > 1):
        attend(k)
    for gather in scaled_gathers:
        gather.second()
    for hop in range(1, count):
        texts.forward(hop)
    kv_gather.third()
    for gather in scaled_gathers:
        gather.third()
    locals_[2].wait()
    kv_gather.done()
    step = tile_of(kv_all.shape[1], 512)
    for c in range(0, kv_all.shape[1], step):
        key_value[:, c : c + step] = jnp.dot(
            text_all[...], kv_all[:, c : c + step], preferred_element_type=f32
        )
    for gather, copy in zip(scaled_gathers, scaled_locals):
        gather.done()
        copy.wait()
    return sums, row_sums, texts, wires


def back_part(
    owner_ref, lengths_ref, text_gain_ref, key_value_ref, queries_ref, mixture_ref, denominator_ref,
    scaled_ref, weight, up_weight_ref, dora_ref, grad_ref, ratio_ref, magnitude_ref,
    image_out, down_out, cols_out, size_out,
    attended, parts, slots, down, up, up_slots, down_slots,
    cols, col_slots, col_stage, col_sums, rows_all, row_slots, row_stage, row_sums,
    size, size_slots, size_stage, size_sums,
    local_sems, chain_send, chain_recv, send_sems, recv_sems,
):
    count, devices = lax.axis_size("seq"), lax.axis_size("dp")
    rank, data_rank = lax.axis_index("seq"), lax.axis_index("dp")
    rows, width = image_out.shape
    depth = queries_ref.shape[1]
    text = key_value_ref.shape[0]
    heads = depth // HD
    own_cols = ratio_ref.shape[1]
    adapter = dora_ref.shape[0]
    pieces = pieces_of(own_cols)
    piece = own_cols // pieces
    flat = flat_columns(own_cols)
    block_rows = depth // devices
    f32, bf16 = jnp.float32, jnp.bfloat16
    over_rows = (((0,), (0,)), ((), ()))
    over_columns = (((1,), (1,)), ((), ()))
    wires = Wires(send_sems, recv_sems)
    place = Place()

    def block_of(owner):
        return lax.rem(rank + count - owner, count)

    chain = Chain(
        lambda owner, p: parts.at[owner, p],
        lambda right, owner, p: slots.at[owner + right, p],
        chain_send,
        chain_recv,
        pieces,
    )
    near, far = chain.near, chain.far
    gathers, owns = [None], [None]
    for source, target, view in scaled_pieces(scaled_ref, up_weight_ref, weight, own_cols)[2:]:
        gathers.append(Gather(wires, place, source, target, view))
        owns.append(
            pltpu.make_async_copy(source, view(target, data_rank, None), local_sems.at[len(owns) - 1])
        )
    if pieces > 1:
        gathers[1].first()
    for copy in owns[1:]:
        copy.start()

    length = jnp.int32(0)
    for p in range(devices):
        length = length + jnp.where(owner_ref[p] == data_rank, lengths_ref[p], 0)

    def head(h):
        return pl.ds(pl.multiple_of(h * HD, HD), HD)

    def head_step(h, carry):
        keys = rms_scale(key_value_ref[:, head(h)], text_gain_ref[...]).astype(bf16)
        values = key_value_ref[:, pl.ds(pl.multiple_of(depth + h * HD, HD), HD)].astype(bf16)
        share = exp_scores(queries_ref[:, head(h)], keys)
        position = lax.broadcasted_iota(jnp.int32, share.shape, 1)
        share = jnp.where(position < length, share, 0.0)
        denominator = denominator_ref[:, head(h)] + jnp.sum(share, -1, keepdims=True)
        mixture = mixture_ref[:, head(h)] + jnp.dot(share.astype(bf16), values, preferred_element_type=f32)
        attended[:, head(h)] = (mixture / denominator).astype(bf16)
        return carry

    lax.fori_loop(0, heads, head_step, 0)

    def products(p, begin=True):
        if p:
            gathers[p].done()
            owns[p].wait()
        source = weight.at[p]
        for step in range(count):
            owner = chain.target(step, near)
            block = attended[pl.ds(pl.multiple_of(block_of(owner) * rows, 16), rows), :]
            if flat:
                parts[owner, p] = jnp.dot(block, source[...], preferred_element_type=f32).astype(bf16)
            else:
                for d in range(devices):
                    parts[owner, p, :, d * piece : (d + 1) * piece] = jnp.dot(
                        block, source[d], preferred_element_type=f32
                    ).astype(bf16)
            if begin and step < count - 1:
                chain.begin(step, (p,))

    if flat:
        down_total = lax.dot_general(grad_ref[...], up_weight_ref[...], over_columns, preferred_element_type=f32)
    else:
        down_total = jnp.zeros((rows, adapter), f32)
        for d in range(devices):
            down_total = down_total + lax.dot_general(
                grad_ref[:, d * own_cols : (d + 1) * own_cols],
                up_weight_ref[d],
                over_columns,
                preferred_element_type=f32,
            )
    down[...] = down_total.astype(bf16)
    ups = lax.dot_general(
        attended[...], dora_ref[...].astype(bf16), over_columns, preferred_element_type=f32
    ).astype(bf16)
    for k in range(count):
        up[k] = ups[k * rows : (k + 1) * rows]
    small = []
    for k, peer in peers("seq"):
        small.append(wires.send(down, down_slots.at[k - 1], "seq", peer))
        before = lax.rem(rank + count - k, count)
        small.append(wires.send(up.at[k], up_slots.at[k - 1], "seq", before))
    def forwards(p):
        for step in range(count - 1):
            chain.forward(step, near, (p,))
            chain.forward(step, far, (p,))

    def prepare(p):
        gathers[p].second()
        if p + 1 < pieces:
            gathers[p + 1].first()
        gathers[p].third()
        products(p, p + 1 < pieces)

    products(0)
    if pieces > 1:
        prepare(1)
        forwards(0)
    for p in range(2, pieces):
        prepare(p)
    for copy in small:
        copy.wait_recv()
    up_total = up[0].astype(f32)
    for k in range(1, count):
        up_total = up_total + up_slots[k - 1].astype(f32)
    up_total = up_total.astype(bf16)
    column_grad = lax.dot_general(up_total, grad_ref[...], over_rows, preferred_element_type=f32).astype(bf16)
    for j in range(devices):
        cols[j] = column_grad[:, j * own_cols : (j + 1) * own_cols]
    row_grad = lax.dot_general(down[...], attended[:rows, :], over_rows, preferred_element_type=f32)
    for k in range(1, count):
        row_grad = row_grad + lax.dot_general(
            down_slots[k - 1], attended[k * rows : (k + 1) * rows, :], over_rows, preferred_element_type=f32
        )
    for j in range(devices):
        rows_all[j] = row_grad[:, j * block_rows : (j + 1) * block_rows].astype(bf16)
    first = []
    for k, peer in peers("dp"):
        first.append(wires.send(cols.at[peer], col_slots.at[k - 1], "dp", peer))
        first.append(wires.send(rows_all.at[peer], row_slots.at[k - 1], "dp", peer))

    for p in range(1, pieces - 1):
        forwards(p)
    for copy in first:
        copy.wait_recv()
    col_total = cols[data_rank].astype(f32)
    row_total = rows_all[data_rank].astype(f32)
    for k, _ in peers("dp"):
        col_total = col_total + col_slots[k - 1].astype(f32)
        row_total = row_total + row_slots[k - 1].astype(f32)
    col_stage[...] = col_total.astype(bf16)
    row_stage[...] = row_total.astype(bf16)
    second = []
    for k, peer in peers("seq"):
        second.append(wires.send(col_stage, col_sums.at[k - 1], "seq", peer))
    for k, peer in peers("dp"):
        second.append(wires.send(row_stage, row_sums.at[data_rank], "dp", peer))
    row_sums[data_rank] = row_stage[...]
    if pieces > 1:
        for step in range(count - 1):
            chain.begin(step, (pieces - 1,))
    forwards(pieces - 1)

    for p in range(pieces):
        chain.arrive(p)
        total = chain.total(parts[rank, p], slots[rank + 1, p], slots[rank, p])
        for d in range(devices):
            own = slice(d * own_cols + p * piece, d * own_cols + (p + 1) * piece)
            block = total[:, d * piece : (d + 1) * piece]
            image_out[:, own] = block.astype(bf16)
            size[d, :, p * piece : (p + 1) * piece] = jnp.sum(
                grad_ref[:, own].astype(f32) * block, 0, keepdims=True
            )
    last = [wires.send(size.at[peer], size_slots.at[k - 1], "dp", peer) for k, peer in peers("dp")]
    for copy in second:
        copy.wait_recv()
    col_total = col_stage[...].astype(f32)
    for k, _ in peers("seq"):
        col_total = col_total + col_sums[k - 1].astype(f32)
    cols_out[...] = col_total * ratio_ref[...]
    for d in range(devices):
        down_out[:, d * block_rows : (d + 1) * block_rows] = row_sums[d].astype(f32)
    for copy in last:
        copy.wait_recv()
    size_total = size[data_rank]
    for k, _ in peers("dp"):
        size_total = size_total + size_slots[k - 1]
    size_stage[...] = size_total
    last = [wires.send(size_stage, size_sums.at[k - 1], "seq", peer) for k, peer in peers("seq")]
    for copy in last:
        copy.wait_recv()
    for k, _ in peers("seq"):
        size_total = size_total + size_sums[k - 1]
    size_out[...] = size_total / magnitude_ref[...].reshape(1, own_cols)
    chain.drain()
    wires.drain()


def program_kernel(counts, *refs):
    names = []
    for n in counts:
        names.append(refs[:n])
        refs = refs[n:]
    front_in, back_in, outs, shared, front_scratch, back_scratch = names
    key_value, queries, mixture, denominator, own_scaled, weight, up_weight, ratio = shared
    owner, down, magnitude = front_in[0], front_in[10], front_in[12]
    waits = front_part(
        *front_in, queries, mixture, denominator, key_value, own_scaled, weight, up_weight, ratio, *front_scratch
    )
    lengths, text_gain, grad = back_in
    back_part(
        owner, lengths, text_gain, key_value, queries, mixture, denominator,
        own_scaled, weight, up_weight, down, grad, ratio, magnitude,
        *outs, *back_scratch,
    )
    for wait in waits:
        wait.drain()


def program(
    owner, enc, gain, w_in, w_out, final_gain, context, kv, image, proj, down, up, magnitude, scale, shift,
    image_gain, lengths, text_gain, grad,
):
    count, devices = lax.axis_size("seq"), lax.axis_size("dp")
    bf16, f32 = jnp.bfloat16, jnp.float32
    width_enc, hidden = w_in.shape[1:]
    feat = width_enc // count
    text = MAX_PROMPT
    width = scale.shape[1]
    text_rows = text // count
    kinds, rows, _ = image.shape
    head_width = width // count
    depth, own_cols = proj.shape
    rank = up.shape[0]
    block_rows = depth // devices
    pieces = pieces_of(own_cols)
    piece = own_cols // pieces
    others, data_others, pairs = count - 1, devices - 1, devices // 4
    tile, out_tile = tile_of(hidden, 128), tile_of(feat, 512)
    slots = 3
    sum_chunks = feat // out_tile
    per_gather = 6 * pairs - 3
    front_wires = 4 * others + 4 * pairs + 4 * per_gather
    back_wires = 4 * others + 4 * data_others + pieces * per_gather
    any_ = pl.BlockSpec(memory_space=pl.ANY)
    vmem, sems = pltpu.VMEM, pltpu.SemaphoreType.DMA
    shared = [
        vmem((text, kv.shape[1]), f32),
        vmem((count * rows, head_width), bf16),
        vmem((count * rows, head_width), f32),
        vmem((count * rows, head_width), f32),
        vmem((depth + rank, own_cols), bf16),
        vmem((pieces,) + column_shape(devices, depth, piece), bf16),
        vmem(column_shape(devices, rank, own_cols), bf16),
        vmem((1, own_cols), f32),
    ]
    front_scratch = [
        vmem((count, kinds, rows, head_width), bf16),
        vmem((text, width_enc), bf16),
        vmem((text, width_enc), bf16),
        vmem((slots, width_enc, 2 * tile), bf16),
        vmem((slots, hidden, out_tile), bf16),
        vmem((text, hidden), bf16),
        vmem((count, text, feat), bf16),
        vmem((count + 1, text, feat), bf16),
        vmem((text, feat), bf16),
        vmem(column_shape(devices, context.shape[0], own_cols), bf16),
        vmem((kv.shape[0] * devices, kv.shape[1]), bf16),
        vmem((text, width), bf16),
        vmem((count + 1, text_rows, width), bf16),
        vmem((text_rows, width), bf16),
        vmem((devices // 2 - 1, text_rows, width), bf16),
        vmem((devices // 2, text_rows, width), bf16),
        vmem((text, width), bf16),
        vmem((depth, own_cols), f32),
        vmem((1, own_cols), f32),
        vmem((others, 1, own_cols), f32),
        sems((slots * 2,)),
        sems((slots,)),
        sems((7,)),
        sems((front_wires,)),
        sems((front_wires,)),
        sems((count * sum_chunks,)),
        sems((count * 2 * sum_chunks,)),
        sems((count * 2,)),
        sems((count * 4,)),
        sems((count * 2,)),
        sems((count * 2,)),
    ]
    back_scratch = [
        vmem((count * rows, head_width), bf16),
        vmem((count, pieces, rows, devices * piece), bf16),
        vmem((count + 1, pieces, rows, devices * piece), bf16),
        vmem((rows, rank), bf16),
        vmem((count, rows, rank), bf16),
        vmem((others, rows, rank), bf16),
        vmem((others, rows, rank), bf16),
        vmem((devices, rank, own_cols), bf16),
        vmem((data_others, rank, own_cols), bf16),
        vmem((rank, own_cols), bf16),
        vmem((others, rank, own_cols), bf16),
        vmem((devices, rank, block_rows), bf16),
        vmem((data_others, rank, block_rows), bf16),
        vmem((rank, block_rows), bf16),
        vmem((devices, rank, block_rows), bf16),
        vmem((devices, 1, own_cols), f32),
        vmem((data_others, 1, own_cols), f32),
        vmem((1, own_cols), f32),
        vmem((others, 1, own_cols), f32),
        sems((pieces + 1,)),
        sems((count * pieces,)),
        sems((count * 2 * pieces,)),
        sems((back_wires,)),
        sems((back_wires,)),
    ]
    front_in = (
        owner, enc, gain, w_in, w_out, final_gain, context, kv, image, proj, down, up, magnitude, scale, shift,
        image_gain,
    )
    back_in = (lengths, text_gain, grad)
    counts = (len(front_in), len(back_in), 4, len(shared), len(front_scratch), len(back_scratch))
    return pl.pallas_call(
        functools.partial(program_kernel, counts),
        out_shape=[
            jax.ShapeDtypeStruct(grad.shape, bf16),
            jax.ShapeDtypeStruct((rank, depth), f32),
            jax.ShapeDtypeStruct((rank, own_cols), f32),
            jax.ShapeDtypeStruct((1, own_cols), f32),
        ],
        in_specs=[SMEM, any_, VMEM, any_, any_, VMEM, any_, any_, any_] + [VMEM] * 7 + [SMEM, VMEM, VMEM],
        out_specs=[VMEM] * 4,
        scratch_shapes=shared + front_scratch + back_scratch,
        compiler_params=pltpu.CompilerParams(
            collective_id=1, has_side_effects=True, vmem_limit_bytes=63 * 2**20
        ),
    )(*front_in, *back_in)


def results_kernel(*refs):
    half = len(refs) // 2
    for source, target in zip(refs[:half], refs[half:]):
        target[...] = source[...].reshape(target.shape)


def results(*values):
    shapes = [jax.ShapeDtypeStruct(v.shape if v.shape[0] > 1 else v.shape[1:], v.dtype) for v in values]
    return pl.pallas_call(
        results_kernel, out_shape=shapes, in_specs=[VMEM] * len(values), out_specs=[VMEM] * len(values)
    )(*values)


def on_device(
    enc_states,
    lengths,
    prompt_owner_sample,
    t5_gain,
    t5_in_weight,
    t5_out_weight,
    t5_final_gain,
    context_weight,
    text_shift,
    text_scale,
    kv_weight,
    text_key_gain,
    image_query_key_value,
    image_qk_gain,
    proj_weight,
    dora_a,
    dora_b,
    magnitude,
    grad_out,
):
    outs = program(
        prompt_owner_sample,
        enc_states,
        t5_gain[None],
        t5_in_weight,
        t5_out_weight,
        t5_final_gain[None],
        context_weight,
        kv_weight.reshape(kv_weight.shape[0], -1),
        jnp.transpose(image_query_key_value[0], (1, 0, 2)),
        proj_weight,
        dora_a.T,
        dora_b,
        magnitude,
        text_scale,
        text_shift,
        image_qk_gain,
        lengths,
        text_key_gain[None],
        grad_out[0],
    )
    image_out, grad_a, grad_b, grad_magnitude = results(*outs)
    return (image_out[None], grad_a.T, grad_b, grad_magnitude)


def solution(mesh):
    mapped = jax.shard_map(
        on_device,
        mesh=mesh,
        in_specs=(
            P("dp", None, None),
            P(),
            P(),
            P(),
            P(None, None, "seq"),
            P("seq", None),
            P(),
            P("seq", "dp"),
            P("dp", None),
            P("dp", None),
            P("dp", None, "seq"),
            P(),
            P("dp", "seq", None, None),
            P(),
            P("seq", "dp"),
            P("seq", None),
            P(None, "dp"),
            P("dp"),
            P("dp", "seq", None),
        ),
        out_specs=(P("dp", "seq", None), P("seq", None), P(None, "dp"), P("dp")),
        check_vma=False,
    )
    return mapped
```
